32 devices in a mesh: rep: 2 (over y), tract: 4 (over x, core), head: 4 (over z).
Axes of the slice: x: 2, y: 2, z: 4, core: 2. Of those that a mesh axis runs over, the one named last changes fastest.
Arguments:
- frames: bfloat16 [8, 256, 6144], P(('rep', 'tract'), 'head'), parts along dimension 0, may hold values from -7 to 7
- levels: int32 [8], P(('rep', 'tract')), parts along dimension 0, may hold values from 0 to 7
- visible: int32 [8, 4], P(('rep', 'tract')), parts along dimension 0, may hold values from 0 to 1, as said below
- w_qkv: bfloat16 [6144, 3, 1024], P(None, None, 'head'), may hold values from -0.2 to 0.2
- w_out: bfloat16 [1024, 6144], P('head'), may hold values from -1.5 to 1.5
- modulation: float32 [8, 3, 6144], replicated, may hold values from -3 to 3
Outputs:
- mixed: bfloat16 [8, 256, 6144], P(('rep', 'tract'), 'head'), parts along dimension 0
The draws below stay inside these ranges and needn't reach their ends.
There are 2 independent parts, one for each index of `rep`. The reference program is written for one: setup_inputs(seed, part) draws one part's arguments, and reference() takes and returns one part's arrays. A program takes and returns all parts, laid end to end along the dimension named above; an argument that names none is the same for every part. Nothing has to cross between parts.
Inputs may be any that keep to these rules, and one draw needn't show every extreme that they name: visible[c, c] is 1 and visible[c, j] is 0 for every j > c.
All inputs are finite; a program needn't handle non-finite values.
Results may differ from the reference program's by a relative error of at most 0.019.
Values may be sent and summed in bfloat16 or wider, within the bound.
A program may use at most 64 MiB of HBM per device.

```python
import jax
import jax.numpy as jnp
from jax import lax

D = 6144
HD = 128
H_DEV = 2
CT = 256
NSTEP = 8
HEADS = 8
NCHUNK = 4
N_HEAD = 4


def draw_frames(key, part):
    base = jax.random.normal(jax.random.fold_in(key, 11), (NCHUNK, CT, D), jnp.float32)
    return jnp.clip(base, -6.5, 6.5).astype(jnp.bfloat16)


def draw_w_qkv(key, part):
    spread = D ** (-0.5)
    queries = spread * jax.random.normal(jax.random.fold_in(key, 21), (D, HEADS * HD), jnp.float32)
    key_part = spread * jax.random.normal(jax.random.fold_in(key, 22), (D, HEADS * HD), jnp.float32)
    values = spread * jax.random.normal(jax.random.fold_in(key, 23), (D, HEADS * HD), jnp.float32)
    stacked = jnp.stack([queries, key_part, values], axis=1)
    return jnp.clip(stacked, -0.19, 0.19).astype(jnp.bfloat16)


def draw_modulation(key, part):
    shift = 0.3 * jax.random.normal(jax.random.fold_in(key, 31), (NSTEP, D), jnp.float32)
    stretch = 0.3 * jax.random.normal(jax.random.fold_in(key, 32), (NSTEP, D), jnp.float32)
    gating = jax.random.normal(jax.random.fold_in(key, 33), (NSTEP, D), jnp.float32)
    return jnp.clip(jnp.stack([shift, stretch, gating], axis=1), -2.9, 2.9)


def draw_visible(key, part):
    coins = jax.random.randint(jax.random.fold_in(key, 41), (NCHUNK, NCHUNK), 0, 4)
    row_ids = jnp.arange(NCHUNK, dtype=jnp.int32)[:, None]
    col_ids = jnp.arange(NCHUNK, dtype=jnp.int32)[None, :]
    lower = jnp.where((coins > 0) & (row_ids > col_ids), 1, 0)
    return jnp.where(row_ids == col_ids, 1, lower).astype(jnp.int32)


def with_ends(result, rng, low, high):
    longest = result.shape.index(max(result.shape))
    spots = []
    for shift in (0, 1):
        where = [jax.random.randint(jax.random.fold_in(rng, axis), (), 0, length) for axis, length in enumerate(result.shape)]
        where[longest] = (where[longest] + shift) % result.shape[longest]
        spots.append(tuple(where))
    return result.at[spots[0]].set(low).at[spots[1]].set(high)


def block_scale(stream_key, dims, shards, least, top_value):
    gain = 1.0
    for dim, parts in shards:
        draws = jax.random.uniform(jax.random.fold_in(jax.random.fold_in(stream_key, 6), dim), (parts,), jnp.float32, least / len(shards), top_value / len(shards))
        gain = gain * jnp.repeat(jnp.exp(draws), dims[dim] // parts).reshape((-1,) + (1,) * (len(dims) - 1 - dim))
    return gain


def bell_draw(own_key, extent, deviation, bound, pieces=(), held_as=jnp.bfloat16):
    level = block_scale(own_key, extent, pieces, -0.22, 0.18) if pieces else 1.0
    array = jax.random.normal(own_key, extent, jnp.float32) * deviation * level
    return jnp.minimum(jnp.maximum(array, -bound), bound).astype(held_as)


def setup_inputs(seed: int = 0, part: int = 0) -> dict:
    splits = jax.random.split(jax.random.key(seed), 7)
    own_keys = jax.random.split(jax.random.fold_in(splits[6], part), 7)
    return {
        "frames": draw_frames(jax.random.fold_in(jax.random.fold_in(splits[6], part), 71), part),
        "levels": with_ends(jax.random.randint(own_keys[1], (NCHUNK,), 0, NSTEP), jax.random.fold_in(own_keys[1], 1), 0, NSTEP - 1).astype(jnp.int32),
        "visible": draw_visible(jax.random.fold_in(jax.random.fold_in(splits[6], part), 71), part),
        "w_qkv": draw_w_qkv(jax.random.fold_in(splits[6], 71), part),
        "w_out": bell_draw(splits[4], (HEADS * HD, D), (HEADS * HD // 64) ** -0.5, 1.5, ((0, 4),)),
        "modulation": draw_modulation(jax.random.fold_in(splits[6], 71), part),
    }


def reference(frames, levels, visible, w_qkv, w_out, modulation):
    styles = modulation[levels]
    floats = frames.astype(jnp.float32)
    normed = floats * lax.rsqrt(lax.optimization_barrier(jnp.mean(floats * floats, axis=-1, keepdims=True)) + 1e-06)
    shaped = (normed * (1.0 + styles[:, 1][:, None, :]) + styles[:, 0][:, None, :]).astype(jnp.bfloat16)
    qkv = jnp.dot(shaped.reshape(NCHUNK * CT, D), w_qkv.reshape(D, 3 * HEADS * HD), preferred_element_type=jnp.float32)
    qkv = qkv.astype(jnp.bfloat16).reshape(NCHUNK, CT, 3, HEADS, HD)
    queries = qkv[:, :, 0].astype(jnp.float32)
    key_rows = qkv[:, :, 1].astype(jnp.float32)
    values = qkv[:, :, 2].astype(jnp.float32)
    score_scale = HD ** (-0.5)

    def attend(inputs):
        query_block, visible_row = inputs
        scores = jnp.einsum('qhd,nkhd->qhnk', query_block, key_rows, precision=lax.Precision.HIGHEST) * score_scale
        allowed = (visible_row > 0)[None, None, :, None]
        scores = jnp.where(allowed, scores, -1e+30)
        row_peak = lax.optimization_barrier(jnp.max(scores, axis=(2, 3), keepdims=True))
        probs = jnp.where(allowed, jnp.exp(scores - row_peak), 0.0)
        denominator = lax.optimization_barrier(jnp.sum(probs, axis=(2, 3)))
        rounded = lax.optimization_barrier(probs.astype(jnp.bfloat16)).astype(jnp.float32)
        weighted = jnp.einsum('qhnk,nkhd->qhd', rounded, values, precision=lax.Precision.HIGHEST)
        return (weighted / denominator[:, :, None]).astype(jnp.bfloat16)
    attended = lax.map(attend, (queries, visible))
    flat = attended.reshape(NCHUNK * CT, HEADS * HD)
    span = H_DEV * HD

    def add_group(group, running):
        cols = lax.dynamic_slice_in_dim(flat, group * span, span, 1)
        rows = lax.dynamic_slice_in_dim(w_out, group * span, span, 0)
        partial_value = jnp.dot(cols, rows, preferred_element_type=jnp.float32)
        return running + lax.optimization_barrier(partial_value.astype(jnp.bfloat16)).astype(jnp.float32)
    summed = lax.fori_loop(0, N_HEAD, add_group, jnp.zeros((NCHUNK * CT, D), jnp.float32))
    summed = summed.reshape(NCHUNK, CT, D)
    return (summed * styles[:, 2][:, None, :]).astype(jnp.bfloat16)
```

```python
import functools

import jax
import jax.numpy as jnp
from jax import lax
from jax.experimental import pallas as pl
from jax.experimental.pallas import tpu as pltpu
from jax.sharding import PartitionSpec as P

HD = 128
GRANT = 60 * 1024 * 1024
MESH = pl.DeviceIdType.MESH


def meet(n, me, tracts, tract, others):
    barrier = pltpu.get_barrier_semaphore()
    for other in (lax.rem(me + 1, n), lax.rem(me + n - 1, n)):
        pl.semaphore_signal(barrier, inc=1, device_id={"head": other}, device_id_type=MESH)
    for ahead in range(1, tracts):
        other = lax.rem(tract + ahead, tracts)
        pl.semaphore_signal(barrier, inc=1, device_id={"tract": other}, device_id_type=MESH)
    for other in others:
        pl.semaphore_signal(barrier, inc=1, device_id=other, device_id_type=MESH)
    pl.semaphore_wait(barrier, 1 + tracts + len(others))


def sublayer_kernel(
    n,
    tracts,
    reps,
    pieces,
    halves,
    x_ref,
    level_ref,
    visible_ref,
    w_hbm,
    out_hbm,
    table_ref,
    out_ref,
    got,
    wq_ref,
    w_ref,
    q_ref,
    kv_ref,
    kv_in,
    att_ref,
    peak_ref,
    sum_ref,
    acc_ref,
    going,
    landed,
    total_ref,
    load_sem,
    g_send,
    g_recv,
    kv_send,
    kv_recv,
    s_send,
    s_recv,
    w_far,
    att_far,
    f_send,
    f_recv,
):
    me, tract = lax.axis_index("head"), lax.axis_index("tract")
    own = pltpu.make_async_copy(x_ref.at[0], got.at[me], load_sem.at[0])
    own.start()
    load = pltpu.make_async_copy(w_hbm, wq_ref, load_sem.at[1])
    load.start()
    load_out = pltpu.make_async_copy(out_hbm, w_ref, load_sem.at[2])
    load_out.start()
    core, wide = tract % 2, tracts // 2
    chips = wide * reps
    chip = lax.axis_index("rep") * wide + tract // 2
    slab = w_ref.shape[0] // (2 * chips)
    helper = (me == 1) | (me == n - 2)
    ends = (me == 0) | (me == n - 1)

    def seat(by):
        other = lax.rem(chip + by, chips)
        return {"rep": other // wide, "tract": lax.rem(other, wide) * 2 + core}

    def slab_of(which, side):
        start = pl.multiple_of((which * 2 + side) * slab, slab)
        return pl.ds(start, slab)

    def far_copy(kind, span, target, source=None):
        return pltpu.make_async_remote_copy(
            src_ref=(w_far if source is None else source).at[span],
            dst_ref=w_far.at[span],
            send_sem=f_send.at[kind],
            recv_sem=f_recv.at[kind],
            device_id=target,
            device_id_type=MESH,
        )

    inward = {"head": jnp.where(me == 0, 1, n - 2)}
    partner = {"tract": tract + 1 - 2 * core}
    mine = slab_of(chip, core)

    def to_helper():
        return far_copy(0, mine, inward, out_hbm)

    def to_chip(by):
        return far_copy(by, mine, seat(by))

    def from_chip(by):
        return far_copy(by, slab_of(lax.rem(chip + chips - by, chips), core), seat(by))

    def to_partner(by):
        span = slab_of(lax.rem(chip + chips - by, chips), core)
        return far_copy(chips + by, span, partner)

    def from_partner(by):
        span = slab_of(lax.rem(chip + chips - by, chips), 1 - core)
        return far_copy(chips + by, span, partner)

    def att_copy():
        return pltpu.make_async_remote_copy(
            src_ref=att_ref,
            dst_ref=att_far,
            send_sem=f_send.at[2 * chips],
            recv_sem=f_recv.at[2 * chips],
            device_id=inward,
            device_id_type=MESH,
        )

    meet(n, me, tracts, tract, [seat(by) for by in range(1, chips)])
    level = level_ref[0]

    def style(kind):
        return table_ref[kind, pl.ds(level, 1), :]

    rows, width = x_ref.shape[1:]
    part = rows // pieces

    def copy(way, step, piece, first=False):
        side = (way + 1) // 2
        span = pl.ds(piece * part, part)
        block = me - way * step
        return pltpu.make_async_remote_copy(
            src_ref=(x_ref.at[0] if first else got.at[block]).at[span],
            dst_ref=got.at[block].at[span],
            send_sem=g_send.at[side, step, piece],
            recv_sem=g_recv.at[side, step, piece],
            device_id={"head": me + way},
            device_id_type=MESH,
        )

    def arrival(way, step, piece):
        side = (way + 1) // 2
        span = pl.ds(piece * part, part)
        return pltpu.make_async_remote_copy(
            src_ref=x_ref.at[0].at[span],
            dst_ref=got.at[me - way * (step + 1)].at[span],
            send_sem=g_send.at[side, step, piece],
            recv_sem=g_recv.at[side, step, piece],
            device_id={"head": me - way},
            device_id_type=MESH,
        )

    def sends(way, step):
        block, target = me - way * step, me + way
        return (block >= 0) & (block < n) & (target >= 0) & (target < n) & (step < n - 1)

    def receives(way, step):
        block = me - way * (step + 1)
        return (block >= 0) & (block < n)

    def kv_copy(ahead, block):
        return pltpu.make_async_remote_copy(
            src_ref=kv_ref.at[block],
            dst_ref=kv_in.at[ahead - 1, block],
            send_sem=kv_send.at[ahead - 1, block],
            recv_sem=kv_recv.at[ahead - 1, block],
            device_id={"tract": tract + ahead},
            device_id_type=MESH,
        )

    def project(block):
        tokens = got[block].astype(jnp.float32)
        power = jnp.mean(tokens * tokens, axis=-1, keepdims=True)
        normed = tokens * lax.rsqrt(power + 1e-06)
        shaped = (normed * (1.0 + style(1)) + style(0)).astype(jnp.bfloat16)
        for kind in (1, 2, 0):
            made = jnp.dot(shaped, wq_ref[kind], preferred_element_type=jnp.float32)
            made = made.astype(jnp.bfloat16)
            if kind == 0:
                q_ref[block] = made
            else:
                kv_ref[block, kind - 1] = made
            if kind == 2:
                for ahead in range(1, tracts):

                    @pl.when(tract + ahead < tracts)
                    def _():
                        kv_copy(ahead, block).start()

    for piece in range(pieces):
        for way in (-1, 1):

            @pl.when(sends(way, 0))
            def _():
                copy(way, 0, piece, True).start()

    @pl.when(ends)
    def _():
        to_helper().start()

    own.wait()
    load.wait()
    project(me)

    @pl.loop(0, n - 1)
    def _(step):
        for piece in range(pieces):
            for way in (-1, 1):

                @pl.when(receives(way, step))
                def _():
                    arrival(way, step, piece).wait_recv()

                @pl.when(sends(way, step + 1))
                def _():
                    copy(way, step + 1, piece).start()

        @pl.loop(0, 2)
        def _(side):
            way = 2 * side - 1

            @pl.when(receives(way, step))
            def _():
                project(me - way * (step + 1))

        @pl.when(helper & (step == 0))
        def _():
            to_helper().wait_recv()
            for by in range(1, chips):
                to_chip(by).start()
            to_partner(0).start()

    @pl.when(helper)
    def _():
        for by in range(1, chips):
            from_chip(by).wait_recv()
            to_partner(by).start()

    tokens_here = n * rows
    heads_here = q_ref.shape[2] // HD
    scale = HD ** (-0.5)

    def attend(source, allowed):
        for head in range(heads_here):
            lanes = slice(head * HD, (head + 1) * HD)
            queries = q_ref[:, :, lanes].reshape(tokens_here, HD)
            keys = source[:, 0, :, lanes].reshape(tokens_here, HD)
            values = source[:, 1, :, lanes].reshape(tokens_here, HD)
            scores = (
                lax.dot_general(
                    queries, keys, (((1,), (1,)), ((), ())), preferred_element_type=jnp.float32
                )
                * scale
            )
            if allowed is None:
                peak = jnp.max(scores, axis=1, keepdims=True)
                probs = jnp.exp(scores - peak)
            else:
                scores = jnp.where(allowed, scores, -1e30)
                old = peak_ref[head]
                peak = jnp.maximum(old, jnp.max(scores, axis=1, keepdims=True))
                probs = jnp.where(allowed, jnp.exp(scores - peak), 0.0)
                rescale = jnp.exp(old - peak)
            row_sum = jnp.sum(probs, axis=1, keepdims=True)
            weighted = jnp.dot(
                probs.astype(jnp.bfloat16), values, preferred_element_type=jnp.float32
            )
            if allowed is not None:
                row_sum += sum_ref[head] * rescale
                weighted += acc_ref[head] * rescale
            peak_ref[head] = peak
            sum_ref[head] = row_sum
            acc_ref[head] = weighted

    attend(kv_ref, None)
    for ahead in range(1, tracts):

        @pl.when(tract >= ahead)
        def _():
            @pl.loop(0, n)
            def _(block):
                kv_copy(ahead, block).wait_recv()

            attend(kv_in.at[ahead - 1], visible_ref[0, lax.max(tract - ahead, 0)] > 0)

    for head in range(heads_here):
        attended = (acc_ref[head] / sum_ref[head]).astype(jnp.bfloat16)
        att_ref[:, :, head * HD : (head + 1) * HD] = attended.reshape(n, rows, HD)

    @pl.when(ends)
    def _():
        att_copy().start()

    load_out.wait()

    @pl.when(helper)
    def _():
        for by in range(chips):
            from_partner(by).wait_recv()
        att_copy().wait_recv()

    cols = width // halves

    def sum_copy(way, step, piece):
        side = (way + 1) // 2
        span = pl.ds(piece * cols, cols)
        return pltpu.make_async_remote_copy(
            src_ref=going.at[side, step].at[:, span],
            dst_ref=landed.at[side, step].at[:, span],
            send_sem=s_send.at[side, step, piece],
            recv_sem=s_recv.at[side, step, piece],
            device_id={"head": me + way},
            device_id_type=MESH,
        )

    def product(block, piece):
        return jnp.dot(
            att_ref[block],
            w_ref[:, piece * cols : (piece + 1) * cols],
            preferred_element_type=jnp.float32,
        )

    def far_product(block, piece):
        return jnp.dot(
            att_far[block],
            w_far[:, piece * cols : (piece + 1) * cols],
            preferred_element_type=jnp.float32,
        )

    def helps(way):
        return me == (1 if way == 1 else n - 2)

    def owner(way, step):
        return (n - 1 - step) if way == 1 else step

    def sum_sends(way, step):
        block = owner(way, step)
        return (block > me) & (me > 0) if way == 1 else (block < me) & (me < n - 1)

    def sum_receives(way, step):
        block = owner(way, step)
        return (block >= me) & (me > 1) if way == 1 else (block <= me) & (me < n - 2)

    @pl.loop(0, n - 1)
    def _(tick):
        for piece in range(halves):
            span = slice(piece * cols, (piece + 1) * cols)
            for way in (-1, 1):
                side = (way + 1) // 2
                step = tick - (me if way == 1 else n - 1 - me)
                held = (step >= 0) & (step < n - 1)

                @pl.when(held & sum_sends(way, step))
                def _():
                    going[side, step, :, span] = product(owner(way, step), piece).astype(
                        going.dtype
                    )

                    @pl.when(helps(way))
                    def _():
                        going[side, step, :, span] = (
                            going[side, step, :, span].astype(jnp.float32)
                            + far_product(owner(way, step), piece)
                        ).astype(going.dtype)

                    @pl.when(sum_receives(way, step))
                    def _():
                        sum_copy(way, step, piece).wait_recv()
                        going[side, step, :, span] = (
                            going[side, step, :, span].astype(jnp.float32)
                            + landed[side, step, :, span].astype(jnp.float32)
                        ).astype(going.dtype)

                    sum_copy(way, step, piece).start()

    for piece in range(halves):
        span = slice(piece * cols, (piece + 1) * cols)
        total_ref[:, span] = product(me, piece).astype(going.dtype).astype(jnp.float32)
    for piece in range(halves):
        span = slice(piece * cols, (piece + 1) * cols)
        for way in (-1, 1):
            side = (way + 1) // 2
            last = n - 1 - me if way == 1 else me

            @pl.when(helps(way))
            def _():
                total_ref[:, span] += far_product(me, piece)

            @pl.when(me > 1 if way == 1 else me < n - 2)
            def _():
                sum_copy(way, last, piece).wait_recv()
                total_ref[:, span] += landed[side, last, :, span].astype(jnp.float32)

        out_ref[0, :, span] = (
            total_ref[:, span] * table_ref[2, pl.ds(level, 1), span]
        ).astype(out_ref.dtype)

    @pl.loop(0, n - 1)
    def _(step):
        for piece in range(halves):
            for way in (-1, 1):

                @pl.when(sum_sends(way, step))
                def _():
                    sum_copy(way, step, piece).wait_send()

    @pl.loop(0, n)
    def _(block):
        for ahead in range(1, tracts):

            @pl.when(tract + ahead < tracts)
            def _():
                kv_copy(ahead, block).wait_send()

    @pl.loop(0, n - 1)
    def _(step):
        for piece in range(pieces):
            for way in (-1, 1):

                @pl.when(sends(way, step))
                def _():
                    copy(way, step, piece).wait_send()

    @pl.when(ends)
    def _():
        to_helper().wait_send()
        att_copy().wait_send()

    @pl.when(helper)
    def _():
        for by in range(1, chips):
            to_chip(by).wait_send()
        for by in range(chips):
            to_partner(by).wait_send()


def ring_body(frames, levels, visible, w_qkv, w_out, modulation):
    n, tracts = lax.axis_size("head"), lax.axis_size("tract")
    reps = lax.axis_size("rep")
    rows, width = frames.shape[1:]
    cols = w_qkv.shape[2]
    heads_here = cols // HD
    pieces = max(1, rows // 32)
    halves = 4 if width % 512 == 0 else 2
    vmem = pl.BlockSpec(memory_space=pltpu.VMEM)
    hbm = pl.BlockSpec(memory_space=pltpu.HBM)
    smem = pl.BlockSpec(memory_space=pltpu.SMEM)
    half = jnp.bfloat16
    dma = pltpu.SemaphoreType.DMA
    return pl.pallas_call(
        functools.partial(sublayer_kernel, n, tracts, reps, pieces, halves),
        out_shape=jax.ShapeDtypeStruct(frames.shape, frames.dtype),
        in_specs=[hbm, smem, smem, hbm, hbm, vmem],
        out_specs=vmem,
        scratch_shapes=[
            pltpu.VMEM((n, rows, width), half),
            pltpu.VMEM((3, width, cols), half),
            pltpu.VMEM(w_out.shape, half),
            pltpu.VMEM((n, rows, cols), half),
            pltpu.VMEM((n, 2, rows, cols), half),
            pltpu.VMEM((max(1, tracts - 1), n, 2, rows, cols), half),
            pltpu.VMEM((n, rows, cols), half),
            pltpu.VMEM((heads_here, n * rows, 1), jnp.float32),
            pltpu.VMEM((heads_here, n * rows, 1), jnp.float32),
            pltpu.VMEM((heads_here, n * rows, HD), jnp.float32),
            pltpu.VMEM((2, n - 1, rows, width), half),
            pltpu.VMEM((2, n - 1, rows, width), half),
            pltpu.VMEM((rows, width), jnp.float32),
            dma((3,)),
            dma((2, n, pieces)),
            dma((2, n, pieces)),
            dma((tracts, n)),
            dma((tracts, n)),
            dma((2, n, halves)),
            dma((2, n, halves)),
            pltpu.VMEM(w_out.shape, half),
            pltpu.VMEM((n, rows, cols), half),
            dma((tracts * reps + 1,)),
            dma((tracts * reps + 1,)),
        ],
        compiler_params=pltpu.CompilerParams(
            collective_id=0, has_side_effects=True, vmem_limit_bytes=GRANT
        ),
    )(
        frames,
        levels,
        visible,
        jnp.transpose(w_qkv, (1, 0, 2)),
        w_out,
        jnp.transpose(modulation, (1, 0, 2)),
    )


def line_kernel(
    n,
    tracts,
    reps,
    pieces,
    near,
    x_ref,
    level_ref,
    visible_ref,
    w_hbm,
    out_hbm,
    table_ref,
    out_ref,
    raw,
    got,
    wq_ref,
    w_far,
    wo_ref,
    acc_ref,
    q_ref,
    kv_ref,
    kv_in,
    part_ref,
    part_in,
    att_ref,
    peak_ref,
    sum_ref,
    mix_ref,
    att_all,
    out_part,
    out_in,
    load_sem,
    wq_sem,
    g_send,
    g_recv,
    f_send,
    f_recv,
    p_send,
    p_recv,
    kv_send,
    kv_recv,
    wo_send,
    wo_recv,
    z_send,
    z_recv,
    a_send,
    a_recv,
    o_send,
    o_recv,
):
    me, tract, rep = lax.axis_index("head"), lax.axis_index("tract"), lax.axis_index("rep")
    rows, width = x_ref.shape[1:]
    deep = width // pieces
    low = me < 2
    sign = jnp.where(low, 1, -1)
    base = jnp.where(low, 0, n - 1)
    is_end = (me == 0) | (me == n - 1)
    is_helper = (me == 1) | (me == n - 2)
    inner, outer = {"head": me + sign}, {"head": me - sign}

    def blk(r):
        return base + sign * r

    core, wide = tract % 2, tracts // 2
    chips = wide * reps
    seats = chips * 2
    chip = rep * wide + tract // 2
    seat = chip * 2 + core
    partner = {"tract": tract + 1 - 2 * core}

    def chip_at(by):
        return lax.rem(chip + by, chips)

    def place(which, side):
        return {"rep": which // wide, "tract": lax.rem(which, wide) * 2 + side}

    own_load = pltpu.make_async_copy(x_ref.at[0], raw, load_sem.at[0])
    own_load.start()
    cols_out = width // seats
    out_span = pl.ds(pl.multiple_of(seat * cols_out, 128), cols_out)
    wo_load = pltpu.make_async_copy(out_hbm.at[:, out_span], wo_ref.at[me], load_sem.at[1])

    def wq_load(p):
        span = pl.ds(pl.multiple_of(p * deep, deep), deep)
        return pltpu.make_async_copy(w_hbm.at[:, span], wq_ref.at[:, span], wq_sem.at[p])

    @pl.loop(0, pieces)
    def _(p):
        wq_load(p).start()

    wo_load.start()

    barrier = pltpu.get_barrier_semaphore()
    for ahead in range(1, n):
        other = lax.rem(me + ahead, n)
        pl.semaphore_signal(barrier, inc=1, device_id={"head": other}, device_id_type=MESH)
    for by in range(chips):
        for side in range(2):
            if by == 0 and side == 1:
                continue
            target = partner if by == 0 else place(chip_at(by), side)
            pl.semaphore_signal(barrier, inc=1, device_id=target, device_id_type=MESH)

    level = level_ref[0]

    def style(kind, start):
        return table_ref[kind, pl.ds(level, 1), start : start + deep]

    def remote(src, dst, send, recv, target):
        return pltpu.make_async_remote_copy(
            src_ref=src,
            dst_ref=dst,
            send_sem=send,
            recv_sem=recv,
            device_id=target,
            device_id_type=MESH,
        )

    def tok(way, r, p):
        b = blk(r)
        ref = got.at[b, p]
        target = inner if way == 0 else outer
        return remote(ref, ref, g_send.at[way, b, p], g_recv.at[b, p], target)

    far_rows = w_far.shape[1] // seats
    far_base = near * deep

    def far_span(which, side):
        start = (which * 2 + side) * far_rows
        return pl.ds(pl.multiple_of(start, far_rows), far_rows)

    def far_first(kind):
        start = far_base + seat * far_rows
        src = w_hbm.at[kind, pl.ds(pl.multiple_of(start, far_rows), far_rows)]
        dst = w_far.at[kind, far_span(chip, core)]
        return remote(src, dst, f_send.at[0, kind], f_recv.at[0, kind], inner)

    def far_chip(by, kind, which):
        ref = w_far.at[kind, far_span(which, core)]
        return remote(ref, ref, f_send.at[by, kind], f_recv.at[by, kind], place(chip_at(by), core))

    def far_out(by, kind):
        return far_chip(by, kind, chip)

    def far_in(by, kind):
        return far_chip(by, kind, chip_at(chips - by))

    def far_pass(by, kind, side):
        ref = w_far.at[kind, far_span(chip_at(chips - by), side)]
        where = chips + by
        return remote(ref, ref, f_send.at[where, kind], f_recv.at[where, kind], partner)

    def far_relay(kind):
        far_first(kind).wait_recv()
        for by in range(1, chips):
            far_out(by, kind).start()
        far_pass(0, kind, core).start()

    def far_hand(kind):
        for by in range(1, chips):
            far_in(by, kind).wait_recv()
            far_pass(by, kind, core).start()

    def far_ready(kind):
        for by in range(chips):
            far_pass(by, kind, 1 - core).wait_recv()

    def part_copy(r, kind):
        b = blk(r)
        return remote(
            part_ref.at[b, kind],
            part_in.at[b, kind],
            p_send.at[b, kind],
            p_recv.at[b, kind],
            outer,
        )

    def far_part(rs, kinds):
        for kind in kinds:
            total = None
            for p in range(near, pieces):
                lhs = jnp.concatenate([got[blk(r), p] for r in rs], axis=0)
                span = slice((p - near) * deep, (p - near + 1) * deep)
                made = jnp.dot(lhs, w_far[kind, span], preferred_element_type=jnp.float32)
                total = made if total is None else total + made
            total = total.astype(part_ref.dtype)
            for i, r in enumerate(rs):
                part_ref[blk(r), kind] = total[i * rows : (i + 1) * rows]
        for r in rs:
            for kind in kinds:
                part_copy(r, kind).start()

    cuts = wo_send.shape[2]
    wo_rows = wo_ref.shape[1] // cuts

    def wo_copy(way, r, cut):
        b = blk(r)
        ref = wo_ref.at[b, pl.ds(cut * wo_rows, wo_rows)]
        target = inner if way == 0 else outer
        return remote(ref, ref, wo_send.at[way, b, cut], wo_recv.at[b, cut], target)

    def wo_start(way, r):
        for cut in range(cuts):
            wo_copy(way, r, cut).start()

    def wo_forward(way, r):
        for cut in range(cuts):
            wo_copy(way, r, cut).wait_recv()
            wo_copy(way, r, cut).start()

    def kv_copy(ahead, block):
        return remote(
            kv_ref.at[block],
            kv_in.at[ahead - 1, block],
            kv_send.at[ahead - 1, block],
            kv_recv.at[ahead - 1, block],
            {"tract": tract + ahead},
        )

    def accumulate(rs, p):
        lhs = jnp.concatenate([got[blk(r), p] for r in rs], axis=0)
        span = pl.ds(pl.multiple_of(p * deep, deep), deep)
        for kind in range(3):
            made = jnp.dot(lhs, wq_ref[kind, span], preferred_element_type=jnp.float32)
            for i, r in enumerate(rs):
                acc_ref[blk(r), kind] += made[i * rows : (i + 1) * rows]

    def settle(r, kinds, extra=False):
        b = blk(r)
        for kind in kinds:
            made = acc_ref[b, kind]
            if extra:
                made = made + part_in[b, kind].astype(jnp.float32)
            made = made.astype(q_ref.dtype)
            if kind == 0:
                q_ref[b] = made
            else:
                kv_ref[b, kind - 1] = made

    def share(r):
        for ahead in range(1, tracts):

            @pl.when(tract + ahead < tracts)
            def _():
                kv_copy(ahead, blk(r)).start()

    acc_ref[...] = jnp.zeros_like(acc_ref)
    own_load.wait()
    power = jnp.zeros((rows, 1), jnp.float32)
    for p in range(pieces):
        tokens = raw[:, p * deep : (p + 1) * deep].astype(jnp.float32)
        power += jnp.sum(tokens * tokens, axis=-1, keepdims=True)
    factor = lax.rsqrt(power * (1.0 / width) + 1e-06)
    for p in range(pieces):
        tokens = raw[:, p * deep : (p + 1) * deep].astype(jnp.float32)
        shaped = tokens * factor * (1.0 + style(1, p * deep)) + style(0, p * deep)
        got[me, p] = shaped.astype(got.dtype)
    pl.semaphore_wait(barrier, n - 1 + seats - 1)

    @pl.when(is_end)
    def _():
        for kind in (1, 2, 0):
            far_first(kind).start()

        @pl.loop(0, pieces)
        def _(j):
            tok(0, 0, lax.rem(j + near, pieces)).start()

        wo_load.wait()
        wo_start(0, 0)

        @pl.loop(0, pieces)
        def _(p):
            wq_load(p).wait()
            accumulate((0,), p)

        settle(0, (1, 2, 0))
        share(0)
        for r in (1, 2):

            @pl.loop(0, near)
            def _(p):
                tok(0, r, p).wait_recv()
                accumulate((r,), p)

        for r in (1, 2):
            for kind in (1, 2):
                part_copy(r, kind).wait_recv()
            settle(r, (1, 2), True)
            share(r)

        @pl.loop(0, near)
        def _(p):
            tok(0, 3, p).wait_recv()
            accumulate((3,), p)

        for kind in (1, 2):
            part_copy(3, kind).wait_recv()
        settle(3, (1, 2), True)
        share(3)
        for r in (1, 2, 3):
            part_copy(r, 0).wait_recv()
            settle(r, (0,), True)

    @pl.when(is_helper)
    def _():
        @pl.loop(0, near)
        def _(p):
            tok(0, 1, p).start()
            tok(1, 1, p).start()

        @pl.loop(near, pieces)
        def _(p):
            tok(0, 1, p).start()

        wo_load.wait()

        @pl.loop(0, pieces)
        def _(p):
            wq_load(p).wait()
            tok(1, 2, p).wait_recv()

            @pl.when(p < near)
            def _():
                tok(1, 2, p).start()

            accumulate((1, 2), p)
            for at, kind in ((1, 1), (3, 2), (5, 0)):

                @pl.when(p == at)
                def _():
                    far_relay(kind)

            @pl.when(p == pieces - 2)
            def _():
                far_hand(1)

        settle(1, (1, 2, 0))
        share(1)
        settle(2, (1, 2, 0))
        share(2)
        wo_start(1, 1)
        far_ready(1)
        far_part((1, 2), (1,))

        @pl.loop(0, pieces)
        def _(j):
            p = lax.rem(j + near, pieces)
            tok(0, 0, p).wait_recv()
            tok(0, 0, p).start()
            tok(1, 3, p).wait_recv()

            @pl.when(p < near)
            def _():
                tok(1, 3, p).start()

            accumulate((0, 3), p)

            @pl.when(j == 2)
            def _():
                far_hand(2)

            @pl.when(j == 3)
            def _():
                far_ready(2)
                far_part((1, 2), (2,))

            @pl.when(j == 5)
            def _():
                far_hand(0)
                far_part((3,), (1, 2))
                far_ready(0)
                far_part((1, 2, 3), (0,))

        settle(0, (1, 2, 0))
        share(0)
        settle(3, (1, 2, 0))
        share(3)
        wo_start(0, 1)

    tokens_here = n * rows
    heads_here = q_ref.shape[2] // HD
    scale = HD ** (-0.5)

    def attend(source, allowed):
        for head in range(heads_here):
            lanes = slice(head * HD, (head + 1) * HD)
            queries = q_ref[:, :, lanes].reshape(tokens_here, HD)
            keys = source[:, 0, :, lanes].reshape(tokens_here, HD)
            values = source[:, 1, :, lanes].reshape(tokens_here, HD)
            scores = (
                lax.dot_general(
                    queries, keys, (((1,), (1,)), ((), ())), preferred_element_type=jnp.float32
                )
                * scale
            )
            if allowed is None:
                peak = jnp.max(scores, axis=1, keepdims=True)
                probs = jnp.exp(scores - peak)
            else:
                scores = jnp.where(allowed, scores, -1e30)
                old = peak_ref[head]
                peak = jnp.maximum(old, jnp.max(scores, axis=1, keepdims=True))
                probs = jnp.where(allowed, jnp.exp(scores - peak), 0.0)
                rescale = jnp.exp(old - peak)
            row_sum = jnp.sum(probs, axis=1, keepdims=True)
            weighted = jnp.dot(
                probs.astype(jnp.bfloat16), values, preferred_element_type=jnp.float32
            )
            if allowed is not None:
                row_sum += sum_ref[head] * rescale
                weighted += mix_ref[head] * rescale
            peak_ref[head] = peak
            sum_ref[head] = row_sum
            mix_ref[head] = weighted

    attend(kv_ref, None)

    @pl.when(is_helper)
    def _():
        wo_forward(0, 0)

    for ahead in range(1, tracts):

        @pl.when(tract >= ahead)
        def _():
            @pl.loop(0, n)
            def _(block):
                kv_copy(ahead, block).wait_recv()

            attend(kv_in.at[ahead - 1], visible_ref[0, lax.max(tract - ahead, 0)] > 0)

    for head in range(heads_here):
        attended = (mix_ref[head] / sum_ref[head]).astype(jnp.bfloat16)
        att_ref[:, :, head * HD : (head + 1) * HD] = attended.reshape(n, rows, HD)

    def att_line(other, source):
        return remote(
            att_ref.at[other],
            att_all.at[seat, source],
            z_send.at[other],
            z_recv.at[source],
            {"head": other},
        )

    for ahead in range(1, n):
        other = lax.rem(me + ahead, n)
        att_line(other, me).start()
    att_all[seat, me] = att_ref[me]

    @pl.when(is_helper)
    def _():
        wo_forward(1, 2)

    def att_chip(by, z, which):
        ref = att_all.at[which * 2 + core, z]
        return remote(ref, ref, a_send.at[by, z], a_recv.at[by, z], place(chip_at(by), core))

    def att_pass(by, z, side):
        ref = att_all.at[chip_at(chips - by) * 2 + side, z]
        where = chips + by
        return remote(ref, ref, a_send.at[where, z], a_recv.at[where, z], partner)

    for ahead in range(n):
        z = lax.rem(me + ahead, n)
        if ahead:
            att_line(z, z).wait_recv()
        for by in range(1, chips):
            att_chip(by, z, chip).start()
        att_pass(0, z, core).start()

    @pl.when(is_helper)
    def _():
        wo_forward(1, 3)

    for ahead in range(n):
        z = lax.rem(me + ahead, n)
        for by in range(1, chips):
            att_chip(by, z, chip_at(chips - by)).wait_recv()
            att_pass(by, z, core).start()

    @pl.when(is_end)
    def _():
        for r in (1, 2, 3):
            for cut in range(cuts):
                wo_copy(0, r, cut).wait_recv()

    def out_copy(which, side, source):
        return remote(
            out_part.at[which * 2 + side],
            out_in.at[source],
            o_send.at[which * 2 + side],
            o_recv.at[source],
            place(which, side),
        )

    heads_wide = wo_ref.shape[1]
    for step in range(1, chips + 1):
        by = step % chips
        which = chip_at(chips - by)
        for z in range(n):
            att_pass(by, z, 1 - core).wait_recv()
        total = None
        for z in range(n):
            lhs = att_all[pl.ds(which * 2, 2), z].reshape(2 * rows, heads_wide)
            made = jnp.dot(lhs, wo_ref[z], preferred_element_type=jnp.float32)
            total = made if total is None else total + made
        total = total.astype(out_part.dtype)
        for side in range(2):
            out_part[which * 2 + side] = total[side * rows : (side + 1) * rows]
        if by:
            for side in range(2):
                out_copy(which, side, seat).start()
        else:
            out_copy(chip, 1 - core, seat).start()

    def finish(ref, source):
        span = pl.ds(pl.multiple_of(source * cols_out, 128), cols_out)
        gate = table_ref[2, pl.ds(level, 1), span]
        out_ref[0, :, span] = (ref[source].astype(jnp.float32) * gate).astype(out_ref.dtype)

    finish(out_part, seat)
    for by in range(chips):
        for side in range(2):
            if by == 0 and side == 0:
                continue
            lane = core if side == 0 else 1 - core
            source = chip_at(chips - by) * 2 + lane
            out_copy(chip, core, source).wait_recv()
            finish(out_in, source)

    for by in range(chips):
        for side in range(2):
            if by == 0 and side == 0:
                continue
            lane = core if side == 0 else 1 - core
            out_copy(chip_at(chips - by), lane, seat).wait_send()
    for z in range(n):
        for by in range(1, chips):
            att_chip(by, z, chip).wait_send()
        for by in range(chips):
            att_pass(by, z, core).wait_send()
    for ahead in range(1, n):
        att_line(lax.rem(me + ahead, n), me).wait_send()

    @pl.loop(0, n)
    def _(block):
        for ahead in range(1, tracts):

            @pl.when(tract + ahead < tracts)
            def _():
                kv_copy(ahead, block).wait_send()

    @pl.when(is_end)
    def _():
        for kind in range(3):
            far_first(kind).wait_send()

        @pl.loop(0, pieces)
        def _(p):
            tok(0, 0, p).wait_send()

        for cut in range(cuts):
            wo_copy(0, 0, cut).wait_send()

    @pl.when(is_helper)
    def _():
        for kind in range(3):
            for by in range(1, chips):
                far_out(by, kind).wait_send()
            for by in range(chips):
                far_pass(by, kind, core).wait_send()
            for r in (1, 2, 3):
                part_copy(r, kind).wait_send()

        @pl.loop(0, pieces)
        def _(p):
            for r in (0, 1):
                tok(0, r, p).wait_send()

        @pl.loop(0, near)
        def _(p):
            for r in (1, 2, 3):
                tok(1, r, p).wait_send()

        for cut in range(cuts):
            for r in (0, 1):
                wo_copy(0, r, cut).wait_send()
            for r in (1, 2, 3):
                wo_copy(1, r, cut).wait_send()


PIECES = 8
NEAR = 4


def fits_line(n, tracts, reps, frames, w_out):
    rows, width = frames.shape[1:]
    seats = tracts * reps
    far = (PIECES - NEAR) * (width // PIECES)
    return (
        n == 4
        and tracts % 2 == 0
        and seats > 2
        and rows % 16 == 0
        and width % (PIECES * 128) == 0
        and width % (seats * 128) == 0
        and far % (seats * 16) == 0
        and w_out.shape[0] % 32 == 0
    )


def line_body(frames, levels, visible, w_qkv, w_out, modulation):
    n, tracts = lax.axis_size("head"), lax.axis_size("tract")
    reps = lax.axis_size("rep")
    rows, width = frames.shape[1:]
    cols = w_qkv.shape[2]
    heads_here = cols // HD
    seats = tracts * reps
    chips = seats // 2
    deep = width // PIECES
    vmem = pl.BlockSpec(memory_space=pltpu.VMEM)
    hbm = pl.BlockSpec(memory_space=pltpu.HBM)
    smem = pl.BlockSpec(memory_space=pltpu.SMEM)
    half = jnp.bfloat16
    dma = pltpu.SemaphoreType.DMA
    return pl.pallas_call(
        functools.partial(line_kernel, n, tracts, reps, PIECES, NEAR),
        out_shape=jax.ShapeDtypeStruct(frames.shape, frames.dtype),
        in_specs=[hbm, smem, smem, hbm, hbm, vmem],
        out_specs=vmem,
        scratch_shapes=[
            pltpu.VMEM((rows, width), half),
            pltpu.VMEM((n, PIECES, rows, deep), half),
            pltpu.VMEM((3, width, cols), half),
            pltpu.VMEM((3, (PIECES - NEAR) * deep, cols), half),
            pltpu.VMEM((n, w_out.shape[0], width // seats), half),
            pltpu.VMEM((n, 3, rows, cols), jnp.float32),
            pltpu.VMEM((n, rows, cols), half),
            pltpu.VMEM((n, 2, rows, cols), half),
            pltpu.VMEM((max(1, tracts - 1), n, 2, rows, cols), half),
            pltpu.VMEM((n, 3, rows, cols), half),
            pltpu.VMEM((n, 3, rows, cols), half),
            pltpu.VMEM((n, rows, cols), half),
            pltpu.VMEM((heads_here, n * rows, 1), jnp.float32),
            pltpu.VMEM((heads_here, n * rows, 1), jnp.float32),
            pltpu.VMEM((heads_here, n * rows, HD), jnp.float32),
            pltpu.VMEM((seats, n, rows, cols), half),
            pltpu.VMEM((seats, rows, width // seats), half),
            pltpu.VMEM((seats, rows, width // seats), half),
            dma((2,)),
            dma((PIECES,)),
            dma((2, n, PIECES)),
            dma((n, PIECES)),
            dma((2 * chips, 3)),
            dma((2 * chips, 3)),
            dma((n, 3)),
            dma((n, 3)),
            dma((tracts, n)),
            dma((tracts, n)),
            dma((2, n, 2)),
            dma((n, 2)),
            dma((n,)),
            dma((n,)),
            dma((2 * chips, n)),
            dma((2 * chips, n)),
            dma((seats,)),
            dma((seats,)),
        ],
        compiler_params=pltpu.CompilerParams(
            collective_id=0, has_side_effects=True, vmem_limit_bytes=GRANT
        ),
    )(
        frames,
        levels,
        visible,
        jnp.transpose(w_qkv, (1, 0, 2)),
        w_out,
        jnp.transpose(modulation, (1, 0, 2)),
    )


def body(frames, levels, visible, w_qkv, w_out, modulation):
    n, tracts = lax.axis_size("head"), lax.axis_size("tract")
    reps = lax.axis_size("rep")
    line = fits_line(n, tracts, reps, frames, w_out)
    chosen = line_body if line else ring_body
    return chosen(frames, levels, visible, w_qkv, w_out, modulation)


def solution(mesh):
    placed = (
        P(("rep", "tract"), "head", None),
        P(("rep", "tract")),
        P(("rep", "tract"), None),
        P(None, None, "head"),
        P("head", None),
        P(),
    )
    return jax.shard_map(
        body,
        mesh=mesh,
        in_specs=placed,
        out_specs=P(("rep", "tract"), "head", None),
        check_vma=False,
    )
```

```python
import functools

import jax
import jax.numpy as jnp
from jax import lax
from jax.experimental import pallas as pl
from jax.experimental.pallas import tpu as pltpu
from jax.sharding import PartitionSpec as P

HD = 128
GRANT = 60 * 1024 * 1024
MESH = pl.DeviceIdType.MESH


def meet(n, me, tracts, tract, others):
    barrier = pltpu.get_barrier_semaphore()
    for other in (lax.rem(me + 1, n), lax.rem(me + n - 1, n)):
        pl.semaphore_signal(barrier, inc=1, device_id={"head": other}, device_id_type=MESH)
    for ahead in range(1, tracts):
        other = lax.rem(tract + ahead, tracts)
        pl.semaphore_signal(barrier, inc=1, device_id={"tract": other}, device_id_type=MESH)
    for other in others:
        pl.semaphore_signal(barrier, inc=1, device_id=other, device_id_type=MESH)
    pl.semaphore_wait(barrier, 1 + tracts + len(others))


def sublayer_kernel(
    n,
    tracts,
    reps,
    pieces,
    halves,
    x_ref,
    level_ref,
    visible_ref,
    w_hbm,
    out_hbm,
    table_ref,
    out_ref,
    got,
    wq_ref,
    w_ref,
    q_ref,
    kv_ref,
    kv_in,
    att_ref,
    peak_ref,
    sum_ref,
    acc_ref,
    going,
    landed,
    total_ref,
    load_sem,
    g_send,
    g_recv,
    kv_send,
    kv_recv,
    s_send,
    s_recv,
    w_far,
    att_far,
    f_send,
    f_recv,
):
    me, tract = lax.axis_index("head"), lax.axis_index("tract")
    own = pltpu.make_async_copy(x_ref.at[0], got.at[me], load_sem.at[0])
    own.start()
    load = pltpu.make_async_copy(w_hbm, wq_ref, load_sem.at[1])
    load.start()
    load_out = pltpu.make_async_copy(out_hbm, w_ref, load_sem.at[2])
    load_out.start()
    core, wide = tract % 2, tracts // 2
    chips = wide * reps
    chip = lax.axis_index("rep") * wide + tract // 2
    slab = w_ref.shape[0] // (2 * chips)
    helper = (me == 1) | (me == n - 2)
    ends = (me == 0) | (me == n - 1)

    def seat(by):
        other = lax.rem(chip + by, chips)
        return {"rep": other // wide, "tract": lax.rem(other, wide) * 2 + core}

    def slab_of(which, side):
        start = pl.multiple_of((which * 2 + side) * slab, slab)
        return pl.ds(start, slab)

    def far_copy(kind, span, target, source=None):
        return pltpu.make_async_remote_copy(
            src_ref=(w_far if source is None else source).at[span],
            dst_ref=w_far.at[span],
            send_sem=f_send.at[kind],
            recv_sem=f_recv.at[kind],
            device_id=target,
            device_id_type=MESH,
        )

    inward = {"head": jnp.where(me == 0, 1, n - 2)}
    partner = {"tract": tract + 1 - 2 * core}
    mine = slab_of(chip, core)

    def to_helper():
        return far_copy(0, mine, inward, out_hbm)

    def to_chip(by):
        return far_copy(by, mine, seat(by))

    def from_chip(by):
        return far_copy(by, slab_of(lax.rem(chip + chips - by, chips), core), seat(by))

    def to_partner(by):
        span = slab_of(lax.rem(chip + chips - by, chips), core)
        return far_copy(chips + by, span, partner)

    def from_partner(by):
        span = slab_of(lax.rem(chip + chips - by, chips), 1 - core)
        return far_copy(chips + by, span, partner)

    def att_copy():
        return pltpu.make_async_remote_copy(
            src_ref=att_ref,
            dst_ref=att_far,
            send_sem=f_send.at[2 * chips],
            recv_sem=f_recv.at[2 * chips],
            device_id=inward,
            device_id_type=MESH,
        )

    meet(n, me, tracts, tract, [seat(by) for by in range(1, chips)])
    level = level_ref[0]

    def style(kind):
        return table_ref[kind, pl.ds(level, 1), :]

    rows, width = x_ref.shape[1:]
    part = rows // pieces

    def copy(way, step, piece, first=False):
        side = (way + 1) // 2
        span = pl.ds(piece * part, part)
        block = me - way * step
        return pltpu.make_async_remote_copy(
            src_ref=(x_ref.at[0] if first else got.at[block]).at[span],
            dst_ref=got.at[block].at[span],
            send_sem=g_send.at[side, step, piece],
            recv_sem=g_recv.at[side, step, piece],
            device_id={"head": me + way},
            device_id_type=MESH,
        )

    def arrival(way, step, piece):
        side = (way + 1) // 2
        span = pl.ds(piece * part, part)
        return pltpu.make_async_remote_copy(
            src_ref=x_ref.at[0].at[span],
            dst_ref=got.at[me - way * (step + 1)].at[span],
            send_sem=g_send.at[side, step, piece],
            recv_sem=g_recv.at[side, step, piece],
            device_id={"head": me - way},
            device_id_type=MESH,
        )

    def sends(way, step):
        block, target = me - way * step, me + way
        return (block >= 0) & (block < n) & (target >= 0) & (target < n) & (step < n - 1)

    def receives(way, step):
        block = me - way * (step + 1)
        return (block >= 0) & (block < n)

    def kv_copy(ahead, block):
        return pltpu.make_async_remote_copy(
            src_ref=kv_ref.at[block],
            dst_ref=kv_in.at[ahead - 1, block],
            send_sem=kv_send.at[ahead - 1, block],
            recv_sem=kv_recv.at[ahead - 1, block],
            device_id={"tract": tract + ahead},
            device_id_type=MESH,
        )

    def project(block):
        tokens = got[block].astype(jnp.float32)
        power = jnp.mean(tokens * tokens, axis=-1, keepdims=True)
        normed = tokens * lax.rsqrt(power + 1e-06)
        shaped = (normed * (1.0 + style(1)) + style(0)).astype(jnp.bfloat16)
        for kind in (1, 2, 0):
            made = jnp.dot(shaped, wq_ref[kind], preferred_element_type=jnp.float32)
            made = made.astype(jnp.bfloat16)
            if kind == 0:
                q_ref[block] = made
            else:
                kv_ref[block, kind - 1] = made
            if kind == 2:
                for ahead in range(1, tracts):

                    @pl.when(tract + ahead < tracts)
                    def _():
                        kv_copy(ahead, block).start()

    for piece in range(pieces):
        for way in (-1, 1):

            @pl.when(sends(way, 0))
            def _():
                copy(way, 0, piece, True).start()

    @pl.when(ends)
    def _():
        to_helper().start()

    own.wait()
    load.wait()
    project(me)

    @pl.loop(0, n - 1)
    def _(step):
        for piece in range(pieces):
            for way in (-1, 1):

                @pl.when(receives(way, step))
                def _():
                    arrival(way, step, piece).wait_recv()

                @pl.when(sends(way, step + 1))
                def _():
                    copy(way, step + 1, piece).start()

        @pl.loop(0, 2)
        def _(side):
            way = 2 * side - 1

            @pl.when(receives(way, step))
            def _():
                project(me - way * (step + 1))

        @pl.when(helper & (step == 0))
        def _():
            to_helper().wait_recv()
            for by in range(1, chips):
                to_chip(by).start()
            to_partner(0).start()

    @pl.when(helper)
    def _():
        for by in range(1, chips):
            from_chip(by).wait_recv()
            to_partner(by).start()

    tokens_here = n * rows
    heads_here = q_ref.shape[2] // HD
    scale = HD ** (-0.5)

    def attend(source, allowed):
        for head in range(heads_here):
            lanes = slice(head * HD, (head + 1) * HD)
            queries = q_ref[:, :, lanes].reshape(tokens_here, HD)
            keys = source[:, 0, :, lanes].reshape(tokens_here, HD)
            values = source[:, 1, :, lanes].reshape(tokens_here, HD)
            scores = (
                lax.dot_general(
                    queries, keys, (((1,), (1,)), ((), ())), preferred_element_type=jnp.float32
                )
                * scale
            )
            if allowed is None:
                peak = jnp.max(scores, axis=1, keepdims=True)
                probs = jnp.exp(scores - peak)
            else:
                scores = jnp.where(allowed, scores, -1e30)
                old = peak_ref[head]
                peak = jnp.maximum(old, jnp.max(scores, axis=1, keepdims=True))
                probs = jnp.where(allowed, jnp.exp(scores - peak), 0.0)
                rescale = jnp.exp(old - peak)
            row_sum = jnp.sum(probs, axis=1, keepdims=True)
            weighted = jnp.dot(
                probs.astype(jnp.bfloat16), values, preferred_element_type=jnp.float32
            )
            if allowed is not None:
                row_sum += sum_ref[head] * rescale
                weighted += acc_ref[head] * rescale
            peak_ref[head] = peak
            sum_ref[head] = row_sum
            acc_ref[head] = weighted

    attend(kv_ref, None)
    for ahead in range(1, tracts):

        @pl.when(tract >= ahead)
        def _():
            @pl.loop(0, n)
            def _(block):
                kv_copy(ahead, block).wait_recv()

            attend(kv_in.at[ahead - 1], visible_ref[0, lax.max(tract - ahead, 0)] > 0)

    for head in range(heads_here):
        attended = (acc_ref[head] / sum_ref[head]).astype(jnp.bfloat16)
        att_ref[:, :, head * HD : (head + 1) * HD] = attended.reshape(n, rows, HD)

    @pl.when(ends)
    def _():
        att_copy().start()

    load_out.wait()

    @pl.when(helper)
    def _():
        for by in range(chips):
            from_partner(by).wait_recv()
        att_copy().wait_recv()

    cols = width // halves

    def sum_copy(way, step, piece):
        side = (way + 1) // 2
        span = pl.ds(piece * cols, cols)
        return pltpu.make_async_remote_copy(
            src_ref=going.at[side, step].at[:, span],
            dst_ref=landed.at[side, step].at[:, span],
            send_sem=s_send.at[side, step, piece],
            recv_sem=s_recv.at[side, step, piece],
            device_id={"head": me + way},
            device_id_type=MESH,
        )

    def product(block, piece):
        return jnp.dot(
            att_ref[block],
            w_ref[:, piece * cols : (piece + 1) * cols],
            preferred_element_type=jnp.float32,
        )

    def far_product(block, piece):
        return jnp.dot(
            att_far[block],
            w_far[:, piece * cols : (piece + 1) * cols],
            preferred_element_type=jnp.float32,
        )

    def helps(way):
        return me == (1 if way == 1 else n - 2)

    def owner(way, step):
        return (n - 1 - step) if way == 1 else step

    def sum_sends(way, step):
        block = owner(way, step)
        return (block > me) & (me > 0) if way == 1 else (block < me) & (me < n - 1)

    def sum_receives(way, step):
        block = owner(way, step)
        return (block >= me) & (me > 1) if way == 1 else (block <= me) & (me < n - 2)

    @pl.loop(0, n - 1)
    def _(tick):
        for piece in range(halves):
            span = slice(piece * cols, (piece + 1) * cols)
            for way in (-1, 1):
                side = (way + 1) // 2
                step = tick - (me if way == 1 else n - 1 - me)
                held = (step >= 0) & (step < n - 1)

                @pl.when(held & sum_sends(way, step))
                def _():
                    going[side, step, :, span] = product(owner(way, step), piece).astype(
                        going.dtype
                    )

                    @pl.when(helps(way))
                    def _():
                        going[side, step, :, span] = (
                            going[side, step, :, span].astype(jnp.float32)
                            + far_product(owner(way, step), piece)
                        ).astype(going.dtype)

                    @pl.when(sum_receives(way, step))
                    def _():
                        sum_copy(way, step, piece).wait_recv()
                        going[side, step, :, span] = (
                            going[side, step, :, span].astype(jnp.float32)
                            + landed[side, step, :, span].astype(jnp.float32)
                        ).astype(going.dtype)

                    sum_copy(way, step, piece).start()

    for piece in range(halves):
        span = slice(piece * cols, (piece + 1) * cols)
        total_ref[:, span] = product(me, piece).astype(going.dtype).astype(jnp.float32)
    for piece in range(halves):
        span = slice(piece * cols, (piece + 1) * cols)
        for way in (-1, 1):
            side = (way + 1) // 2
            last = n - 1 - me if way == 1 else me

            @pl.when(helps(way))
            def _():
                total_ref[:, span] += far_product(me, piece)

            @pl.when(me > 1 if way == 1 else me < n - 2)
            def _():
                sum_copy(way, last, piece).wait_recv()
                total_ref[:, span] += landed[side, last, :, span].astype(jnp.float32)

        out_ref[0, :, span] = (
            total_ref[:, span] * table_ref[2, pl.ds(level, 1), span]
        ).astype(out_ref.dtype)

    @pl.loop(0, n - 1)
    def _(step):
        for piece in range(halves):
            for way in (-1, 1):

                @pl.when(sum_sends(way, step))
                def _():
                    sum_copy(way, step, piece).wait_send()

    @pl.loop(0, n)
    def _(block):
        for ahead in range(1, tracts):

            @pl.when(tract + ahead < tracts)
            def _():
                kv_copy(ahead, block).wait_send()

    @pl.loop(0, n - 1)
    def _(step):
        for piece in range(pieces):
            for way in (-1, 1):

                @pl.when(sends(way, step))
                def _():
                    copy(way, step, piece).wait_send()

    @pl.when(ends)
    def _():
        to_helper().wait_send()
        att_copy().wait_send()

    @pl.when(helper)
    def _():
        for by in range(1, chips):
            to_chip(by).wait_send()
        for by in range(chips):
            to_partner(by).wait_send()


def ring_body(frames, levels, visible, w_qkv, w_out, modulation):
    n, tracts = lax.axis_size("head"), lax.axis_size("tract")
    reps = lax.axis_size("rep")
    rows, width = frames.shape[1:]
    cols = w_qkv.shape[2]
    heads_here = cols // HD
    pieces = max(1, rows // 32)
    halves = 4 if width % 512 == 0 else 2
    vmem = pl.BlockSpec(memory_space=pltpu.VMEM)
    hbm = pl.BlockSpec(memory_space=pltpu.HBM)
    smem = pl.BlockSpec(memory_space=pltpu.SMEM)
    half = jnp.bfloat16
    dma = pltpu.SemaphoreType.DMA
    return pl.pallas_call(
        functools.partial(sublayer_kernel, n, tracts, reps, pieces, halves),
        out_shape=jax.ShapeDtypeStruct(frames.shape, frames.dtype),
        in_specs=[hbm, smem, smem, hbm, hbm, vmem],
        out_specs=vmem,
        scratch_shapes=[
            pltpu.VMEM((n, rows, width), half),
            pltpu.VMEM((3, width, cols), half),
            pltpu.VMEM(w_out.shape, half),
            pltpu.VMEM((n, rows, cols), half),
            pltpu.VMEM((n, 2, rows, cols), half),
            pltpu.VMEM((max(1, tracts - 1), n, 2, rows, cols), half),
            pltpu.VMEM((n, rows, cols), half),
            pltpu.VMEM((heads_here, n * rows, 1), jnp.float32),
            pltpu.VMEM((heads_here, n * rows, 1), jnp.float32),
            pltpu.VMEM((heads_here, n * rows, HD), jnp.float32),
            pltpu.VMEM((2, n - 1, rows, width), half),
            pltpu.VMEM((2, n - 1, rows, width), half),
            pltpu.VMEM((rows, width), jnp.float32),
            dma((3,)),
            dma((2, n, pieces)),
            dma((2, n, pieces)),
            dma((tracts, n)),
            dma((tracts, n)),
            dma((2, n, halves)),
            dma((2, n, halves)),
            pltpu.VMEM(w_out.shape, half),
            pltpu.VMEM((n, rows, cols), half),
            dma((tracts * reps + 1,)),
            dma((tracts * reps + 1,)),
        ],
        compiler_params=pltpu.CompilerParams(
            collective_id=0, has_side_effects=True, vmem_limit_bytes=GRANT
        ),
    )(
        frames,
        levels,
        visible,
        jnp.transpose(w_qkv, (1, 0, 2)),
        w_out,
        jnp.transpose(modulation, (1, 0, 2)),
    )


def line_kernel(
    n,
    tracts,
    reps,
    pieces,
    near,
    x_ref,
    level_ref,
    visible_ref,
    w_hbm,
    out_hbm,
    table_hbm,
    out_ref,
    table_ref,
    raw,
    got,
    wq_ref,
    w_far,
    wo_ref,
    acc_ref,
    q_ref,
    kv_ref,
    kv_in,
    part_ref,
    part_in,
    att_ref,
    peak_ref,
    sum_ref,
    mix_ref,
    att_all,
    out_part,
    out_in,
    load_sem,
    wq_sem,
    wo_sem,
    g_send,
    g_recv,
    f_send,
    f_recv,
    p_send,
    p_recv,
    kv_send,
    kv_recv,
    wo_send,
    wo_recv,
    z_send,
    z_recv,
    a_send,
    a_recv,
    o_send,
    o_recv,
):
    me, tract, rep = lax.axis_index("head"), lax.axis_index("tract"), lax.axis_index("rep")
    rows, width = x_ref.shape[1:]
    deep = width // pieces
    low = me < 2
    sign = jnp.where(low, 1, -1)
    base = jnp.where(low, 0, n - 1)
    is_end = (me == 0) | (me == n - 1)
    is_helper = (me == 1) | (me == n - 2)
    inner, outer = {"head": me + sign}, {"head": me - sign}

    def blk(r):
        return base + sign * r

    core, wide = tract % 2, tracts // 2
    chips = wide * reps
    seats = chips * 2
    chip = rep * wide + tract // 2
    seat = chip * 2 + core
    partner = {"tract": tract + 1 - 2 * core}

    def chip_at(by):
        return lax.rem(chip + by, chips)

    def place(which, side):
        return {"rep": which // wide, "tract": lax.rem(which, wide) * 2 + side}

    own_load = pltpu.make_async_copy(x_ref.at[0], raw, load_sem.at[0])
    own_load.start()
    table_load = pltpu.make_async_copy(table_hbm, table_ref, load_sem.at[1])
    table_load.start()
    cols_out = width // seats
    cuts = wo_ref.shape[1]
    cut_cols = cols_out // cuts

    def wo_load(cut):
        start = pl.multiple_of(seat * cols_out + cut * cut_cols, 128)
        src = out_hbm.at[:, pl.ds(start, cut_cols)]
        return pltpu.make_async_copy(src, wo_ref.at[me, cut], wo_sem.at[cut])


    def wq_load(p):
        span = pl.ds(pl.multiple_of(p * deep, deep), deep)
        return pltpu.make_async_copy(w_hbm.at[:, span], wq_ref.at[:, span], wq_sem.at[p])

    @pl.loop(0, pieces)
    def _(p):
        wq_load(p).start()

    for cut in range(cuts):
        wo_load(cut).start()

    barrier = pltpu.get_barrier_semaphore()
    for ahead in range(1, n):
        other = lax.rem(me + ahead, n)
        pl.semaphore_signal(barrier, inc=1, device_id={"head": other}, device_id_type=MESH)
    for by in range(chips):
        for side in range(2):
            if by == 0 and side == 1:
                continue
            target = partner if by == 0 else place(chip_at(by), side)
            pl.semaphore_signal(barrier, inc=1, device_id=target, device_id_type=MESH)

    level = level_ref[0]

    def style(kind, start):
        return table_ref[kind, pl.ds(level, 1), start : start + deep]

    def remote(src, dst, send, recv, target):
        return pltpu.make_async_remote_copy(
            src_ref=src,
            dst_ref=dst,
            send_sem=send,
            recv_sem=recv,
            device_id=target,
            device_id_type=MESH,
        )

    def tok(way, r, p):
        b = blk(r)
        ref = got.at[b, p]
        target = inner if way == 0 else outer
        return remote(ref, ref, g_send.at[way, b, p], g_recv.at[b, p], target)

    far_rows = w_far.shape[1] // seats
    far_base = near * deep

    def far_span(which, side):
        start = (which * 2 + side) * far_rows
        return pl.ds(pl.multiple_of(start, far_rows), far_rows)

    def far_first(kind):
        start = far_base + seat * far_rows
        src = w_hbm.at[kind, pl.ds(pl.multiple_of(start, far_rows), far_rows)]
        dst = w_far.at[kind, far_span(chip, core)]
        return remote(src, dst, f_send.at[0, kind], f_recv.at[0, kind], inner)

    def far_chip(by, kind, which):
        ref = w_far.at[kind, far_span(which, core)]
        return remote(ref, ref, f_send.at[by, kind], f_recv.at[by, kind], place(chip_at(by), core))

    def far_out(by, kind):
        return far_chip(by, kind, chip)

    def far_in(by, kind):
        return far_chip(by, kind, chip_at(chips - by))

    def far_pass(by, kind, side):
        ref = w_far.at[kind, far_span(chip_at(chips - by), side)]
        where = chips + by
        return remote(ref, ref, f_send.at[where, kind], f_recv.at[where, kind], partner)

    def far_relay(kind):
        far_first(kind).wait_recv()
        for by in range(1, chips):
            far_out(by, kind).start()
        far_pass(0, kind, core).start()

    def far_hand(kind):
        for by in range(1, chips):
            far_in(by, kind).wait_recv()
            far_pass(by, kind, core).start()

    def far_ready(kind):
        for by in range(chips):
            far_pass(by, kind, 1 - core).wait_recv()

    def part_copy(r, kind):
        b = blk(r)
        return remote(
            part_ref.at[b, kind],
            part_in.at[b, kind],
            p_send.at[b, kind],
            p_recv.at[b, kind],
            outer,
        )

    def far_part(rs, kinds):
        for kind in kinds:
            total = None
            for p in range(near, pieces):
                lhs = jnp.concatenate([got[blk(r), p] for r in rs], axis=0)
                span = slice((p - near) * deep, (p - near + 1) * deep)
                made = jnp.dot(lhs, w_far[kind, span], preferred_element_type=jnp.float32)
                total = made if total is None else total + made
            total = total.astype(part_ref.dtype)
            for i, r in enumerate(rs):
                part_ref[blk(r), kind] = total[i * rows : (i + 1) * rows]
        for r in rs:
            for kind in kinds:
                part_copy(r, kind).start()

    def wo_copy(way, r, cut):
        b = blk(r)
        ref = wo_ref.at[b, cut]
        target = inner if way == 0 else outer
        return remote(ref, ref, wo_send.at[way, b, cut], wo_recv.at[b, cut], target)

    def wo_start(way, r, which):
        for cut in which:
            wo_copy(way, r, cut).start()

    def wo_forward(way, r, cut):
        wo_copy(way, r, cut).wait_recv()
        wo_copy(way, r, cut).start()

    def kv_copy(ahead, block):
        return remote(
            kv_ref.at[block],
            kv_in.at[ahead - 1, block],
            kv_send.at[ahead - 1, block],
            kv_recv.at[ahead - 1, block],
            {"tract": tract + ahead},
        )

    def accumulate(rs, p):
        lhs = jnp.concatenate([got[blk(r), p] for r in rs], axis=0)
        span = pl.ds(pl.multiple_of(p * deep, deep), deep)
        for kind in range(3):
            made = jnp.dot(lhs, wq_ref[kind, span], preferred_element_type=jnp.float32)
            for i, r in enumerate(rs):
                acc_ref[blk(r), kind] += made[i * rows : (i + 1) * rows]

    def settle(r, kinds, extra=False):
        b = blk(r)
        for kind in kinds:
            made = acc_ref[b, kind]
            if extra:
                made = made + part_in[b, kind].astype(jnp.float32)
            made = made.astype(q_ref.dtype)
            if kind == 0:
                q_ref[b] = made
            else:
                kv_ref[b, kind - 1] = made

    def share(r):
        for ahead in range(1, tracts):

            @pl.when(tract + ahead < tracts)
            def _():
                kv_copy(ahead, blk(r)).start()

    acc_ref[...] = jnp.zeros_like(acc_ref)
    own_load.wait()
    power = jnp.zeros((rows, 1), jnp.float32)
    for p in range(pieces):
        tokens = raw[:, p * deep : (p + 1) * deep].astype(jnp.float32)
        power += jnp.sum(tokens * tokens, axis=-1, keepdims=True)
    table_load.wait()
    factor = lax.rsqrt(power * (1.0 / width) + 1e-06)
    for p in range(pieces):
        tokens = raw[:, p * deep : (p + 1) * deep].astype(jnp.float32)
        shaped = tokens * factor * (1.0 + style(1, p * deep)) + style(0, p * deep)
        got[me, p] = shaped.astype(got.dtype)
    pl.semaphore_wait(barrier, n - 1 + seats - 1)

    @pl.when(is_end)
    def _():
        for kind in (1, 2, 0):
            far_first(kind).start()

        @pl.loop(0, pieces)
        def _(j):
            tok(0, 0, lax.rem(j + near, pieces)).start()

        @pl.loop(0, pieces)
        def _(p):
            wq_load(p).wait()
            accumulate((0,), p)

        for cut in range(cuts):
            wo_load(cut).wait()
        wo_start(0, 0, range(cuts))

        settle(0, (1, 2, 0))
        share(0)
        for r in (1, 2):

            @pl.loop(0, near)
            def _(p):
                tok(0, r, p).wait_recv()
                accumulate((r,), p)

        for r in (1, 2):
            for kind in (1, 2):
                part_copy(r, kind).wait_recv()
            settle(r, (1, 2), True)
            share(r)

        @pl.loop(0, near)
        def _(p):
            tok(0, 3, p).wait_recv()
            accumulate((3,), p)

        for kind in (1, 2):
            part_copy(3, kind).wait_recv()
        settle(3, (1, 2), True)
        share(3)
        for r in (1, 2, 3):
            part_copy(r, 0).wait_recv()
            settle(r, (0,), True)

    @pl.when(is_helper)
    def _():
        @pl.loop(0, near)
        def _(p):
            tok(0, 1, p).start()
            tok(1, 1, p).start()

        @pl.loop(near, pieces)
        def _(p):
            tok(0, 1, p).start()

        @pl.loop(0, pieces)
        def _(p):
            wq_load(p).wait()
            tok(1, 2, p).wait_recv()

            @pl.when(p < near)
            def _():
                tok(1, 2, p).start()

            accumulate((1, 2), p)
            for at, kind in ((1, 1), (3, 2), (5, 0)):

                @pl.when(p == at)
                def _():
                    far_relay(kind)

            @pl.when(p == pieces - 2)
            def _():
                far_hand(1)

        settle(1, (1, 2, 0))
        share(1)
        settle(2, (1, 2, 0))
        share(2)
        for cut in range(cuts):
            wo_load(cut).wait()
        wo_start(1, 1, range(cuts))
        far_ready(1)
        far_part((1, 2), (1,))

        def pass_on(j):
            p = lax.rem(j + near, pieces)
            tok(0, 0, p).wait_recv()
            tok(0, 0, p).start()

        @pl.loop(0, 2)
        def _(j):
            pass_on(j)

        @pl.loop(0, pieces)
        def _(j):
            @pl.when(j + 2 < pieces)
            def _():
                pass_on(j + 2)

            p = lax.rem(j + near, pieces)
            tok(1, 3, p).wait_recv()

            @pl.when(p < near)
            def _():
                tok(1, 3, p).start()

            accumulate((0, 3), p)

            @pl.when(j == 2)
            def _():
                far_hand(2)

            @pl.when(j == 3)
            def _():
                far_ready(2)
                far_part((1, 2), (2,))

            @pl.when(j == 5)
            def _():
                far_hand(0)
                far_part((3,), (1, 2))
                far_ready(0)
                far_part((1, 2, 3), (0,))

        settle(0, (1, 2, 0))
        share(0)
        settle(3, (1, 2, 0))
        share(3)
        for cut in range(cuts - 1):
            wo_start(0, 1, (cut,))
            wo_forward(0, 0, cut)

    tokens_here = n * rows
    heads_here = q_ref.shape[2] // HD
    scale = HD ** (-0.5)

    def attend(source, allowed):
        for head in range(heads_here):
            lanes = slice(head * HD, (head + 1) * HD)
            queries = q_ref[:, :, lanes].reshape(tokens_here, HD)
            keys = source[:, 0, :, lanes].reshape(tokens_here, HD)
            values = source[:, 1, :, lanes].reshape(tokens_here, HD)
            scores = (
                lax.dot_general(
                    queries, keys, (((1,), (1,)), ((), ())), preferred_element_type=jnp.float32
                )
                * scale
            )
            if allowed is None:
                peak = jnp.max(scores, axis=1, keepdims=True)
                probs = jnp.exp(scores - peak)
            else:
                scores = jnp.where(allowed, scores, -1e30)
                old = peak_ref[head]
                peak = jnp.maximum(old, jnp.max(scores, axis=1, keepdims=True))
                probs = jnp.where(allowed, jnp.exp(scores - peak), 0.0)
                rescale = jnp.exp(old - peak)
            row_sum = jnp.sum(probs, axis=1, keepdims=True)
            weighted = jnp.dot(
                probs.astype(jnp.bfloat16), values, preferred_element_type=jnp.float32
            )
            if allowed is not None:
                row_sum += sum_ref[head] * rescale
                weighted += mix_ref[head] * rescale
            peak_ref[head] = peak
            sum_ref[head] = row_sum
            mix_ref[head] = weighted

    attend(kv_ref, None)

    for ahead in range(1, tracts):

        @pl.when(tract >= ahead)
        def _():
            @pl.loop(0, n)
            def _(block):
                kv_copy(ahead, block).wait_recv()

            attend(kv_in.at[ahead - 1], visible_ref[0, lax.max(tract - ahead, 0)] > 0)

    for head in range(heads_here):
        attended = (mix_ref[head] / sum_ref[head]).astype(jnp.bfloat16)
        att_ref[:, :, head * HD : (head + 1) * HD] = attended.reshape(n, rows, HD)

    def att_line(other, source):
        return remote(
            att_ref.at[other],
            att_all.at[seat, source],
            z_send.at[other],
            z_recv.at[source],
            {"head": other},
        )

    for ahead in range(1, n):
        other = lax.rem(me + ahead, n)
        att_line(other, me).start()
    att_all[seat, me] = att_ref[me]

    @pl.when(is_helper)
    def _():
        wo_start(0, 1, (cuts - 1,))
        wo_forward(0, 0, cuts - 1)
        for cut in range(cuts - 1):
            for r in (2, 3):
                wo_forward(1, r, cut)

    def att_chip(by, z, which):
        ref = att_all.at[which * 2 + core, z]
        return remote(ref, ref, a_send.at[by, z], a_recv.at[by, z], place(chip_at(by), core))

    def att_pass(by, z, side):
        ref = att_all.at[chip_at(chips - by) * 2 + side, z]
        where = chips + by
        return remote(ref, ref, a_send.at[where, z], a_recv.at[where, z], partner)

    for ahead in range(n):
        z = lax.rem(me + ahead, n)
        if ahead:
            att_line(z, z).wait_recv()
        for by in range(1, chips):
            att_chip(by, z, chip).start()
        att_pass(0, z, core).start()

    @pl.when(is_helper)
    def _():
        for r in (2, 3):
            wo_forward(1, r, cuts - 1)

    for ahead in range(n):
        z = lax.rem(me + ahead, n)
        for by in range(1, chips):
            att_chip(by, z, chip_at(chips - by)).wait_recv()
            att_pass(by, z, core).start()

    for z in range(n):
        for by in range(chips):
            att_pass(by, z, 1 - core).wait_recv()

    def out_copy(which, side, source, cut):
        return remote(
            out_part.at[which * 2 + side, cut],
            out_in.at[source, cut],
            o_send.at[which * 2 + side, cut],
            o_recv.at[source, cut],
            place(which, side),
        )

    others = [(by, side) for by in range(1, chips) for side in range(2)] + [(0, 1)]
    heads_wide = wo_ref.shape[2]
    for cut in range(cuts):

        @pl.when(is_end)
        def _():
            for r in (1, 2, 3):
                wo_copy(0, r, cut).wait_recv()

        total = None
        for z in range(n):
            lhs = att_all[:, z].reshape(seats * rows, heads_wide)
            made = jnp.dot(lhs, wo_ref[z, cut], preferred_element_type=jnp.float32)
            total = made if total is None else total + made
        out_part[:, cut] = total.astype(out_part.dtype).reshape(seats, rows, cut_cols)
        for by, side in others:
            lane = core if side == 0 else 1 - core
            out_copy(chip_at(by), lane, seat, cut).start()

    def finish(ref, source, cut):
        span = pl.ds(pl.multiple_of(source * cols_out + cut * cut_cols, 128), cut_cols)
        gate = table_ref[2, pl.ds(level, 1), span]
        out_ref[0, :, span] = (ref[source, cut].astype(jnp.float32) * gate).astype(out_ref.dtype)

    for cut in range(cuts):
        finish(out_part, seat, cut)
        for by, side in others:
            lane = core if side == 0 else 1 - core
            source = chip_at(chips - by) * 2 + lane
            out_copy(chip, core, source, cut).wait_recv()
            finish(out_in, source, cut)

    for cut in range(cuts):
        for by, side in others:
            lane = core if side == 0 else 1 - core
            out_copy(chip_at(by), lane, seat, cut).wait_send()
    for z in range(n):
        for by in range(1, chips):
            att_chip(by, z, chip).wait_send()
        for by in range(chips):
            att_pass(by, z, core).wait_send()
    for ahead in range(1, n):
        att_line(lax.rem(me + ahead, n), me).wait_send()

    @pl.loop(0, n)
    def _(block):
        for ahead in range(1, tracts):

            @pl.when(tract + ahead < tracts)
            def _():
                kv_copy(ahead, block).wait_send()

    @pl.when(is_end)
    def _():
        for kind in range(3):
            far_first(kind).wait_send()

        @pl.loop(0, pieces)
        def _(p):
            tok(0, 0, p).wait_send()

        for cut in range(cuts):
            wo_copy(0, 0, cut).wait_send()

    @pl.when(is_helper)
    def _():
        for kind in range(3):
            for by in range(1, chips):
                far_out(by, kind).wait_send()
            for by in range(chips):
                far_pass(by, kind, core).wait_send()
            for r in (1, 2, 3):
                part_copy(r, kind).wait_send()

        @pl.loop(0, pieces)
        def _(p):
            for r in (0, 1):
                tok(0, r, p).wait_send()

        @pl.loop(0, near)
        def _(p):
            for r in (1, 2, 3):
                tok(1, r, p).wait_send()

        for cut in range(cuts):
            for r in (0, 1):
                wo_copy(0, r, cut).wait_send()
            for r in (1, 2, 3):
                wo_copy(1, r, cut).wait_send()


PIECES = 8
NEAR = 4


def fits_line(n, tracts, reps, frames, w_out):
    rows, width = frames.shape[1:]
    seats = tracts * reps
    far = (PIECES - NEAR) * (width // PIECES)
    return (
        n == 4
        and tracts % 2 == 0
        and seats > 2
        and rows % 16 == 0
        and width % (PIECES * 128) == 0
        and width % (seats * 256) == 0
        and far % (seats * 16) == 0
        and w_out.shape[0] % 32 == 0
    )


def line_body(frames, levels, visible, w_qkv, w_out, modulation):
    n, tracts = lax.axis_size("head"), lax.axis_size("tract")
    reps = lax.axis_size("rep")
    rows, width = frames.shape[1:]
    cols = w_qkv.shape[2]
    heads_here = cols // HD
    seats = tracts * reps
    chips = seats // 2
    deep = width // PIECES
    cuts = width // seats // 256
    vmem = pl.BlockSpec(memory_space=pltpu.VMEM)
    hbm = pl.BlockSpec(memory_space=pltpu.HBM)
    smem = pl.BlockSpec(memory_space=pltpu.SMEM)
    half = jnp.bfloat16
    dma = pltpu.SemaphoreType.DMA
    return pl.pallas_call(
        functools.partial(line_kernel, n, tracts, reps, PIECES, NEAR),
        out_shape=pltpu.VMEM(frames.shape, frames.dtype),
        in_specs=[hbm, smem, smem, hbm, hbm, hbm],
        out_specs=vmem,
        scratch_shapes=[
            pltpu.VMEM((3, *modulation.shape[::2]), jnp.float32),
            pltpu.VMEM((rows, width), half),
            pltpu.VMEM((n, PIECES, rows, deep), half),
            pltpu.VMEM((3, width, cols), half),
            pltpu.VMEM((3, (PIECES - NEAR) * deep, cols), half),
            pltpu.VMEM((n, cuts, w_out.shape[0], 256), half),
            pltpu.VMEM((n, 3, rows, cols), jnp.float32),
            pltpu.VMEM((n, rows, cols), half),
            pltpu.VMEM((n, 2, rows, cols), half),
            pltpu.VMEM((max(1, tracts - 1), n, 2, rows, cols), half),
            pltpu.VMEM((n, 3, rows, cols), half),
            pltpu.VMEM((n, 3, rows, cols), half),
            pltpu.VMEM((n, rows, cols), half),
            pltpu.VMEM((heads_here, n * rows, 1), jnp.float32),
            pltpu.VMEM((heads_here, n * rows, 1), jnp.float32),
            pltpu.VMEM((heads_here, n * rows, HD), jnp.float32),
            pltpu.VMEM((seats, n, rows, cols), half),
            pltpu.VMEM((seats, cuts, rows, 256), half),
            pltpu.VMEM((seats, cuts, rows, 256), half),
            dma((2,)),
            dma((PIECES,)),
            dma((cuts,)),
            dma((2, n, PIECES)),
            dma((n, PIECES)),
            dma((2 * chips, 3)),
            dma((2 * chips, 3)),
            dma((n, 3)),
            dma((n, 3)),
            dma((tracts, n)),
            dma((tracts, n)),
            dma((2, n, cuts)),
            dma((n, cuts)),
            dma((n,)),
            dma((n,)),
            dma((2 * chips, n)),
            dma((2 * chips, n)),
            dma((seats, cuts)),
            dma((seats, cuts)),
        ],
        compiler_params=pltpu.CompilerParams(
            collective_id=0, has_side_effects=True, vmem_limit_bytes=GRANT
        ),
    )(
        frames,
        levels,
        visible,
        jnp.transpose(w_qkv, (1, 0, 2)),
        w_out,
        jnp.transpose(modulation, (1, 0, 2)),
    )


def body(frames, levels, visible, w_qkv, w_out, modulation):
    n, tracts = lax.axis_size("head"), lax.axis_size("tract")
    reps = lax.axis_size("rep")
    line = fits_line(n, tracts, reps, frames, w_out)
    chosen = line_body if line else ring_body
    return chosen(frames, levels, visible, w_qkv, w_out, modulation)


def solution(mesh):
    placed = (
        P(("rep", "tract"), "head", None),
        P(("rep", "tract")),
        P(("rep", "tract"), None),
        P(None, None, "head"),
        P("head", None),
        P(),
    )
    return jax.shard_map(
        body,
        mesh=mesh,
        in_specs=placed,
        out_specs=P(("rep", "tract"), "head", None),
        check_vma=False,
    )
```

```python
import functools

import jax
import jax.numpy as jnp
from jax import lax
from jax.experimental import pallas as pl
from jax.experimental.pallas import tpu as pltpu
from jax.sharding import PartitionSpec as P

HD = 128
GRANT = 60 * 1024 * 1024
MESH = pl.DeviceIdType.MESH


def meet(n, me, tracts, tract, others):
    barrier = pltpu.get_barrier_semaphore()
    for other in (lax.rem(me + 1, n), lax.rem(me + n - 1, n)):
        pl.semaphore_signal(barrier, inc=1, device_id={"head": other}, device_id_type=MESH)
    for ahead in range(1, tracts):
        other = lax.rem(tract + ahead, tracts)
        pl.semaphore_signal(barrier, inc=1, device_id={"tract": other}, device_id_type=MESH)
    for other in others:
        pl.semaphore_signal(barrier, inc=1, device_id=other, device_id_type=MESH)
    pl.semaphore_wait(barrier, 1 + tracts + len(others))


def sublayer_kernel(
    n,
    tracts,
    reps,
    pieces,
    halves,
    x_ref,
    level_ref,
    visible_ref,
    w_hbm,
    out_hbm,
    table_ref,
    out_ref,
    got,
    wq_ref,
    w_ref,
    q_ref,
    kv_ref,
    kv_in,
    att_ref,
    peak_ref,
    sum_ref,
    acc_ref,
    going,
    landed,
    total_ref,
    load_sem,
    g_send,
    g_recv,
    kv_send,
    kv_recv,
    s_send,
    s_recv,
    w_far,
    att_far,
    f_send,
    f_recv,
):
    me, tract = lax.axis_index("head"), lax.axis_index("tract")
    own = pltpu.make_async_copy(x_ref.at[0], got.at[me], load_sem.at[0])
    own.start()
    load = pltpu.make_async_copy(w_hbm, wq_ref, load_sem.at[1])
    load.start()
    load_out = pltpu.make_async_copy(out_hbm, w_ref, load_sem.at[2])
    load_out.start()
    core, wide = tract % 2, tracts // 2
    chips = wide * reps
    chip = lax.axis_index("rep") * wide + tract // 2
    slab = w_ref.shape[0] // (2 * chips)
    helper = (me == 1) | (me == n - 2)
    ends = (me == 0) | (me == n - 1)

    def seat(by):
        other = lax.rem(chip + by, chips)
        return {"rep": other // wide, "tract": lax.rem(other, wide) * 2 + core}

    def slab_of(which, side):
        start = pl.multiple_of((which * 2 + side) * slab, slab)
        return pl.ds(start, slab)

    def far_copy(kind, span, target, source=None):
        return pltpu.make_async_remote_copy(
            src_ref=(w_far if source is None else source).at[span],
            dst_ref=w_far.at[span],
            send_sem=f_send.at[kind],
            recv_sem=f_recv.at[kind],
            device_id=target,
            device_id_type=MESH,
        )

    inward = {"head": jnp.where(me == 0, 1, n - 2)}
    partner = {"tract": tract + 1 - 2 * core}
    mine = slab_of(chip, core)

    def to_helper():
        return far_copy(0, mine, inward, out_hbm)

    def to_chip(by):
        return far_copy(by, mine, seat(by))

    def from_chip(by):
        return far_copy(by, slab_of(lax.rem(chip + chips - by, chips), core), seat(by))

    def to_partner(by):
        span = slab_of(lax.rem(chip + chips - by, chips), core)
        return far_copy(chips + by, span, partner)

    def from_partner(by):
        span = slab_of(lax.rem(chip + chips - by, chips), 1 - core)
        return far_copy(chips + by, span, partner)

    def att_copy():
        return pltpu.make_async_remote_copy(
            src_ref=att_ref,
            dst_ref=att_far,
            send_sem=f_send.at[2 * chips],
            recv_sem=f_recv.at[2 * chips],
            device_id=inward,
            device_id_type=MESH,
        )

    meet(n, me, tracts, tract, [seat(by) for by in range(1, chips)])
    level = level_ref[0]

    def style(kind):
        return table_ref[kind, pl.ds(level, 1), :]

    rows, width = x_ref.shape[1:]
    part = rows // pieces

    def copy(way, step, piece, first=False):
        side = (way + 1) // 2
        span = pl.ds(piece * part, part)
        block = me - way * step
        return pltpu.make_async_remote_copy(
            src_ref=(x_ref.at[0] if first else got.at[block]).at[span],
            dst_ref=got.at[block].at[span],
            send_sem=g_send.at[side, step, piece],
            recv_sem=g_recv.at[side, step, piece],
            device_id={"head": me + way},
            device_id_type=MESH,
        )

    def arrival(way, step, piece):
        side = (way + 1) // 2
        span = pl.ds(piece * part, part)
        return pltpu.make_async_remote_copy(
            src_ref=x_ref.at[0].at[span],
            dst_ref=got.at[me - way * (step + 1)].at[span],
            send_sem=g_send.at[side, step, piece],
            recv_sem=g_recv.at[side, step, piece],
            device_id={"head": me - way},
            device_id_type=MESH,
        )

    def sends(way, step):
        block, target = me - way * step, me + way
        return (block >= 0) & (block < n) & (target >= 0) & (target < n) & (step < n - 1)

    def receives(way, step):
        block = me - way * (step + 1)
        return (block >= 0) & (block < n)

    def kv_copy(ahead, block):
        return pltpu.make_async_remote_copy(
            src_ref=kv_ref.at[block],
            dst_ref=kv_in.at[ahead - 1, block],
            send_sem=kv_send.at[ahead - 1, block],
            recv_sem=kv_recv.at[ahead - 1, block],
            device_id={"tract": tract + ahead},
            device_id_type=MESH,
        )

    def project(block):
        tokens = got[block].astype(jnp.float32)
        power = jnp.mean(tokens * tokens, axis=-1, keepdims=True)
        normed = tokens * lax.rsqrt(power + 1e-06)
        shaped = (normed * (1.0 + style(1)) + style(0)).astype(jnp.bfloat16)
        for kind in (1, 2, 0):
            made = jnp.dot(shaped, wq_ref[kind], preferred_element_type=jnp.float32)
            made = made.astype(jnp.bfloat16)
            if kind == 0:
                q_ref[block] = made
            else:
                kv_ref[block, kind - 1] = made
            if kind == 2:
                for ahead in range(1, tracts):

                    @pl.when(tract + ahead < tracts)
                    def _():
                        kv_copy(ahead, block).start()

    for piece in range(pieces):
        for way in (-1, 1):

            @pl.when(sends(way, 0))
            def _():
                copy(way, 0, piece, True).start()

    @pl.when(ends)
    def _():
        to_helper().start()

    own.wait()
    load.wait()
    project(me)

    @pl.loop(0, n - 1)
    def _(step):
        for piece in range(pieces):
            for way in (-1, 1):

                @pl.when(receives(way, step))
                def _():
                    arrival(way, step, piece).wait_recv()

                @pl.when(sends(way, step + 1))
                def _():
                    copy(way, step + 1, piece).start()

        @pl.loop(0, 2)
        def _(side):
            way = 2 * side - 1

            @pl.when(receives(way, step))
            def _():
                project(me - way * (step + 1))

        @pl.when(helper & (step == 0))
        def _():
            to_helper().wait_recv()
            for by in range(1, chips):
                to_chip(by).start()
            to_partner(0).start()

    @pl.when(helper)
    def _():
        for by in range(1, chips):
            from_chip(by).wait_recv()
            to_partner(by).start()

    tokens_here = n * rows
    heads_here = q_ref.shape[2] // HD
    scale = HD ** (-0.5)

    def attend(source, allowed):
        for head in range(heads_here):
            lanes = slice(head * HD, (head + 1) * HD)
            queries = q_ref[:, :, lanes].reshape(tokens_here, HD)
            keys = source[:, 0, :, lanes].reshape(tokens_here, HD)
            values = source[:, 1, :, lanes].reshape(tokens_here, HD)
            scores = (
                lax.dot_general(
                    queries, keys, (((1,), (1,)), ((), ())), preferred_element_type=jnp.float32
                )
                * scale
            )
            if allowed is None:
                peak = jnp.max(scores, axis=1, keepdims=True)
                probs = jnp.exp(scores - peak)
            else:
                scores = jnp.where(allowed, scores, -1e30)
                old = peak_ref[head]
                peak = jnp.maximum(old, jnp.max(scores, axis=1, keepdims=True))
                probs = jnp.where(allowed, jnp.exp(scores - peak), 0.0)
                rescale = jnp.exp(old - peak)
            row_sum = jnp.sum(probs, axis=1, keepdims=True)
            weighted = jnp.dot(
                probs.astype(jnp.bfloat16), values, preferred_element_type=jnp.float32
            )
            if allowed is not None:
                row_sum += sum_ref[head] * rescale
                weighted += acc_ref[head] * rescale
            peak_ref[head] = peak
            sum_ref[head] = row_sum
            acc_ref[head] = weighted

    attend(kv_ref, None)
    for ahead in range(1, tracts):

        @pl.when(tract >= ahead)
        def _():
            @pl.loop(0, n)
            def _(block):
                kv_copy(ahead, block).wait_recv()

            attend(kv_in.at[ahead - 1], visible_ref[0, lax.max(tract - ahead, 0)] > 0)

    for head in range(heads_here):
        attended = (acc_ref[head] / sum_ref[head]).astype(jnp.bfloat16)
        att_ref[:, :, head * HD : (head + 1) * HD] = attended.reshape(n, rows, HD)

    @pl.when(ends)
    def _():
        att_copy().start()

    load_out.wait()

    @pl.when(helper)
    def _():
        for by in range(chips):
            from_partner(by).wait_recv()
        att_copy().wait_recv()

    cols = width // halves

    def sum_copy(way, step, piece):
        side = (way + 1) // 2
        span = pl.ds(piece * cols, cols)
        return pltpu.make_async_remote_copy(
            src_ref=going.at[side, step].at[:, span],
            dst_ref=landed.at[side, step].at[:, span],
            send_sem=s_send.at[side, step, piece],
            recv_sem=s_recv.at[side, step, piece],
            device_id={"head": me + way},
            device_id_type=MESH,
        )

    def product(block, piece):
        return jnp.dot(
            att_ref[block],
            w_ref[:, piece * cols : (piece + 1) * cols],
            preferred_element_type=jnp.float32,
        )

    def far_product(block, piece):
        return jnp.dot(
            att_far[block],
            w_far[:, piece * cols : (piece + 1) * cols],
            preferred_element_type=jnp.float32,
        )

    def helps(way):
        return me == (1 if way == 1 else n - 2)

    def owner(way, step):
        return (n - 1 - step) if way == 1 else step

    def sum_sends(way, step):
        block = owner(way, step)
        return (block > me) & (me > 0) if way == 1 else (block < me) & (me < n - 1)

    def sum_receives(way, step):
        block = owner(way, step)
        return (block >= me) & (me > 1) if way == 1 else (block <= me) & (me < n - 2)

    @pl.loop(0, n - 1)
    def _(tick):
        for piece in range(halves):
            span = slice(piece * cols, (piece + 1) * cols)
            for way in (-1, 1):
                side = (way + 1) // 2
                step = tick - (me if way == 1 else n - 1 - me)
                held = (step >= 0) & (step < n - 1)

                @pl.when(held & sum_sends(way, step))
                def _():
                    going[side, step, :, span] = product(owner(way, step), piece).astype(
                        going.dtype
                    )

                    @pl.when(helps(way))
                    def _():
                        going[side, step, :, span] = (
                            going[side, step, :, span].astype(jnp.float32)
                            + far_product(owner(way, step), piece)
                        ).astype(going.dtype)

                    @pl.when(sum_receives(way, step))
                    def _():
                        sum_copy(way, step, piece).wait_recv()
                        going[side, step, :, span] = (
                            going[side, step, :, span].astype(jnp.float32)
                            + landed[side, step, :, span].astype(jnp.float32)
                        ).astype(going.dtype)

                    sum_copy(way, step, piece).start()

    for piece in range(halves):
        span = slice(piece * cols, (piece + 1) * cols)
        total_ref[:, span] = product(me, piece).astype(going.dtype).astype(jnp.float32)
    for piece in range(halves):
        span = slice(piece * cols, (piece + 1) * cols)
        for way in (-1, 1):
            side = (way + 1) // 2
            last = n - 1 - me if way == 1 else me

            @pl.when(helps(way))
            def _():
                total_ref[:, span] += far_product(me, piece)

            @pl.when(me > 1 if way == 1 else me < n - 2)
            def _():
                sum_copy(way, last, piece).wait_recv()
                total_ref[:, span] += landed[side, last, :, span].astype(jnp.float32)

        out_ref[0, :, span] = (
            total_ref[:, span] * table_ref[2, pl.ds(level, 1), span]
        ).astype(out_ref.dtype)

    @pl.loop(0, n - 1)
    def _(step):
        for piece in range(halves):
            for way in (-1, 1):

                @pl.when(sum_sends(way, step))
                def _():
                    sum_copy(way, step, piece).wait_send()

    @pl.loop(0, n)
    def _(block):
        for ahead in range(1, tracts):

            @pl.when(tract + ahead < tracts)
            def _():
                kv_copy(ahead, block).wait_send()

    @pl.loop(0, n - 1)
    def _(step):
        for piece in range(pieces):
            for way in (-1, 1):

                @pl.when(sends(way, step))
                def _():
                    copy(way, step, piece).wait_send()

    @pl.when(ends)
    def _():
        to_helper().wait_send()
        att_copy().wait_send()

    @pl.when(helper)
    def _():
        for by in range(1, chips):
            to_chip(by).wait_send()
        for by in range(chips):
            to_partner(by).wait_send()


def ring_body(frames, levels, visible, w_qkv, w_out, modulation):
    n, tracts = lax.axis_size("head"), lax.axis_size("tract")
    reps = lax.axis_size("rep")
    rows, width = frames.shape[1:]
    cols = w_qkv.shape[2]
    heads_here = cols // HD
    pieces = max(1, rows // 32)
    halves = 4 if width % 512 == 0 else 2
    vmem = pl.BlockSpec(memory_space=pltpu.VMEM)
    hbm = pl.BlockSpec(memory_space=pltpu.HBM)
    smem = pl.BlockSpec(memory_space=pltpu.SMEM)
    half = jnp.bfloat16
    dma = pltpu.SemaphoreType.DMA
    return pl.pallas_call(
        functools.partial(sublayer_kernel, n, tracts, reps, pieces, halves),
        out_shape=jax.ShapeDtypeStruct(frames.shape, frames.dtype),
        in_specs=[hbm, smem, smem, hbm, hbm, vmem],
        out_specs=vmem,
        scratch_shapes=[
            pltpu.VMEM((n, rows, width), half),
            pltpu.VMEM((3, width, cols), half),
            pltpu.VMEM(w_out.shape, half),
            pltpu.VMEM((n, rows, cols), half),
            pltpu.VMEM((n, 2, rows, cols), half),
            pltpu.VMEM((max(1, tracts - 1), n, 2, rows, cols), half),
            pltpu.VMEM((n, rows, cols), half),
            pltpu.VMEM((heads_here, n * rows, 1), jnp.float32),
            pltpu.VMEM((heads_here, n * rows, 1), jnp.float32),
            pltpu.VMEM((heads_here, n * rows, HD), jnp.float32),
            pltpu.VMEM((2, n - 1, rows, width), half),
            pltpu.VMEM((2, n - 1, rows, width), half),
            pltpu.VMEM((rows, width), jnp.float32),
            dma((3,)),
            dma((2, n, pieces)),
            dma((2, n, pieces)),
            dma((tracts, n)),
            dma((tracts, n)),
            dma((2, n, halves)),
            dma((2, n, halves)),
            pltpu.VMEM(w_out.shape, half),
            pltpu.VMEM((n, rows, cols), half),
            dma((tracts * reps + 1,)),
            dma((tracts * reps + 1,)),
        ],
        compiler_params=pltpu.CompilerParams(
            collective_id=0, has_side_effects=True, vmem_limit_bytes=GRANT
        ),
    )(
        frames,
        levels,
        visible,
        jnp.transpose(w_qkv, (1, 0, 2)),
        w_out,
        jnp.transpose(modulation, (1, 0, 2)),
    )


def line_kernel(
    n,
    tracts,
    reps,
    pieces,
    near,
    x_ref,
    level_ref,
    visible_ref,
    w_hbm,
    out_hbm,
    table_hbm,
    out_ref,
    table_ref,
    raw,
    got,
    wq_ref,
    w_far,
    wo_ref,
    acc_ref,
    q_ref,
    kv_ref,
    kv_in,
    part_ref,
    part_in,
    att_ref,
    peak_ref,
    sum_ref,
    mix_ref,
    att_all,
    out_part,
    out_in,
    load_sem,
    wq_sem,
    wo_sem,
    g_send,
    g_recv,
    f_send,
    f_recv,
    p_send,
    p_recv,
    kv_send,
    kv_recv,
    wo_send,
    wo_recv,
    z_send,
    z_recv,
    a_send,
    a_recv,
    b_recv,
    o_send,
    o_recv,
):
    me, tract, rep = lax.axis_index("head"), lax.axis_index("tract"), lax.axis_index("rep")
    rows, width = x_ref.shape[1:]
    deep = width // pieces
    low = me < 2
    sign = jnp.where(low, 1, -1)
    base = jnp.where(low, 0, n - 1)
    is_end = (me == 0) | (me == n - 1)
    is_helper = (me == 1) | (me == n - 2)
    inner, outer = {"head": me + sign}, {"head": me - sign}

    def blk(r):
        return base + sign * r

    core, wide = tract % 2, tracts // 2
    chips = wide * reps
    seats = chips * 2
    chip = rep * wide + tract // 2
    seat = chip * 2 + core
    partner = {"tract": tract + 1 - 2 * core}

    def chip_at(by):
        return lax.rem(chip + by, chips)

    def place(which, side):
        return {"rep": which // wide, "tract": lax.rem(which, wide) * 2 + side}

    own_load = pltpu.make_async_copy(x_ref.at[0], raw, load_sem.at[0])
    own_load.start()
    table_load = pltpu.make_async_copy(table_hbm, table_ref, load_sem.at[1])
    table_load.start()
    cols_out = width // seats
    cuts = wo_ref.shape[1]
    cut_cols = cols_out // cuts

    def wo_load(cut):
        start = pl.multiple_of(seat * cols_out + cut * cut_cols, 128)
        src = out_hbm.at[:, pl.ds(start, cut_cols)]
        return pltpu.make_async_copy(src, wo_ref.at[me, cut], wo_sem.at[cut])


    def wq_load(p):
        span = pl.ds(pl.multiple_of(p * deep, deep), deep)
        return pltpu.make_async_copy(w_hbm.at[:, span], wq_ref.at[:, span], wq_sem.at[p])

    @pl.loop(0, pieces)
    def _(p):
        wq_load(p).start()

    for cut in range(cuts):
        wo_load(cut).start()

    barrier = pltpu.get_barrier_semaphore()
    for ahead in range(1, n):
        other = lax.rem(me + ahead, n)
        pl.semaphore_signal(barrier, inc=1, device_id={"head": other}, device_id_type=MESH)
    for by in range(chips):
        for side in range(2):
            if by == 0 and side == 1:
                continue
            target = partner if by == 0 else place(chip_at(by), side)
            pl.semaphore_signal(barrier, inc=1, device_id=target, device_id_type=MESH)

    level = level_ref[0]

    def style(kind, start):
        return table_ref[kind, pl.ds(level, 1), start : start + deep]

    def remote(src, dst, send, recv, target):
        return pltpu.make_async_remote_copy(
            src_ref=src,
            dst_ref=dst,
            send_sem=send,
            recv_sem=recv,
            device_id=target,
            device_id_type=MESH,
        )

    def tok(way, r, p):
        b = blk(r)
        ref = got.at[b, p]
        target = inner if way == 0 else outer
        return remote(ref, ref, g_send.at[way, b], g_recv.at[b, p], target)

    def tok_sent(way, r, count):
        b = blk(r)
        ref = got.at[b, pl.ds(0, count)]
        target = inner if way == 0 else outer
        remote(ref, ref, g_send.at[way, b], g_recv.at[b, 0], target).wait_send()

    far_rows = w_far.shape[1] // seats
    far_base = near * deep

    def far_span(which, side):
        start = (which * 2 + side) * far_rows
        return pl.ds(pl.multiple_of(start, far_rows), far_rows)

    def far_first(kind):
        start = far_base + seat * far_rows
        src = w_hbm.at[kind, pl.ds(pl.multiple_of(start, far_rows), far_rows)]
        dst = w_far.at[kind, far_span(chip, core)]
        return remote(src, dst, f_send.at[0], f_recv.at[0, kind], inner)

    across = [
        chip,
        rep * wide + 1 - lax.rem(chip, wide),
        (1 - rep) * wide + lax.rem(chip, wide),
        (1 - rep) * wide + 1 - lax.rem(chip, wide),
    ]
    along_x, along_y = place(across[1], core), place(across[2], core)

    def far_move(slot, kind, which):
        ref = w_far.at[kind, far_span(which, core)]
        target = along_x if slot == 1 else along_y
        return remote(ref, ref, f_send.at[slot], f_recv.at[slot, kind], target)

    def far_pass(slot, kind, side):
        ref = w_far.at[kind, far_span(across[slot], side)]
        where = chips + slot
        return remote(ref, ref, f_send.at[where], f_recv.at[where, kind], partner)

    def far_relay(kind):
        far_first(kind).wait_recv()
        far_move(1, kind, chip).start()
        far_move(2, kind, chip).start()
        far_pass(0, kind, core).start()

    def far_hand_x(kind):
        far_move(1, kind, across[1]).wait_recv()
        far_move(3, kind, across[1]).start()
        far_pass(1, kind, core).start()

    def far_hand_y(kind):
        for slot in (2, 3):
            far_move(slot, kind, across[slot]).wait_recv()
            far_pass(slot, kind, core).start()

    def far_ready(kind):
        for slot in range(chips):
            far_pass(slot, kind, 1 - core).wait_recv()

    def part_copy(r, kind):
        b = blk(r)
        return remote(
            part_ref.at[b, kind],
            part_in.at[b, kind],
            p_send.at[b],
            p_recv.at[b, kind],
            outer,
        )

    def far_part(rs, kinds):
        for kind in kinds:
            total = None
            for p in range(near, pieces):
                lhs = jnp.concatenate([got[blk(r), p] for r in rs], axis=0)
                span = slice((p - near) * deep, (p - near + 1) * deep)
                made = jnp.dot(lhs, w_far[kind, span], preferred_element_type=jnp.float32)
                total = made if total is None else total + made
            total = total.astype(part_ref.dtype)
            for i, r in enumerate(rs):
                part_ref[blk(r), kind] = total[i * rows : (i + 1) * rows]
        for r in rs:
            for kind in kinds:
                part_copy(r, kind).start()

    def wo_copy(way, r, cut):
        b = blk(r)
        ref = wo_ref.at[b, cut]
        target = inner if way == 0 else outer
        return remote(ref, ref, wo_send.at[way, b], wo_recv.at[b, cut], target)

    def wo_start(way, r, which):
        for cut in which:
            wo_copy(way, r, cut).start()

    along = [(0, r, cut) for cut in range(cuts) for r in (1, 0)]
    back = [(1, r, cut) for cut in range(cuts) for r in (2, 3)]
    early = 2

    def wo_next(way, r, cut):
        if r == 1:
            wo_start(way, r, (cut,))
        else:
            wo_forward(way, r, cut)

    def wo_forward(way, r, cut):
        wo_copy(way, r, cut).wait_recv()
        wo_copy(way, r, cut).start()

    def kv_near(b):
        ref, slot = kv_ref.at[b], kv_in.at[0, b]
        return remote(ref, slot, kv_send.at[0], kv_recv.at[0], partner)

    def kv_far(b):
        ref, slot = kv_ref.at[b], kv_in.at[1, b]
        return remote(ref, slot, kv_send.at[1], kv_recv.at[1], along_x)

    def kv_relay():
        slot = 2 * (1 - core)
        return remote(kv_in.at[1], kv_in.at[slot], kv_send.at[2], kv_recv.at[slot], partner)

    def kv_slot(slot):
        return remote(kv_ref, kv_in.at[slot], kv_send.at[slot], kv_recv.at[slot], partner)

    def accumulate(rs, p):
        lhs = jnp.concatenate([got[blk(r), p] for r in rs], axis=0)
        span = pl.ds(pl.multiple_of(p * deep, deep), deep)
        for kind in range(3):
            made = jnp.dot(lhs, wq_ref[kind, span], preferred_element_type=jnp.float32)
            for i, r in enumerate(rs):
                acc_ref[blk(r), kind] += made[i * rows : (i + 1) * rows]

    def settle(r, kinds, extra=False):
        b = blk(r)
        for kind in kinds:
            made = acc_ref[b, kind]
            if extra:
                made = made + part_in[b, kind].astype(jnp.float32)
            made = made.astype(q_ref.dtype)
            if kind == 0:
                q_ref[b] = made
            else:
                kv_ref[b, kind - 1] = made

    def share(r):
        @pl.when(tract < 2)
        def _():
            kv_far(blk(r)).start()

        @pl.when(core == 0)
        def _():
            kv_near(blk(r)).start()

    acc_ref[...] = jnp.zeros_like(acc_ref)
    own_load.wait()
    power = jnp.zeros((rows, 1), jnp.float32)
    for p in range(pieces):
        tokens = raw[:, p * deep : (p + 1) * deep].astype(jnp.float32)
        power += jnp.sum(tokens * tokens, axis=-1, keepdims=True)
    table_load.wait()
    factor = lax.rsqrt(power * (1.0 / width) + 1e-06)
    pl.semaphore_wait(barrier, n - 1 + seats - 1)

    @pl.when(is_end)
    def _():
        for kind in (1, 2, 0):
            far_first(kind).start()

    def send_own(p):
        @pl.when(is_end)
        def _():
            tok(0, 0, p).start()

        @pl.when(is_helper)
        def _():
            tok(0, 1, p).start()
            if p < near:
                tok(1, 1, p).start()

    for p in range(pieces):
        tokens = raw[:, p * deep : (p + 1) * deep].astype(jnp.float32)
        shaped = tokens * factor * (1.0 + style(1, p * deep)) + style(0, p * deep)
        got[me, p] = shaped.astype(got.dtype)
        if p:
            send_own(p - 1)
    send_own(pieces - 1)

    @pl.when(is_end)
    def _():
        @pl.loop(0, pieces)
        def _(p):
            wq_load(p).wait()
            accumulate((0,), p)

        for cut in range(cuts):
            wo_load(cut).wait()
        wo_start(0, 0, range(cuts))

        settle(0, (1, 2, 0))
        share(0)
        for r in (1, 2):

            @pl.loop(0, near)
            def _(p):
                tok(0, r, p).wait_recv()
                accumulate((r,), p)

        for r in (1, 2):
            for kind in (1, 2):
                part_copy(r, kind).wait_recv()
            settle(r, (1, 2), True)
            share(r)

        @pl.loop(0, near)
        def _(p):
            tok(0, 3, p).wait_recv()
            accumulate((3,), p)

        for kind in (1, 2):
            part_copy(3, kind).wait_recv()
        settle(3, (1, 2), True)
        share(3)
        for r in (1, 2, 3):
            part_copy(r, 0).wait_recv()
            settle(r, (0,), True)

    @pl.when(is_helper)
    def _():
        def pass_on(p):
            tok(0, 0, p).wait_recv()
            tok(0, 0, p).start()

        @pl.loop(0, pieces)
        def _(p):
            wq_load(p).wait()
            tok(1, 2, p).wait_recv()

            @pl.when(p < near)
            def _():
                tok(1, 2, p).start()

            accumulate((1, 2), p)
            for at, kind in ((1, 1), (3, 2), (5, 0)):

                @pl.when(p == at)
                def _():
                    far_relay(kind)

            for at, kind in ((4, 1), (6, 2)):

                @pl.when(p == at)
                def _():
                    far_hand_x(kind)

            @pl.when(p >= pieces - 2)
            def _():
                pass_on(p - (pieces - 2))

        settle(1, (1, 2, 0))
        share(1)
        settle(2, (1, 2, 0))
        share(2)
        for cut in range(cuts):
            wo_load(cut).wait()
        wo_start(1, 1, range(cuts - 1))

        @pl.loop(0, pieces)
        def _(p):
            @pl.when(p + 2 < pieces)
            def _():
                pass_on(p + 2)

            tok(1, 3, p).wait_recv()

            @pl.when(p < near)
            def _():
                tok(1, 3, p).start()

            accumulate((0, 3), p)

            @pl.when(p == 0)
            def _():
                far_hand_x(0)

            @pl.when(p == 1)
            def _():
                far_hand_y(1)
                far_ready(1)
                far_part((1, 2), (1,))

            @pl.when(p == 3)
            def _():
                far_hand_y(2)

            @pl.when(p == 4)
            def _():
                far_ready(2)
                far_part((1, 2), (2,))

            @pl.when(p == 6)
            def _():
                far_hand_y(0)

        far_part((3,), (1, 2))
        settle(0, (1, 2, 0))
        share(0)
        settle(3, (1, 2, 0))
        share(3)
        far_ready(0)
        far_part((1, 2, 3), (0,))
        wo_start(1, 1, (cuts - 1,))
        for way, r, cut in along[:early]:
            wo_next(way, r, cut)

    tokens_here = n * rows
    heads_here = q_ref.shape[2] // HD
    scale = HD ** (-0.5)

    def attend(source, bias):
        for head in range(heads_here):
            lanes = slice(head * HD, (head + 1) * HD)
            queries = q_ref[:, :, lanes].reshape(tokens_here, HD)
            keys = source[:, 0, :, lanes].reshape(tokens_here, HD)
            values = source[:, 1, :, lanes].reshape(tokens_here, HD)
            scores = (
                lax.dot_general(
                    keys, queries, (((1,), (1,)), ((), ())), preferred_element_type=jnp.float32
                )
                * scale
            )
            if bias is not None:
                scores = scores + bias
            peak = jnp.max(scores, axis=0, keepdims=True)
            if bias is not None:
                old = peak_ref[head]
                peak = jnp.maximum(old, peak)
            probs = jnp.exp(scores - peak)
            row_sum = jnp.sum(probs, axis=0, keepdims=True)
            weighted = lax.dot_general(
                values,
                probs.astype(jnp.bfloat16),
                (((0,), (0,)), ((), ())),
                preferred_element_type=jnp.float32,
            )
            if bias is not None:
                rescale = jnp.exp(old - peak)
                row_sum += sum_ref[head] * rescale
                weighted += mix_ref[head] * rescale
            peak_ref[head] = peak
            sum_ref[head] = row_sum
            mix_ref[head] = weighted

    attend(kv_ref, None)

    @pl.when(tract >= 2)
    def _():
        kv_slot(1).wait_recv()
        kv_relay().start()

    for ahead in (2, 1, 3):

        @pl.when(tract >= ahead)
        def _():
            if ahead != 2:
                kv_slot(ahead - 1).wait_recv()
            seen = visible_ref[0, lax.max(tract - ahead, 0)] > 0
            attend(kv_in.at[ahead - 1], jnp.where(seen, 0.0, -1e30))

    for head in range(heads_here):
        attended = jnp.transpose(mix_ref[head] / sum_ref[head]).astype(jnp.bfloat16)
        att_ref[:, :, head * HD : (head + 1) * HD] = attended.reshape(n, rows, HD)

    def att_line(other, source):
        return remote(
            att_ref.at[other],
            att_all.at[seat, source],
            z_send.at[other],
            z_recv.at[source],
            {"head": other},
        )

    def att_passed(by, side):
        ref = att_all.at[chip_at(chips - by) * 2 + side]
        return remote(ref, ref, a_send.at[chips + by], b_recv.at[by], partner)

    for ahead in range(1, n):
        other = lax.rem(me + ahead, n)
        att_line(other, me).start()
    att_all[seat, me] = att_ref[me]

    @pl.when(is_helper)
    def _():
        for way, r, cut in along[early:]:
            wo_next(way, r, cut)
        for way, r, cut in back[:early]:
            wo_next(way, r, cut)

    def att_chip(by, z, which):
        ref = att_all.at[which * 2 + core, z]
        return remote(ref, ref, a_send.at[by], a_recv.at[by, z], place(chip_at(by), core))

    def att_pass(by, z, side):
        ref = att_all.at[chip_at(chips - by) * 2 + side, z]
        where = chips + by
        return remote(ref, ref, a_send.at[where], b_recv.at[by], partner)

    for ahead in range(n):
        z = lax.rem(me + ahead, n)
        if ahead:
            att_line(z, z).wait_recv()
        for by in range(1, chips):
            att_chip(by, z, chip).start()
        att_pass(0, z, core).start()

    for ahead in range(n):
        z = lax.rem(me + ahead, n)
        for by in range(1, chips):
            att_chip(by, z, chip_at(chips - by)).wait_recv()
            att_pass(by, z, core).start()
        if ahead == 1:

            @pl.when(is_helper)
            def _():
                for move in back[2:3]:
                    wo_next(*move)

    @pl.when(is_helper)
    def _():
        for move in back[3:4]:
            wo_next(*move)

    for by in range(chips):
        att_passed(by, 1 - core).wait_recv()

    def out_copy(which, side, source, cut):
        return remote(
            out_part.at[which * 2 + side, cut],
            out_in.at[source, cut],
            o_send.at[which * 2 + side],
            o_recv.at[source, cut],
            place(which, side),
        )

    others = [(by, side) for by in range(1, chips) for side in range(2)] + [(0, 1)]
    heads_wide = wo_ref.shape[2]
    for cut in range(cuts):

        @pl.when(is_end)
        def _():
            for r in (1, 2, 3):
                wo_copy(0, r, cut).wait_recv()

        @pl.when(is_helper)
        def _():
            for way, r, at in back[4:]:
                if cut == (max(0, at - 2) if r == 2 else at):
                    wo_next(way, r, at)

        total = None
        for z in range(n):
            lhs = att_all[:, z].reshape(seats * rows, heads_wide)
            made = jnp.dot(lhs, wo_ref[z, cut], preferred_element_type=jnp.float32)
            total = made if total is None else total + made
        out_part[:, cut] = total.astype(out_part.dtype).reshape(seats, rows, cut_cols)
        for by, side in others:
            lane = core if side == 0 else 1 - core
            out_copy(chip_at(by), lane, seat, cut).start()

    def finish(ref, source, cut):
        span = pl.ds(pl.multiple_of(source * cols_out + cut * cut_cols, 128), cut_cols)
        gate = table_ref[2, pl.ds(level, 1), span]
        out_ref[0, :, span] = (ref[source, cut].astype(jnp.float32) * gate).astype(out_ref.dtype)

    for cut in range(cuts):
        finish(out_part, seat, cut)
        for by, side in others:
            lane = core if side == 0 else 1 - core
            source = chip_at(chips - by) * 2 + lane
            out_copy(chip, core, source, cut).wait_recv()
            finish(out_in, source, cut)

    for by, side in others:
        lane = core if side == 0 else 1 - core
        target = chip_at(by) * 2 + lane
        ref = out_part.at[target]
        sems = o_send.at[target], o_recv.at[seat, 0]
        remote(ref, out_in.at[seat], *sems, place(chip_at(by), lane)).wait_send()
    for by in range(chips):
        if by:
            ref = att_all.at[seat]
            remote(ref, ref, a_send.at[by], a_recv.at[by, 0], partner).wait_send()
        att_passed(by, core).wait_send()
    for ahead in range(1, n):
        att_line(lax.rem(me + ahead, n), me).wait_send()
    for slot, used in ((0, core == 0), (1, tract < 2), (2, tract >= 2)):

        @pl.when(used)
        def _():
            kv_slot(slot).wait_send()

    def far_sent(where, which):
        ref = w_far.at[:, far_span(which, core)]
        remote(ref, ref, f_send.at[where], f_recv.at[where, 0], partner).wait_send()

    def wo_sent(way, r):
        ref = wo_ref.at[blk(r)]
        remote(ref, ref, wo_send.at[way, blk(r)], wo_recv.at[blk(r), 0], partner).wait_send()

    @pl.when(is_end)
    def _():
        far_sent(0, chip)
        tok_sent(0, 0, pieces)
        wo_sent(0, 0)

    @pl.when(is_helper)
    def _():
        for slot in range(chips):
            if slot:
                far_sent(slot, across[1] if slot == 3 else chip)
            far_sent(chips + slot, across[slot])
        for r in (1, 2, 3):
            ref = part_ref.at[blk(r)]
            sems = p_send.at[blk(r)], p_recv.at[blk(r), 0]
            remote(ref, ref, *sems, partner).wait_send()
            tok_sent(1, r, near)
            wo_sent(1, r)
        for r in (0, 1):
            tok_sent(0, r, pieces)
            wo_sent(0, r)


PIECES = 8
NEAR = 4


def fits_line(n, tracts, reps, frames, w_out):
    rows, width = frames.shape[1:]
    seats = tracts * reps
    far = (PIECES - NEAR) * (width // PIECES)
    return (
        n == 4
        and (tracts, reps) == (4, 2)
        and rows % 16 == 0
        and width % (PIECES * 128) == 0
        and width % (seats * 256) == 0
        and far % (seats * 16) == 0
        and w_out.shape[0] % 32 == 0
    )


def line_body(frames, levels, visible, w_qkv, w_out, modulation):
    n, tracts = lax.axis_size("head"), lax.axis_size("tract")
    reps = lax.axis_size("rep")
    rows, width = frames.shape[1:]
    cols = w_qkv.shape[2]
    heads_here = cols // HD
    seats = tracts * reps
    chips = seats // 2
    deep = width // PIECES
    cuts = width // seats // 256
    vmem = pl.BlockSpec(memory_space=pltpu.VMEM)
    hbm = pl.BlockSpec(memory_space=pltpu.HBM)
    smem = pl.BlockSpec(memory_space=pltpu.SMEM)
    half = jnp.bfloat16
    dma = pltpu.SemaphoreType.DMA
    return pl.pallas_call(
        functools.partial(line_kernel, n, tracts, reps, PIECES, NEAR),
        out_shape=pltpu.VMEM(frames.shape, frames.dtype),
        in_specs=[hbm, smem, smem, hbm, hbm, hbm],
        out_specs=vmem,
        scratch_shapes=[
            pltpu.VMEM((3, *modulation.shape[::2]), jnp.float32),
            pltpu.VMEM((rows, width), half),
            pltpu.VMEM((n, PIECES, rows, deep), half),
            pltpu.VMEM((3, width, cols), half),
            pltpu.VMEM((3, (PIECES - NEAR) * deep, cols), half),
            pltpu.VMEM((n, cuts, w_out.shape[0], 256), half),
            pltpu.VMEM((n, 3, rows, cols), jnp.float32),
            pltpu.VMEM((n, rows, cols), half),
            pltpu.VMEM((n, 2, rows, cols), half),
            pltpu.VMEM((max(1, tracts - 1), n, 2, rows, cols), half),
            pltpu.VMEM((n, 3, rows, cols), half),
            pltpu.VMEM((n, 3, rows, cols), half),
            pltpu.VMEM((n, rows, cols), half),
            pltpu.VMEM((heads_here, 1, n * rows), jnp.float32),
            pltpu.VMEM((heads_here, 1, n * rows), jnp.float32),
            pltpu.VMEM((heads_here, HD, n * rows), jnp.float32),
            pltpu.VMEM((seats, n, rows, cols), half),
            pltpu.VMEM((seats, cuts, rows, 256), half),
            pltpu.VMEM((seats, cuts, rows, 256), half),
            dma((2,)),
            dma((PIECES,)),
            dma((cuts,)),
            dma((2, n)),
            dma((n, PIECES)),
            dma((2 * chips,)),
            dma((2 * chips, 3)),
            dma((n,)),
            dma((n, 3)),
            dma((tracts,)),
            dma((tracts,)),
            dma((2, n)),
            dma((n, cuts)),
            dma((n,)),
            dma((n,)),
            dma((2 * chips,)),
            dma((chips, n)),
            dma((chips,)),
            dma((seats,)),
            dma((seats, cuts)),
        ],
        compiler_params=pltpu.CompilerParams(
            collective_id=0, has_side_effects=True, vmem_limit_bytes=GRANT
        ),
    )(
        frames,
        levels,
        visible,
        jnp.transpose(w_qkv, (1, 0, 2)),
        w_out,
        jnp.transpose(modulation, (1, 0, 2)),
    )


def body(frames, levels, visible, w_qkv, w_out, modulation):
    n, tracts = lax.axis_size("head"), lax.axis_size("tract")
    reps = lax.axis_size("rep")
    line = fits_line(n, tracts, reps, frames, w_out)
    chosen = line_body if line else ring_body
    return chosen(frames, levels, visible, w_qkv, w_out, modulation)


def solution(mesh):
    placed = (
        P(("rep", "tract"), "head", None),
        P(("rep", "tract")),
        P(("rep", "tract"), None),
        P(None, None, "head"),
        P("head", None),
        P(),
    )
    return jax.shard_map(
        body,
        mesh=mesh,
        in_specs=placed,
        out_specs=P(("rep", "tract"), "head", None),
        check_vma=False,
    )
```

```python
import functools

import jax
import jax.numpy as jnp
from jax import lax
from jax.experimental import pallas as pl
from jax.experimental.pallas import tpu as pltpu
from jax.sharding import PartitionSpec as P

HD = 128
GRANT = 60 * 1024 * 1024
MESH = pl.DeviceIdType.MESH


def meet(n, me, tracts, tract, others):
    barrier = pltpu.get_barrier_semaphore()
    for other in (lax.rem(me + 1, n), lax.rem(me + n - 1, n)):
        pl.semaphore_signal(barrier, inc=1, device_id={"head": other}, device_id_type=MESH)
    for ahead in range(1, tracts):
        other = lax.rem(tract + ahead, tracts)
        pl.semaphore_signal(barrier, inc=1, device_id={"tract": other}, device_id_type=MESH)
    for other in others:
        pl.semaphore_signal(barrier, inc=1, device_id=other, device_id_type=MESH)
    pl.semaphore_wait(barrier, 1 + tracts + len(others))


def sublayer_kernel(
    n,
    tracts,
    reps,
    pieces,
    halves,
    x_ref,
    level_ref,
    visible_ref,
    w_hbm,
    out_hbm,
    table_ref,
    out_ref,
    got,
    wq_ref,
    w_ref,
    q_ref,
    kv_ref,
    kv_in,
    att_ref,
    peak_ref,
    sum_ref,
    acc_ref,
    going,
    landed,
    total_ref,
    load_sem,
    g_send,
    g_recv,
    kv_send,
    kv_recv,
    s_send,
    s_recv,
    w_far,
    att_far,
    f_send,
    f_recv,
):
    me, tract = lax.axis_index("head"), lax.axis_index("tract")
    own = pltpu.make_async_copy(x_ref.at[0], got.at[me], load_sem.at[0])
    own.start()
    load = pltpu.make_async_copy(w_hbm, wq_ref, load_sem.at[1])
    load.start()
    load_out = pltpu.make_async_copy(out_hbm, w_ref, load_sem.at[2])
    load_out.start()
    core, wide = tract % 2, tracts // 2
    chips = wide * reps
    chip = lax.axis_index("rep") * wide + tract // 2
    slab = w_ref.shape[0] // (2 * chips)
    helper = (me == 1) | (me == n - 2)
    ends = (me == 0) | (me == n - 1)

    def seat(by):
        other = lax.rem(chip + by, chips)
        return {"rep": other // wide, "tract": lax.rem(other, wide) * 2 + core}

    def slab_of(which, side):
        start = pl.multiple_of((which * 2 + side) * slab, slab)
        return pl.ds(start, slab)

    def far_copy(kind, span, target, source=None):
        return pltpu.make_async_remote_copy(
            src_ref=(w_far if source is None else source).at[span],
            dst_ref=w_far.at[span],
            send_sem=f_send.at[kind],
            recv_sem=f_recv.at[kind],
            device_id=target,
            device_id_type=MESH,
        )

    inward = {"head": jnp.where(me == 0, 1, n - 2)}
    partner = {"tract": tract + 1 - 2 * core}
    mine = slab_of(chip, core)

    def to_helper():
        return far_copy(0, mine, inward, out_hbm)

    def to_chip(by):
        return far_copy(by, mine, seat(by))

    def from_chip(by):
        return far_copy(by, slab_of(lax.rem(chip + chips - by, chips), core), seat(by))

    def to_partner(by):
        span = slab_of(lax.rem(chip + chips - by, chips), core)
        return far_copy(chips + by, span, partner)

    def from_partner(by):
        span = slab_of(lax.rem(chip + chips - by, chips), 1 - core)
        return far_copy(chips + by, span, partner)

    def att_copy():
        return pltpu.make_async_remote_copy(
            src_ref=att_ref,
            dst_ref=att_far,
            send_sem=f_send.at[2 * chips],
            recv_sem=f_recv.at[2 * chips],
            device_id=inward,
            device_id_type=MESH,
        )

    meet(n, me, tracts, tract, [seat(by) for by in range(1, chips)])
    level = level_ref[0]

    def style(kind):
        return table_ref[kind, pl.ds(level, 1), :]

    rows, width = x_ref.shape[1:]
    part = rows // pieces

    def copy(way, step, piece, first=False):
        side = (way + 1) // 2
        span = pl.ds(piece * part, part)
        block = me - way * step
        return pltpu.make_async_remote_copy(
            src_ref=(x_ref.at[0] if first else got.at[block]).at[span],
            dst_ref=got.at[block].at[span],
            send_sem=g_send.at[side, step, piece],
            recv_sem=g_recv.at[side, step, piece],
            device_id={"head": me + way},
            device_id_type=MESH,
        )

    def arrival(way, step, piece):
        side = (way + 1) // 2
        span = pl.ds(piece * part, part)
        return pltpu.make_async_remote_copy(
            src_ref=x_ref.at[0].at[span],
            dst_ref=got.at[me - way * (step + 1)].at[span],
            send_sem=g_send.at[side, step, piece],
            recv_sem=g_recv.at[side, step, piece],
            device_id={"head": me - way},
            device_id_type=MESH,
        )

    def sends(way, step):
        block, target = me - way * step, me + way
        return (block >= 0) & (block < n) & (target >= 0) & (target < n) & (step < n - 1)

    def receives(way, step):
        block = me - way * (step + 1)
        return (block >= 0) & (block < n)

    def kv_copy(ahead, block):
        return pltpu.make_async_remote_copy(
            src_ref=kv_ref.at[block],
            dst_ref=kv_in.at[ahead - 1, block],
            send_sem=kv_send.at[ahead - 1, block],
            recv_sem=kv_recv.at[ahead - 1, block],
            device_id={"tract": tract + ahead},
            device_id_type=MESH,
        )

    def project(block):
        tokens = got[block].astype(jnp.float32)
        power = jnp.mean(tokens * tokens, axis=-1, keepdims=True)
        normed = tokens * lax.rsqrt(power + 1e-06)
        shaped = (normed * (1.0 + style(1)) + style(0)).astype(jnp.bfloat16)
        for kind in (1, 2, 0):
            made = jnp.dot(shaped, wq_ref[kind], preferred_element_type=jnp.float32)
            made = made.astype(jnp.bfloat16)
            if kind == 0:
                q_ref[block] = made
            else:
                kv_ref[block, kind - 1] = made
            if kind == 2:
                for ahead in range(1, tracts):

                    @pl.when(tract + ahead < tracts)
                    def _():
                        kv_copy(ahead, block).start()

    for piece in range(pieces):
        for way in (-1, 1):

            @pl.when(sends(way, 0))
            def _():
                copy(way, 0, piece, True).start()

    @pl.when(ends)
    def _():
        to_helper().start()

    own.wait()
    load.wait()
    project(me)

    @pl.loop(0, n - 1)
    def _(step):
        for piece in range(pieces):
            for way in (-1, 1):

                @pl.when(receives(way, step))
                def _():
                    arrival(way, step, piece).wait_recv()

                @pl.when(sends(way, step + 1))
                def _():
                    copy(way, step + 1, piece).start()

        @pl.loop(0, 2)
        def _(side):
            way = 2 * side - 1

            @pl.when(receives(way, step))
            def _():
                project(me - way * (step + 1))

        @pl.when(helper & (step == 0))
        def _():
            to_helper().wait_recv()
            for by in range(1, chips):
                to_chip(by).start()
            to_partner(0).start()

    @pl.when(helper)
    def _():
        for by in range(1, chips):
            from_chip(by).wait_recv()
            to_partner(by).start()

    tokens_here = n * rows
    heads_here = q_ref.shape[2] // HD
    scale = HD ** (-0.5)

    def attend(source, allowed):
        for head in range(heads_here):
            lanes = slice(head * HD, (head + 1) * HD)
            queries = q_ref[:, :, lanes].reshape(tokens_here, HD)
            keys = source[:, 0, :, lanes].reshape(tokens_here, HD)
            values = source[:, 1, :, lanes].reshape(tokens_here, HD)
            scores = (
                lax.dot_general(
                    queries, keys, (((1,), (1,)), ((), ())), preferred_element_type=jnp.float32
                )
                * scale
            )
            if allowed is None:
                peak = jnp.max(scores, axis=1, keepdims=True)
                probs = jnp.exp(scores - peak)
            else:
                scores = jnp.where(allowed, scores, -1e30)
                old = peak_ref[head]
                peak = jnp.maximum(old, jnp.max(scores, axis=1, keepdims=True))
                probs = jnp.where(allowed, jnp.exp(scores - peak), 0.0)
                rescale = jnp.exp(old - peak)
            row_sum = jnp.sum(probs, axis=1, keepdims=True)
            weighted = jnp.dot(
                probs.astype(jnp.bfloat16), values, preferred_element_type=jnp.float32
            )
            if allowed is not None:
                row_sum += sum_ref[head] * rescale
                weighted += acc_ref[head] * rescale
            peak_ref[head] = peak
            sum_ref[head] = row_sum
            acc_ref[head] = weighted

    attend(kv_ref, None)
    for ahead in range(1, tracts):

        @pl.when(tract >= ahead)
        def _():
            @pl.loop(0, n)
            def _(block):
                kv_copy(ahead, block).wait_recv()

            attend(kv_in.at[ahead - 1], visible_ref[0, lax.max(tract - ahead, 0)] > 0)

    for head in range(heads_here):
        attended = (acc_ref[head] / sum_ref[head]).astype(jnp.bfloat16)
        att_ref[:, :, head * HD : (head + 1) * HD] = attended.reshape(n, rows, HD)

    @pl.when(ends)
    def _():
        att_copy().start()

    load_out.wait()

    @pl.when(helper)
    def _():
        for by in range(chips):
            from_partner(by).wait_recv()
        att_copy().wait_recv()

    cols = width // halves

    def sum_copy(way, step, piece):
        side = (way + 1) // 2
        span = pl.ds(piece * cols, cols)
        return pltpu.make_async_remote_copy(
            src_ref=going.at[side, step].at[:, span],
            dst_ref=landed.at[side, step].at[:, span],
            send_sem=s_send.at[side, step, piece],
            recv_sem=s_recv.at[side, step, piece],
            device_id={"head": me + way},
            device_id_type=MESH,
        )

    def product(block, piece):
        return jnp.dot(
            att_ref[block],
            w_ref[:, piece * cols : (piece + 1) * cols],
            preferred_element_type=jnp.float32,
        )

    def far_product(block, piece):
        return jnp.dot(
            att_far[block],
            w_far[:, piece * cols : (piece + 1) * cols],
            preferred_element_type=jnp.float32,
        )

    def helps(way):
        return me == (1 if way == 1 else n - 2)

    def owner(way, step):
        return (n - 1 - step) if way == 1 else step

    def sum_sends(way, step):
        block = owner(way, step)
        return (block > me) & (me > 0) if way == 1 else (block < me) & (me < n - 1)

    def sum_receives(way, step):
        block = owner(way, step)
        return (block >= me) & (me > 1) if way == 1 else (block <= me) & (me < n - 2)

    @pl.loop(0, n - 1)
    def _(tick):
        for piece in range(halves):
            span = slice(piece * cols, (piece + 1) * cols)
            for way in (-1, 1):
                side = (way + 1) // 2
                step = tick - (me if way == 1 else n - 1 - me)
                held = (step >= 0) & (step < n - 1)

                @pl.when(held & sum_sends(way, step))
                def _():
                    going[side, step, :, span] = product(owner(way, step), piece).astype(
                        going.dtype
                    )

                    @pl.when(helps(way))
                    def _():
                        going[side, step, :, span] = (
                            going[side, step, :, span].astype(jnp.float32)
                            + far_product(owner(way, step), piece)
                        ).astype(going.dtype)

                    @pl.when(sum_receives(way, step))
                    def _():
                        sum_copy(way, step, piece).wait_recv()
                        going[side, step, :, span] = (
                            going[side, step, :, span].astype(jnp.float32)
                            + landed[side, step, :, span].astype(jnp.float32)
                        ).astype(going.dtype)

                    sum_copy(way, step, piece).start()

    for piece in range(halves):
        span = slice(piece * cols, (piece + 1) * cols)
        total_ref[:, span] = product(me, piece).astype(going.dtype).astype(jnp.float32)
    for piece in range(halves):
        span = slice(piece * cols, (piece + 1) * cols)
        for way in (-1, 1):
            side = (way + 1) // 2
            last = n - 1 - me if way == 1 else me

            @pl.when(helps(way))
            def _():
                total_ref[:, span] += far_product(me, piece)

            @pl.when(me > 1 if way == 1 else me < n - 2)
            def _():
                sum_copy(way, last, piece).wait_recv()
                total_ref[:, span] += landed[side, last, :, span].astype(jnp.float32)

        out_ref[0, :, span] = (
            total_ref[:, span] * table_ref[2, pl.ds(level, 1), span]
        ).astype(out_ref.dtype)

    @pl.loop(0, n - 1)
    def _(step):
        for piece in range(halves):
            for way in (-1, 1):

                @pl.when(sum_sends(way, step))
                def _():
                    sum_copy(way, step, piece).wait_send()

    @pl.loop(0, n)
    def _(block):
        for ahead in range(1, tracts):

            @pl.when(tract + ahead < tracts)
            def _():
                kv_copy(ahead, block).wait_send()

    @pl.loop(0, n - 1)
    def _(step):
        for piece in range(pieces):
            for way in (-1, 1):

                @pl.when(sends(way, step))
                def _():
                    copy(way, step, piece).wait_send()

    @pl.when(ends)
    def _():
        to_helper().wait_send()
        att_copy().wait_send()

    @pl.when(helper)
    def _():
        for by in range(1, chips):
            to_chip(by).wait_send()
        for by in range(chips):
            to_partner(by).wait_send()


def ring_body(frames, levels, visible, w_qkv, w_out, modulation):
    n, tracts = lax.axis_size("head"), lax.axis_size("tract")
    reps = lax.axis_size("rep")
    rows, width = frames.shape[1:]
    cols = w_qkv.shape[2]
    heads_here = cols // HD
    pieces = max(1, rows // 32)
    halves = 4 if width % 512 == 0 else 2
    vmem = pl.BlockSpec(memory_space=pltpu.VMEM)
    hbm = pl.BlockSpec(memory_space=pltpu.HBM)
    smem = pl.BlockSpec(memory_space=pltpu.SMEM)
    half = jnp.bfloat16
    dma = pltpu.SemaphoreType.DMA
    return pl.pallas_call(
        functools.partial(sublayer_kernel, n, tracts, reps, pieces, halves),
        out_shape=jax.ShapeDtypeStruct(frames.shape, frames.dtype),
        in_specs=[hbm, smem, smem, hbm, hbm, vmem],
        out_specs=vmem,
        scratch_shapes=[
            pltpu.VMEM((n, rows, width), half),
            pltpu.VMEM((3, width, cols), half),
            pltpu.VMEM(w_out.shape, half),
            pltpu.VMEM((n, rows, cols), half),
            pltpu.VMEM((n, 2, rows, cols), half),
            pltpu.VMEM((max(1, tracts - 1), n, 2, rows, cols), half),
            pltpu.VMEM((n, rows, cols), half),
            pltpu.VMEM((heads_here, n * rows, 1), jnp.float32),
            pltpu.VMEM((heads_here, n * rows, 1), jnp.float32),
            pltpu.VMEM((heads_here, n * rows, HD), jnp.float32),
            pltpu.VMEM((2, n - 1, rows, width), half),
            pltpu.VMEM((2, n - 1, rows, width), half),
            pltpu.VMEM((rows, width), jnp.float32),
            dma((3,)),
            dma((2, n, pieces)),
            dma((2, n, pieces)),
            dma((tracts, n)),
            dma((tracts, n)),
            dma((2, n, halves)),
            dma((2, n, halves)),
            pltpu.VMEM(w_out.shape, half),
            pltpu.VMEM((n, rows, cols), half),
            dma((tracts * reps + 1,)),
            dma((tracts * reps + 1,)),
        ],
        compiler_params=pltpu.CompilerParams(
            collective_id=0, has_side_effects=True, vmem_limit_bytes=GRANT
        ),
    )(
        frames,
        levels,
        visible,
        jnp.transpose(w_qkv, (1, 0, 2)),
        w_out,
        jnp.transpose(modulation, (1, 0, 2)),
    )


def line_kernel(
    n,
    tracts,
    reps,
    pieces,
    near,
    x_ref,
    level_ref,
    visible_ref,
    w_hbm,
    out_hbm,
    table_hbm,
    out_ref,
    table_ref,
    raw,
    got,
    wq_ref,
    w_far,
    wo_ref,
    acc_ref,
    q_ref,
    kv_ref,
    kv_in,
    part_ref,
    part_in,
    att_ref,
    peak_ref,
    sum_ref,
    mix_ref,
    att_all,
    out_part,
    out_in,
    load_sem,
    wq_sem,
    wo_sem,
    g_send,
    g_recv,
    f_send,
    f_recv,
    p_send,
    p_recv,
    kv_send,
    kv_recv,
    wo_send,
    wo_recv,
    z_send,
    z_recv,
    a_send,
    a_recv,
    b_recv,
    o_send,
    o_recv,
):
    me, tract, rep = lax.axis_index("head"), lax.axis_index("tract"), lax.axis_index("rep")
    rows, width = x_ref.shape[1:]
    deep = width // pieces
    low = me < 2
    sign = jnp.where(low, 1, -1)
    base = jnp.where(low, 0, n - 1)
    is_end = (me == 0) | (me == n - 1)
    is_helper = (me == 1) | (me == n - 2)
    inner, outer = {"head": me + sign}, {"head": me - sign}

    def blk(r):
        return base + sign * r

    core, wide = tract % 2, tracts // 2
    chips = wide * reps
    seats = chips * 2
    chip = rep * wide + tract // 2
    seat = chip * 2 + core
    partner = {"tract": tract + 1 - 2 * core}

    def chip_at(by):
        return lax.rem(chip + by, chips)

    def place(which, side):
        return {"rep": which // wide, "tract": lax.rem(which, wide) * 2 + side}

    across = [
        chip,
        rep * wide + 1 - lax.rem(chip, wide),
        (1 - rep) * wide + lax.rem(chip, wide),
        (1 - rep) * wide + 1 - lax.rem(chip, wide),
    ]
    along_x, along_y = place(across[1], core), place(across[2], core)
    others = [(by, side) for by in (1, 2, 3) for side in (0, 1)] + [(0, 1)]

    def seat_of(by, side):
        return across[(3, 1, 2)[by - 1] if by else 0], core if side == 0 else 1 - core


    own_load = pltpu.make_async_copy(x_ref.at[0], raw, load_sem.at[0])
    own_load.start()
    table_load = pltpu.make_async_copy(table_hbm, table_ref, load_sem.at[1])
    table_load.start()
    cols_out = width // seats
    cuts = wo_ref.shape[1]
    cut_cols = cols_out // cuts

    def wo_load(cut):
        start = pl.multiple_of(seat * cols_out + cut * cut_cols, 128)
        src = out_hbm.at[:, pl.ds(start, cut_cols)]
        return pltpu.make_async_copy(src, wo_ref.at[me, cut], wo_sem.at[cut])

    def wo_loaded():
        for cut in range(cuts):
            wo_load(cut).wait()

    def wq_load(p):
        span = pl.ds(pl.multiple_of(p * deep, deep), deep)
        return pltpu.make_async_copy(w_hbm.at[:, span], wq_ref.at[:, span], wq_sem.at[p])

    @pl.loop(0, pieces)
    def _(p):
        wq_load(p).start()

    for cut in range(cuts):
        wo_load(cut).start()

    barrier = pltpu.get_barrier_semaphore()
    for ahead in range(1, n):
        other = lax.rem(me + ahead, n)
        pl.semaphore_signal(barrier, inc=1, device_id={"head": other}, device_id_type=MESH)
    for other in others:
        target = place(*seat_of(*other))
        pl.semaphore_signal(barrier, inc=1, device_id=target, device_id_type=MESH)

    level = level_ref[0]

    def style(kind, start):
        return table_ref[kind, pl.ds(level, 1), start : start + deep]

    def remote(src, dst, send, recv, target):
        return pltpu.make_async_remote_copy(
            src_ref=src,
            dst_ref=dst,
            send_sem=send,
            recv_sem=recv,
            device_id=target,
            device_id_type=MESH,
        )

    def tok(way, r, p):
        b = blk(r)
        ref = got.at[b, p]
        target = inner if way == 0 else outer
        return remote(ref, ref, g_send.at[way, b], g_recv.at[b, p], target)

    def tok_sent(way, r, count):
        b = blk(r)
        ref = got.at[b, pl.ds(0, count)]
        target = inner if way == 0 else outer
        remote(ref, ref, g_send.at[way, b], g_recv.at[b, 0], target).wait_send()

    far_rows = w_far.shape[1] // seats
    far_base = near * deep

    def far_span(which, side):
        start = (which * 2 + side) * far_rows
        return pl.ds(pl.multiple_of(start, far_rows), far_rows)

    def far_first(kind):
        start = far_base + seat * far_rows
        src = w_hbm.at[kind, pl.ds(pl.multiple_of(start, far_rows), far_rows)]
        dst = w_far.at[kind, far_span(chip, core)]
        return remote(src, dst, f_send.at[0], f_recv.at[0, kind], inner)

    def far_move(slot, kind, which):
        ref = w_far.at[kind, far_span(which, core)]
        target = along_x if slot == 1 else along_y
        return remote(ref, ref, f_send.at[slot], f_recv.at[slot, kind], target)

    def far_pass(slot, kind, side):
        ref = w_far.at[kind, far_span(across[slot], side)]
        where = chips + slot
        return remote(ref, ref, f_send.at[where], f_recv.at[where, kind], partner)

    def far_relay(kind):
        far_first(kind).wait_recv()
        far_move(1, kind, chip).start()
        far_move(2, kind, chip).start()
        far_pass(0, kind, core).start()

    def far_hand_x(kind):
        far_move(1, kind, across[1]).wait_recv()
        far_move(3, kind, across[1]).start()
        far_pass(1, kind, core).start()

    def far_hand_y(kind):
        for slot in (2, 3):
            far_move(slot, kind, across[slot]).wait_recv()
            far_pass(slot, kind, core).start()

    def far_ready(kind):
        for slot in range(chips):
            far_pass(slot, kind, 1 - core).wait_recv()

    def part_copy(r, kind):
        b = blk(r)
        return remote(
            part_ref.at[b, kind],
            part_in.at[b, kind],
            p_send.at[b],
            p_recv.at[b, kind],
            outer,
        )

    def far_part(rs, kinds):
        for kind in kinds:
            total = None
            for p in range(near, pieces):
                lhs = jnp.concatenate([got[blk(r), p] for r in rs], axis=0)
                span = slice((p - near) * deep, (p - near + 1) * deep)
                made = jnp.dot(lhs, w_far[kind, span], preferred_element_type=jnp.float32)
                total = made if total is None else total + made
            total = total.astype(part_ref.dtype)
            for i, r in enumerate(rs):
                part_ref[blk(r), kind] = total[i * rows : (i + 1) * rows]
        for r in rs:
            for kind in kinds:
                part_copy(r, kind).start()

    halves = wo_recv.shape[2]
    half_rows = wo_ref.shape[2] // halves

    def wo_copy(way, r, cut, half):
        b = blk(r)
        ref = wo_ref.at[b, cut, pl.ds(half * half_rows, half_rows)]
        target = inner if way == 0 else outer
        return remote(ref, ref, wo_send.at[way, b], wo_recv.at[b, cut, half], target)

    def wo_start(way, r, which):
        for cut in which:
            for half in range(halves):
                wo_copy(way, r, cut, half).start()

    along = [(0, r, cut) for cut in range(cuts) for r in (1, 0)]
    back = [(1, r, cut) for cut in range(cuts) for r in (2, 3)]
    early = 2

    def wo_next(way, r, cut):
        for half in range(halves):
            if r != 1:
                wo_copy(way, r, cut, half).wait_recv()
            wo_copy(way, r, cut, half).start()

    def wo_moves(*moves):
        @pl.when(is_helper)
        def _():
            for move in moves:
                wo_next(*move)

    def kv_near(b):
        ref, slot = kv_ref.at[b], kv_in.at[0, b]
        return remote(ref, slot, kv_send.at[0], kv_recv.at[0], partner)

    def kv_far(b):
        ref, slot = kv_ref.at[b], kv_in.at[1, b]
        return remote(ref, slot, kv_send.at[1], kv_recv.at[1], along_x)

    def kv_relay():
        slot = 2 * (1 - core)
        return remote(kv_in.at[1], kv_in.at[slot], kv_send.at[2], kv_recv.at[slot], partner)

    def kv_slot(slot):
        return remote(kv_ref, kv_in.at[slot], kv_send.at[slot], kv_recv.at[slot], partner)

    def accumulate(rs, p):
        lhs = jnp.concatenate([got[blk(r), p] for r in rs], axis=0)
        span = pl.ds(pl.multiple_of(p * deep, deep), deep)
        for kind in range(3):
            made = jnp.dot(lhs, wq_ref[kind, span], preferred_element_type=jnp.float32)
            for i, r in enumerate(rs):
                acc_ref[blk(r), kind] += made[i * rows : (i + 1) * rows]

    def settle(r, kinds, extra=False):
        b = blk(r)
        for kind in kinds:
            made = acc_ref[b, kind]
            if extra:
                made = made + part_in[b, kind].astype(jnp.float32)
            made = made.astype(q_ref.dtype)
            if kind == 0:
                q_ref[b] = made
            else:
                kv_ref[b, kind - 1] = made

    def share(r):
        @pl.when(tract < 2)
        def _():
            kv_far(blk(r)).start()

        @pl.when(core == 0)
        def _():
            kv_near(blk(r)).start()

    acc_ref[...] = jnp.zeros_like(acc_ref)
    own_load.wait()
    power = jnp.zeros((rows, 1), jnp.float32)
    for p in range(pieces):
        tokens = raw[:, p * deep : (p + 1) * deep].astype(jnp.float32)
        power += jnp.sum(tokens * tokens, axis=-1, keepdims=True)
    table_load.wait()
    factor = lax.rsqrt(power * (1.0 / width) + 1e-06)
    pl.semaphore_wait(barrier, n - 1 + len(others))

    @pl.when(is_end)
    def _():
        for kind in (1, 2):
            far_first(kind).start()

    def send_own(p):
        @pl.when(is_end)
        def _():
            tok(0, 0, p).start()
            if p == 0:
                far_first(0).start()

        @pl.when(is_helper)
        def _():
            tok(0, 1, p).start()
            if p < near:
                tok(1, 1, p).start()

    for p in range(pieces):
        tokens = raw[:, p * deep : (p + 1) * deep].astype(jnp.float32)
        shaped = tokens * factor * (1.0 + style(1, p * deep)) + style(0, p * deep)
        got[me, p] = shaped.astype(got.dtype)
        if p:
            send_own(p - 1)
    send_own(pieces - 1)

    @pl.when(is_end)
    def _():
        @pl.loop(0, pieces)
        def _(p):
            wq_load(p).wait()
            accumulate((0,), p)

        wo_loaded()
        wo_start(0, 0, range(cuts))

        settle(0, (1, 2, 0))
        share(0)
        for r in (1, 2):

            @pl.loop(0, near)
            def _(p):
                tok(0, r, p).wait_recv()
                accumulate((r,), p)

        for r in (1, 2):
            for kind in (1, 2):
                part_copy(r, kind).wait_recv()
            settle(r, (1, 2), True)
            share(r)

        @pl.loop(0, near)
        def _(p):
            tok(0, 3, p).wait_recv()
            accumulate((3,), p)

        for kind in (1, 2):
            part_copy(3, kind).wait_recv()
        settle(3, (1, 2), True)
        share(3)
        for r in (1, 2, 3):
            part_copy(r, 0).wait_recv()
            settle(r, (0,), True)

    @pl.when(is_helper)
    def _():
        def pass_on(p):
            tok(0, 0, p).wait_recv()
            tok(0, 0, p).start()
            accumulate((0,), p)

        @pl.loop(0, pieces)
        def _(p):
            wq_load(p).wait()
            tok(1, 2, p).wait_recv()

            @pl.when(p < near)
            def _():
                tok(1, 2, p).start()

            accumulate((1, 2), p)
            for at, kind in ((1, 1), (3, 2), (7, 0)):

                @pl.when(p == at)
                def _():
                    far_relay(kind)

            @pl.when(p == near)
            def _():
                wo_loaded()
                wo_start(1, 1, range(cuts - 1))

            for at, kind in ((4, 1), (6, 2)):

                @pl.when(p == at)
                def _():
                    far_hand_x(kind)

            @pl.when(p >= pieces - 2)
            def _():
                pass_on(p - (pieces - 2))

        settle(1, (1, 2, 0))
        share(1)
        settle(2, (1, 2, 0))
        share(2)

        @pl.loop(0, pieces)
        def _(p):
            @pl.when(p + 2 < pieces)
            def _():
                pass_on(p + 2)

            @pl.when(p == pieces - 1)
            def _():
                far_ready(0)
                far_part((1, 2), (0,))

            tok(1, 3, p).wait_recv()

            @pl.when(p < near)
            def _():
                tok(1, 3, p).start()

            accumulate((3,), p)

            @pl.when(p == 1)
            def _():
                far_hand_y(1)

            @pl.when(p == 2)
            def _():
                far_hand_x(0)
                far_ready(1)
                far_part((1, 2), (1,))

            @pl.when(p == 3)
            def _():
                far_hand_y(2)

            @pl.when(p == 4)
            def _():
                far_ready(2)
                far_part((1, 2), (2,))
                wo_start(1, 1, (cuts - 1,))

            @pl.when(p == 5)
            def _():
                settle(0, (1, 2, 0))
                share(0)

            @pl.when(p == 5)
            def _():
                far_hand_y(0)

        far_part((3,), (1, 2, 0))
        settle(3, (1, 2))
        share(3)
        settle(3, (0,))
        for way, r, cut in along[:early]:
            wo_next(way, r, cut)

    tokens_here = n * rows
    heads_here = q_ref.shape[2] // HD
    scale = HD ** (-0.5)

    def attend(source, bias):
        for head in range(heads_here):
            lanes = slice(head * HD, (head + 1) * HD)
            queries = q_ref[:, :, lanes].reshape(tokens_here, HD)
            keys = source[:, 0, :, lanes].reshape(tokens_here, HD)
            values = source[:, 1, :, lanes].reshape(tokens_here, HD)
            scores = (
                lax.dot_general(
                    keys, queries, (((1,), (1,)), ((), ())), preferred_element_type=jnp.float32
                )
                * scale
            )
            if bias is not None:
                scores = scores + bias
            peak = jnp.max(scores, axis=0, keepdims=True)
            if bias is not None:
                old = peak_ref[head]
                peak = jnp.maximum(old, peak)
            probs = jnp.exp(scores - peak)
            row_sum = jnp.sum(probs, axis=0, keepdims=True)
            weighted = lax.dot_general(
                values,
                probs.astype(jnp.bfloat16),
                (((0,), (0,)), ((), ())),
                preferred_element_type=jnp.float32,
            )
            if bias is not None:
                rescale = jnp.exp(old - peak)
                row_sum += sum_ref[head] * rescale
                weighted += mix_ref[head] * rescale
            peak_ref[head] = peak
            sum_ref[head] = row_sum
            mix_ref[head] = weighted

    attend(kv_ref, None)

    @pl.when(tract >= 2)
    def _():
        kv_slot(1).wait_recv()
        kv_relay().start()

    for ahead in (2, 1, 3):
        if ahead == 3:

            @pl.when(is_helper)
            def _():
                wo_next(*back[0])

        @pl.when(tract >= ahead)
        def _():
            if ahead != 2:
                kv_slot(ahead - 1).wait_recv()
            seen = visible_ref[0, lax.max(tract - ahead, 0)] > 0
            attend(kv_in.at[ahead - 1], jnp.where(seen, 0.0, -1e30))

    for head in range(heads_here):
        attended = jnp.transpose(mix_ref[head] / sum_ref[head]).astype(jnp.bfloat16)
        att_ref[:, :, head * HD : (head + 1) * HD] = attended.reshape(n, rows, HD)

    def att_line(other, source):
        return remote(
            att_ref.at[other],
            att_all.at[seat, source],
            z_send.at[other],
            z_recv.at[source],
            {"head": other},
        )

    for ahead in range(1, n):
        other = lax.rem(me + ahead, n)
        att_line(other, me).start()
    att_all[seat, me] = att_ref[me]

    def att_chip(by, z, which):
        ref = att_all.at[which * 2 + core] if z is None else att_all.at[which * 2 + core, z]
        at = a_recv.at[by, 0 if z is None else z]
        return remote(ref, ref, a_send.at[by], at, place(seat_of(by, 0)[0], core))

    def att_pass(by, z, side):
        owner = seat_of(by, 0)[0] * 2 + side
        ref = att_all.at[owner] if z is None else att_all.at[owner, z]
        return remote(ref, ref, a_send.at[chips + by], b_recv.at[by], partner)

    @pl.when(is_helper)
    def _():
        for move in along[early:]:
            wo_next(*move)

    line = [blk(jnp.where(is_end, end, help)) for end, help in ((0, 1), (1, 2), (2, 0), (3, 3))]

    for ahead, z in enumerate(line):
        if ahead:
            att_line(z, z).wait_recv()
        for by in range(1, chips):
            att_chip(by, z, chip).start()
        att_pass(0, z, core).start()
        if ahead < 2:
            wo_moves(back[1 + ahead])

    wo_moves(*back[3:4])
    for z in line:
        for by in range(1, chips):
            att_chip(by, z, seat_of(by, 0)[0]).wait_recv()
            att_pass(by, z, core).start()
    wo_moves(*back[4:5])
    for by in range(chips):
        att_pass(by, None, 1 - core).wait_recv()

    def out_copy(by, side, source, cut):
        which, lane = seat_of(by, side)
        return remote(
            out_part.at[which * 2 + lane, cut],
            out_in.at[source, cut],
            o_send.at[which * 2 + lane],
            o_recv.at[source, cut],
            place(which, lane),
        )

    heads_wide = wo_ref.shape[2]

    def finish(ref, source, cut):
        span = pl.ds(pl.multiple_of(source * cols_out + cut * cut_cols, 128), cut_cols)
        gate = table_ref[2, pl.ds(level, 1), span]
        done = ref[source, cut].astype(jnp.float32) * gate
        out_ref[0, :, span] = done.astype(out_ref.dtype)

    def finish_cut(cut):
        finish(out_part, seat, cut)
        for by, side in reversed(others):
            which, lane = seat_of(by, side)
            source = which * 2 + lane
            out_copy(by, side, source, cut).wait_recv()
            finish(out_in, source, cut)

    for cut in range(cuts):

        @pl.when(is_end)
        def _():
            if cut == 2:
                finish_cut(0)
            for r in (1, 2, 3):
                for half in range(halves):
                    wo_copy(0, r, cut, half).wait_recv()

        total = None
        for z in range(n):
            lhs = att_all[:, z].reshape(seats * rows, heads_wide)
            made = jnp.dot(lhs, wo_ref[z, cut], preferred_element_type=jnp.float32)
            total = made if total is None else total + made
        out_part[:, cut] = total.astype(out_part.dtype).reshape(seats, rows, cut_cols)
        for by, side in others:
            out_copy(by, side, seat, cut).start()
        if cut == 0:
            wo_moves(*back[5:])

    for cut in range(cuts):
        if cut == 0 and cuts > 2:

            @pl.when(is_helper)
            def _():
                finish_cut(0)
        else:
            finish_cut(cut)

    for by, side in others:
        which, lane = seat_of(by, side)
        to = which * 2 + lane
        sems = o_send.at[to], o_recv.at[seat, 0]
        remote(out_part.at[to], out_in.at[seat], *sems, partner).wait_send()
    for by in range(chips):
        if by:
            att_chip(by, None, chip).wait_send()
        att_pass(by, None, core).wait_send()
    for ahead in range(1, n):
        att_line(lax.rem(me + ahead, n), me).wait_send()
    for slot, used in ((0, core == 0), (1, tract < 2), (2, tract >= 2)):

        @pl.when(used)
        def _():
            kv_slot(slot).wait_send()

    def far_sent(where, which):
        ref = w_far.at[:, far_span(which, core)]
        remote(ref, ref, f_send.at[where], f_recv.at[where, 0], partner).wait_send()

    def wo_sent(way, r):
        ref = wo_ref.at[blk(r)]
        sems = wo_send.at[way, blk(r)], wo_recv.at[blk(r), 0, 0]
        remote(ref, ref, *sems, partner).wait_send()

    @pl.when(is_end)
    def _():
        far_sent(0, chip)
        tok_sent(0, 0, pieces)
        wo_sent(0, 0)

    @pl.when(is_helper)
    def _():
        for slot in range(chips):
            if slot:
                far_sent(slot, across[1] if slot == 3 else chip)
            far_sent(chips + slot, across[slot])
        for r in (1, 2, 3):
            ref = part_ref.at[blk(r)]
            sems = p_send.at[blk(r)], p_recv.at[blk(r), 0]
            remote(ref, ref, *sems, partner).wait_send()
            tok_sent(1, r, near)
            wo_sent(1, r)
        for r in (0, 1):
            tok_sent(0, r, pieces)
            wo_sent(0, r)


PIECES = 8
NEAR = 4


def fits_line(n, tracts, reps, frames, w_out):
    rows, width = frames.shape[1:]
    seats = tracts * reps
    far = (PIECES - NEAR) * (width // PIECES)
    return (
        n == 4
        and (tracts, reps) == (4, 2)
        and rows % 16 == 0
        and width % (PIECES * 128) == 0
        and width % (seats * 256) == 0
        and far % (seats * 16) == 0
        and w_out.shape[0] % 32 == 0
    )


def line_body(frames, levels, visible, w_qkv, w_out, modulation):
    n, tracts = lax.axis_size("head"), lax.axis_size("tract")
    reps = lax.axis_size("rep")
    rows, width = frames.shape[1:]
    cols = w_qkv.shape[2]
    heads_here = cols // HD
    seats = tracts * reps
    chips = seats // 2
    deep = width // PIECES
    cuts = width // seats // 256
    vmem = pl.BlockSpec(memory_space=pltpu.VMEM)
    hbm = pl.BlockSpec(memory_space=pltpu.HBM)
    smem = pl.BlockSpec(memory_space=pltpu.SMEM)
    half = jnp.bfloat16
    dma = pltpu.SemaphoreType.DMA
    return pl.pallas_call(
        functools.partial(line_kernel, n, tracts, reps, PIECES, NEAR),
        out_shape=pltpu.VMEM(frames.shape, frames.dtype),
        in_specs=[hbm, smem, smem, hbm, hbm, hbm],
        out_specs=vmem,
        scratch_shapes=[
            pltpu.VMEM((3, *modulation.shape[::2]), jnp.float32),
            pltpu.VMEM((rows, width), half),
            pltpu.VMEM((n, PIECES, rows, deep), half),
            pltpu.VMEM((3, width, cols), half),
            pltpu.VMEM((3, (PIECES - NEAR) * deep, cols), half),
            pltpu.VMEM((n, cuts, w_out.shape[0], 256), half),
            pltpu.VMEM((n, 3, rows, cols), jnp.float32),
            pltpu.VMEM((n, rows, cols), half),
            pltpu.VMEM((n, 2, rows, cols), half),
            pltpu.VMEM((max(1, tracts - 1), n, 2, rows, cols), half),
            pltpu.VMEM((n, 3, rows, cols), half),
            pltpu.VMEM((n, 3, rows, cols), half),
            pltpu.VMEM((n, rows, cols), half),
            pltpu.VMEM((heads_here, 1, n * rows), jnp.float32),
            pltpu.VMEM((heads_here, 1, n * rows), jnp.float32),
            pltpu.VMEM((heads_here, HD, n * rows), jnp.float32),
            pltpu.VMEM((seats, n, rows, cols), half),
            pltpu.VMEM((seats, cuts, rows, 256), half),
            pltpu.VMEM((seats, cuts, rows, 256), half),
            dma((2,)),
            dma((PIECES,)),
            dma((cuts,)),
            dma((2, n)),
            dma((n, PIECES)),
            dma((2 * chips,)),
            dma((2 * chips, 3)),
            dma((n,)),
            dma((n, 3)),
            dma((tracts,)),
            dma((tracts,)),
            dma((2, n)),
            dma((n, cuts, 2)),
            dma((n,)),
            dma((n,)),
            dma((2 * chips,)),
            dma((chips, n)),
            dma((chips,)),
            dma((seats,)),
            dma((seats, cuts)),
        ],
        compiler_params=pltpu.CompilerParams(
            collective_id=0, has_side_effects=True, vmem_limit_bytes=GRANT
        ),
    )(
        frames,
        levels,
        visible,
        jnp.transpose(w_qkv, (1, 0, 2)),
        w_out,
        jnp.transpose(modulation, (1, 0, 2)),
    )


def body(frames, levels, visible, w_qkv, w_out, modulation):
    n, tracts = lax.axis_size("head"), lax.axis_size("tract")
    reps = lax.axis_size("rep")
    line = fits_line(n, tracts, reps, frames, w_out)
    chosen = line_body if line else ring_body
    return chosen(frames, levels, visible, w_qkv, w_out, modulation)


def solution(mesh):
    placed = (
        P(("rep", "tract"), "head", None),
        P(("rep", "tract")),
        P(("rep", "tract"), None),
        P(None, None, "head"),
        P("head", None),
        P(),
    )
    return jax.shard_map(
        body,
        mesh=mesh,
        in_specs=placed,
        out_specs=P(("rep", "tract"), "head", None),
        check_vma=False,
    )
```

```python
import functools

import jax
import jax.numpy as jnp
from jax import lax
from jax.experimental import pallas as pl
from jax.experimental.pallas import tpu as pltpu
from jax.sharding import PartitionSpec as P

HD = 128
GRANT = 60 * 1024 * 1024
MESH = pl.DeviceIdType.MESH


def meet(n, me, tracts, tract, others):
    barrier = pltpu.get_barrier_semaphore()
    for other in (lax.rem(me + 1, n), lax.rem(me + n - 1, n)):
        pl.semaphore_signal(barrier, inc=1, device_id={"head": other}, device_id_type=MESH)
    for ahead in range(1, tracts):
        other = lax.rem(tract + ahead, tracts)
        pl.semaphore_signal(barrier, inc=1, device_id={"tract": other}, device_id_type=MESH)
    for other in others:
        pl.semaphore_signal(barrier, inc=1, device_id=other, device_id_type=MESH)
    pl.semaphore_wait(barrier, 1 + tracts + len(others))


def sublayer_kernel(
    n,
    tracts,
    reps,
    pieces,
    halves,
    x_ref,
    level_ref,
    visible_ref,
    w_hbm,
    out_hbm,
    table_ref,
    out_ref,
    got,
    wq_ref,
    w_ref,
    q_ref,
    kv_ref,
    kv_in,
    att_ref,
    peak_ref,
    sum_ref,
    acc_ref,
    going,
    landed,
    total_ref,
    load_sem,
    g_send,
    g_recv,
    kv_send,
    kv_recv,
    s_send,
    s_recv,
    w_far,
    att_far,
    f_send,
    f_recv,
):
    me, tract = lax.axis_index("head"), lax.axis_index("tract")
    own = pltpu.make_async_copy(x_ref.at[0], got.at[me], load_sem.at[0])
    own.start()
    load = pltpu.make_async_copy(w_hbm, wq_ref, load_sem.at[1])
    load.start()
    load_out = pltpu.make_async_copy(out_hbm, w_ref, load_sem.at[2])
    load_out.start()
    core, wide = tract % 2, tracts // 2
    chips = wide * reps
    chip = lax.axis_index("rep") * wide + tract // 2
    slab = w_ref.shape[0] // (2 * chips)
    helper = (me == 1) | (me == n - 2)
    ends = (me == 0) | (me == n - 1)

    def seat(by):
        other = lax.rem(chip + by, chips)
        return {"rep": other // wide, "tract": lax.rem(other, wide) * 2 + core}

    def slab_of(which, side):
        start = pl.multiple_of((which * 2 + side) * slab, slab)
        return pl.ds(start, slab)

    def far_copy(kind, span, target, source=None):
        return pltpu.make_async_remote_copy(
            src_ref=(w_far if source is None else source).at[span],
            dst_ref=w_far.at[span],
            send_sem=f_send.at[kind],
            recv_sem=f_recv.at[kind],
            device_id=target,
            device_id_type=MESH,
        )

    inward = {"head": jnp.where(me == 0, 1, n - 2)}
    partner = {"tract": tract + 1 - 2 * core}
    mine = slab_of(chip, core)

    def to_helper():
        return far_copy(0, mine, inward, out_hbm)

    def to_chip(by):
        return far_copy(by, mine, seat(by))

    def from_chip(by):
        return far_copy(by, slab_of(lax.rem(chip + chips - by, chips), core), seat(by))

    def to_partner(by):
        span = slab_of(lax.rem(chip + chips - by, chips), core)
        return far_copy(chips + by, span, partner)

    def from_partner(by):
        span = slab_of(lax.rem(chip + chips - by, chips), 1 - core)
        return far_copy(chips + by, span, partner)

    def att_copy():
        return pltpu.make_async_remote_copy(
            src_ref=att_ref,
            dst_ref=att_far,
            send_sem=f_send.at[2 * chips],
            recv_sem=f_recv.at[2 * chips],
            device_id=inward,
            device_id_type=MESH,
        )

    meet(n, me, tracts, tract, [seat(by) for by in range(1, chips)])
    level = level_ref[0]

    def style(kind):
        return table_ref[kind, pl.ds(level, 1), :]

    rows, width = x_ref.shape[1:]
    part = rows // pieces

    def copy(way, step, piece, first=False):
        side = (way + 1) // 2
        span = pl.ds(piece * part, part)
        block = me - way * step
        return pltpu.make_async_remote_copy(
            src_ref=(x_ref.at[0] if first else got.at[block]).at[span],
            dst_ref=got.at[block].at[span],
            send_sem=g_send.at[side, step, piece],
            recv_sem=g_recv.at[side, step, piece],
            device_id={"head": me + way},
            device_id_type=MESH,
        )

    def arrival(way, step, piece):
        side = (way + 1) // 2
        span = pl.ds(piece * part, part)
        return pltpu.make_async_remote_copy(
            src_ref=x_ref.at[0].at[span],
            dst_ref=got.at[me - way * (step + 1)].at[span],
            send_sem=g_send.at[side, step, piece],
            recv_sem=g_recv.at[side, step, piece],
            device_id={"head": me - way},
            device_id_type=MESH,
        )

    def sends(way, step):
        block, target = me - way * step, me + way
        return (block >= 0) & (block < n) & (target >= 0) & (target < n) & (step < n - 1)

    def receives(way, step):
        block = me - way * (step + 1)
        return (block >= 0) & (block < n)

    def kv_copy(ahead, block):
        return pltpu.make_async_remote_copy(
            src_ref=kv_ref.at[block],
            dst_ref=kv_in.at[ahead - 1, block],
            send_sem=kv_send.at[ahead - 1, block],
            recv_sem=kv_recv.at[ahead - 1, block],
            device_id={"tract": tract + ahead},
            device_id_type=MESH,
        )

    def project(block):
        tokens = got[block].astype(jnp.float32)
        power = jnp.mean(tokens * tokens, axis=-1, keepdims=True)
        normed = tokens * lax.rsqrt(power + 1e-06)
        shaped = (normed * (1.0 + style(1)) + style(0)).astype(jnp.bfloat16)
        for kind in (1, 2, 0):
            made = jnp.dot(shaped, wq_ref[kind], preferred_element_type=jnp.float32)
            made = made.astype(jnp.bfloat16)
            if kind == 0:
                q_ref[block] = made
            else:
                kv_ref[block, kind - 1] = made
            if kind == 2:
                for ahead in range(1, tracts):

                    @pl.when(tract + ahead < tracts)
                    def _():
                        kv_copy(ahead, block).start()

    for piece in range(pieces):
        for way in (-1, 1):

            @pl.when(sends(way, 0))
            def _():
                copy(way, 0, piece, True).start()

    @pl.when(ends)
    def _():
        to_helper().start()

    own.wait()
    load.wait()
    project(me)

    @pl.loop(0, n - 1)
    def _(step):
        for piece in range(pieces):
            for way in (-1, 1):

                @pl.when(receives(way, step))
                def _():
                    arrival(way, step, piece).wait_recv()

                @pl.when(sends(way, step + 1))
                def _():
                    copy(way, step + 1, piece).start()

        @pl.loop(0, 2)
        def _(side):
            way = 2 * side - 1

            @pl.when(receives(way, step))
            def _():
                project(me - way * (step + 1))

        @pl.when(helper & (step == 0))
        def _():
            to_helper().wait_recv()
            for by in range(1, chips):
                to_chip(by).start()
            to_partner(0).start()

    @pl.when(helper)
    def _():
        for by in range(1, chips):
            from_chip(by).wait_recv()
            to_partner(by).start()

    tokens_here = n * rows
    heads_here = q_ref.shape[2] // HD
    scale = HD ** (-0.5)

    def attend(source, allowed):
        for head in range(heads_here):
            lanes = slice(head * HD, (head + 1) * HD)
            queries = q_ref[:, :, lanes].reshape(tokens_here, HD)
            keys = source[:, 0, :, lanes].reshape(tokens_here, HD)
            values = source[:, 1, :, lanes].reshape(tokens_here, HD)
            scores = (
                lax.dot_general(
                    queries, keys, (((1,), (1,)), ((), ())), preferred_element_type=jnp.float32
                )
                * scale
            )
            if allowed is None:
                peak = jnp.max(scores, axis=1, keepdims=True)
                probs = jnp.exp(scores - peak)
            else:
                scores = jnp.where(allowed, scores, -1e30)
                old = peak_ref[head]
                peak = jnp.maximum(old, jnp.max(scores, axis=1, keepdims=True))
                probs = jnp.where(allowed, jnp.exp(scores - peak), 0.0)
                rescale = jnp.exp(old - peak)
            row_sum = jnp.sum(probs, axis=1, keepdims=True)
            weighted = jnp.dot(
                probs.astype(jnp.bfloat16), values, preferred_element_type=jnp.float32
            )
            if allowed is not None:
                row_sum += sum_ref[head] * rescale
                weighted += acc_ref[head] * rescale
            peak_ref[head] = peak
            sum_ref[head] = row_sum
            acc_ref[head] = weighted

    attend(kv_ref, None)
    for ahead in range(1, tracts):

        @pl.when(tract >= ahead)
        def _():
            @pl.loop(0, n)
            def _(block):
                kv_copy(ahead, block).wait_recv()

            attend(kv_in.at[ahead - 1], visible_ref[0, lax.max(tract - ahead, 0)] > 0)

    for head in range(heads_here):
        attended = (acc_ref[head] / sum_ref[head]).astype(jnp.bfloat16)
        att_ref[:, :, head * HD : (head + 1) * HD] = attended.reshape(n, rows, HD)

    @pl.when(ends)
    def _():
        att_copy().start()

    load_out.wait()

    @pl.when(helper)
    def _():
        for by in range(chips):
            from_partner(by).wait_recv()
        att_copy().wait_recv()

    cols = width // halves

    def sum_copy(way, step, piece):
        side = (way + 1) // 2
        span = pl.ds(piece * cols, cols)
        return pltpu.make_async_remote_copy(
            src_ref=going.at[side, step].at[:, span],
            dst_ref=landed.at[side, step].at[:, span],
            send_sem=s_send.at[side, step, piece],
            recv_sem=s_recv.at[side, step, piece],
            device_id={"head": me + way},
            device_id_type=MESH,
        )

    def product(block, piece):
        return jnp.dot(
            att_ref[block],
            w_ref[:, piece * cols : (piece + 1) * cols],
            preferred_element_type=jnp.float32,
        )

    def far_product(block, piece):
        return jnp.dot(
            att_far[block],
            w_far[:, piece * cols : (piece + 1) * cols],
            preferred_element_type=jnp.float32,
        )

    def helps(way):
        return me == (1 if way == 1 else n - 2)

    def owner(way, step):
        return (n - 1 - step) if way == 1 else step

    def sum_sends(way, step):
        block = owner(way, step)
        return (block > me) & (me > 0) if way == 1 else (block < me) & (me < n - 1)

    def sum_receives(way, step):
        block = owner(way, step)
        return (block >= me) & (me > 1) if way == 1 else (block <= me) & (me < n - 2)

    @pl.loop(0, n - 1)
    def _(tick):
        for piece in range(halves):
            span = slice(piece * cols, (piece + 1) * cols)
            for way in (-1, 1):
                side = (way + 1) // 2
                step = tick - (me if way == 1 else n - 1 - me)
                held = (step >= 0) & (step < n - 1)

                @pl.when(held & sum_sends(way, step))
                def _():
                    going[side, step, :, span] = product(owner(way, step), piece).astype(
                        going.dtype
                    )

                    @pl.when(helps(way))
                    def _():
                        going[side, step, :, span] = (
                            going[side, step, :, span].astype(jnp.float32)
                            + far_product(owner(way, step), piece)
                        ).astype(going.dtype)

                    @pl.when(sum_receives(way, step))
                    def _():
                        sum_copy(way, step, piece).wait_recv()
                        going[side, step, :, span] = (
                            going[side, step, :, span].astype(jnp.float32)
                            + landed[side, step, :, span].astype(jnp.float32)
                        ).astype(going.dtype)

                    sum_copy(way, step, piece).start()

    for piece in range(halves):
        span = slice(piece * cols, (piece + 1) * cols)
        total_ref[:, span] = product(me, piece).astype(going.dtype).astype(jnp.float32)
    for piece in range(halves):
        span = slice(piece * cols, (piece + 1) * cols)
        for way in (-1, 1):
            side = (way + 1) // 2
            last = n - 1 - me if way == 1 else me

            @pl.when(helps(way))
            def _():
                total_ref[:, span] += far_product(me, piece)

            @pl.when(me > 1 if way == 1 else me < n - 2)
            def _():
                sum_copy(way, last, piece).wait_recv()
                total_ref[:, span] += landed[side, last, :, span].astype(jnp.float32)

        out_ref[0, :, span] = (
            total_ref[:, span] * table_ref[2, pl.ds(level, 1), span]
        ).astype(out_ref.dtype)

    @pl.loop(0, n - 1)
    def _(step):
        for piece in range(halves):
            for way in (-1, 1):

                @pl.when(sum_sends(way, step))
                def _():
                    sum_copy(way, step, piece).wait_send()

    @pl.loop(0, n)
    def _(block):
        for ahead in range(1, tracts):

            @pl.when(tract + ahead < tracts)
            def _():
                kv_copy(ahead, block).wait_send()

    @pl.loop(0, n - 1)
    def _(step):
        for piece in range(pieces):
            for way in (-1, 1):

                @pl.when(sends(way, step))
                def _():
                    copy(way, step, piece).wait_send()

    @pl.when(ends)
    def _():
        to_helper().wait_send()
        att_copy().wait_send()

    @pl.when(helper)
    def _():
        for by in range(1, chips):
            to_chip(by).wait_send()
        for by in range(chips):
            to_partner(by).wait_send()


def ring_body(frames, levels, visible, w_qkv, w_out, modulation):
    n, tracts = lax.axis_size("head"), lax.axis_size("tract")
    reps = lax.axis_size("rep")
    rows, width = frames.shape[1:]
    cols = w_qkv.shape[2]
    heads_here = cols // HD
    pieces = max(1, rows // 32)
    halves = 4 if width % 512 == 0 else 2
    vmem = pl.BlockSpec(memory_space=pltpu.VMEM)
    hbm = pl.BlockSpec(memory_space=pltpu.HBM)
    smem = pl.BlockSpec(memory_space=pltpu.SMEM)
    half = jnp.bfloat16
    dma = pltpu.SemaphoreType.DMA
    return pl.pallas_call(
        functools.partial(sublayer_kernel, n, tracts, reps, pieces, halves),
        out_shape=jax.ShapeDtypeStruct(frames.shape, frames.dtype),
        in_specs=[hbm, smem, smem, hbm, hbm, vmem],
        out_specs=vmem,
        scratch_shapes=[
            pltpu.VMEM((n, rows, width), half),
            pltpu.VMEM((3, width, cols), half),
            pltpu.VMEM(w_out.shape, half),
            pltpu.VMEM((n, rows, cols), half),
            pltpu.VMEM((n, 2, rows, cols), half),
            pltpu.VMEM((max(1, tracts - 1), n, 2, rows, cols), half),
            pltpu.VMEM((n, rows, cols), half),
            pltpu.VMEM((heads_here, n * rows, 1), jnp.float32),
            pltpu.VMEM((heads_here, n * rows, 1), jnp.float32),
            pltpu.VMEM((heads_here, n * rows, HD), jnp.float32),
            pltpu.VMEM((2, n - 1, rows, width), half),
            pltpu.VMEM((2, n - 1, rows, width), half),
            pltpu.VMEM((rows, width), jnp.float32),
            dma((3,)),
            dma((2, n, pieces)),
            dma((2, n, pieces)),
            dma((tracts, n)),
            dma((tracts, n)),
            dma((2, n, halves)),
            dma((2, n, halves)),
            pltpu.VMEM(w_out.shape, half),
            pltpu.VMEM((n, rows, cols), half),
            dma((tracts * reps + 1,)),
            dma((tracts * reps + 1,)),
        ],
        compiler_params=pltpu.CompilerParams(
            collective_id=0, has_side_effects=True, vmem_limit_bytes=GRANT
        ),
    )(
        frames,
        levels,
        visible,
        jnp.transpose(w_qkv, (1, 0, 2)),
        w_out,
        jnp.transpose(modulation, (1, 0, 2)),
    )


def line_kernel(
    n,
    tracts,
    reps,
    pieces,
    near,
    x_ref,
    level_ref,
    visible_ref,
    w_hbm,
    out_hbm,
    table_hbm,
    out_ref,
    table_ref,
    gate_ref,
    raw,
    got,
    wq_ref,
    w_far,
    wo_ref,
    acc_ref,
    q_ref,
    kv_ref,
    kv_in,
    part_ref,
    part_in,
    att_ref,
    peak_ref,
    sum_ref,
    mix_ref,
    att_all,
    out_part,
    out_in,
    load_sem,
    wo_sem,
    g_send,
    g_recv,
    f_send,
    f_recv,
    p_send,
    p_recv,
    kv_send,
    kv_recv,
    wo_send,
    wo_recv,
    z_send,
    z_recv,
    a_send,
    a_recv,
    b_recv,
    o_send,
    o_recv,
):
    me, tract, rep = lax.axis_index("head"), lax.axis_index("tract"), lax.axis_index("rep")
    rows, width = x_ref.shape[1:]
    deep = width // pieces
    low = me < 2
    sign = jnp.where(low, 1, -1)
    base = jnp.where(low, 0, n - 1)
    is_end = (me == 0) | (me == n - 1)
    is_helper = (me == 1) | (me == n - 2)
    inner, outer = {"head": me + sign}, {"head": me - sign}

    def blk(r):
        return base + sign * r

    core, wide = tract % 2, tracts // 2
    chips = wide * reps
    seats = chips * 2
    chip = rep * wide + tract // 2
    seat = chip * 2 + core
    partner = {"tract": tract + 1 - 2 * core}

    def chip_at(by):
        return lax.rem(chip + by, chips)

    def place(which, side):
        return {"rep": which // wide, "tract": lax.rem(which, wide) * 2 + side}

    across = [
        chip,
        rep * wide + 1 - lax.rem(chip, wide),
        (1 - rep) * wide + lax.rem(chip, wide),
        (1 - rep) * wide + 1 - lax.rem(chip, wide),
    ]
    along_x, along_y = place(across[1], core), place(across[2], core)
    others = [(by, side) for by in (1, 2, 3) for side in (0, 1)] + [(0, 1)]

    def seat_of(by, side):
        return across[(3, 1, 2)[by - 1] if by else 0], core if side == 0 else 1 - core


    own_load = pltpu.make_async_copy(x_ref.at[0], raw, load_sem.at[0])
    own_load.start()
    table_load = pltpu.make_async_copy(table_hbm, table_ref, load_sem.at[1])
    table_load.start()
    cols_out = width // seats
    units = wo_ref.shape[1]
    cuts, unit = units // 2, cols_out // units

    def wo_load(k):
        start = pl.multiple_of(seat * cols_out + k * unit, 128)
        src = out_hbm.at[:, pl.ds(start, unit)]
        return pltpu.make_async_copy(src, wo_ref.at[me, k], wo_sem.at[k])

    def wo_loaded():
        for k in range(units):
            wo_load(k).wait()

    wq_load = pltpu.make_async_copy(w_hbm, wq_ref, load_sem.at[2])
    wq_load.start()

    for k in range(units):
        wo_load(k).start()

    barrier = pltpu.get_barrier_semaphore()
    for ahead in range(1, n):
        other = lax.rem(me + ahead, n)
        pl.semaphore_signal(barrier, inc=1, device_id={"head": other}, device_id_type=MESH)
    for other in others:
        target = place(*seat_of(*other))
        pl.semaphore_signal(barrier, inc=1, device_id=target, device_id_type=MESH)

    level = level_ref[0]

    def style(kind, start):
        return table_ref[kind, pl.ds(level, 1), start : start + deep]

    def remote(src, dst, send, recv, target):
        return pltpu.make_async_remote_copy(
            src_ref=src,
            dst_ref=dst,
            send_sem=send,
            recv_sem=recv,
            device_id=target,
            device_id_type=MESH,
        )

    parts = g_recv.shape[2]
    part_rows = rows // parts

    def tok(way, r, p, part):
        b = blk(r)
        ref = got.at[b, p, pl.ds(part * part_rows, part_rows)]
        target = inner if way == 0 else outer
        return remote(ref, ref, g_send.at[way, b], g_recv.at[b, p, part], target)

    def tok_take(way, r, p, onward):
        for part in range(parts):
            tok(way, r, p, part).wait_recv()

            @pl.when(onward)
            def _():
                tok(way, r, p, part).start()

    def tok_sent(way, r, count):
        b = blk(r)
        ref = got.at[b, pl.ds(0, count)]
        target = inner if way == 0 else outer
        remote(ref, ref, g_send.at[way, b], g_recv.at[b, 0, 0], target).wait_send()

    far_rows = w_far.shape[1] // seats
    far_base = near * deep

    def far_span(which, side):
        start = (which * 2 + side) * far_rows
        return pl.ds(pl.multiple_of(start, far_rows), far_rows)

    def far_first(kind):
        start = far_base + seat * far_rows
        src = w_hbm.at[kind, pl.ds(pl.multiple_of(start, far_rows), far_rows)]
        dst = w_far.at[kind, far_span(chip, core)]
        return remote(src, dst, f_send.at[0], f_recv.at[0, kind], inner)

    def far_move(slot, kind, which):
        ref = w_far.at[kind, far_span(which, core)]
        target = along_x if slot == 1 else along_y
        return remote(ref, ref, f_send.at[slot], f_recv.at[slot, kind], target)

    def far_pass(slot, kind, side):
        ref = w_far.at[kind, far_span(across[slot], side)]
        where = chips + slot
        return remote(ref, ref, f_send.at[where], f_recv.at[where, kind], partner)

    def far_relay(kind):
        far_first(kind).wait_recv()
        far_move(1, kind, chip).start()
        far_move(2, kind, chip).start()
        far_pass(0, kind, core).start()

    def far_hand_x(kind):
        far_move(1, kind, across[1]).wait_recv()
        far_move(3, kind, across[1]).start()
        far_pass(1, kind, core).start()

    def far_hand_y(kind):
        for slot in (2, 3):
            far_move(slot, kind, across[slot]).wait_recv()
            far_pass(slot, kind, core).start()

    def far_ready(kind):
        for slot in range(chips):
            far_pass(slot, kind, 1 - core).wait_recv()

    def part_copy(r, kind):
        b = blk(r)
        return remote(
            part_ref.at[b, kind],
            part_in.at[b, kind],
            p_send.at[b],
            p_recv.at[b, kind],
            outer,
        )

    def far_part(rs, kinds):
        for kind in kinds:
            total = None
            for p in range(near, pieces):
                lhs = jnp.concatenate([got[blk(r), p] for r in rs], axis=0)
                span = slice((p - near) * deep, (p - near + 1) * deep)
                made = jnp.dot(lhs, w_far[kind, span], preferred_element_type=jnp.float32)
                total = made if total is None else total + made
            total = total.astype(part_ref.dtype)
            for i, r in enumerate(rs):
                part_ref[blk(r), kind] = total[i * rows : (i + 1) * rows]
        for r in rs:
            for kind in kinds:
                part_copy(r, kind).start()

    halves = wo_recv.shape[2]

    def wo_copy(way, r, cut, half):
        b = blk(r)
        ref = wo_ref.at[b, cut * halves + half]
        target = inner if way == 0 else outer
        return remote(ref, ref, wo_send.at[way, b], wo_recv.at[b, cut, half], target)

    def wo_start(way, r, which):
        for cut in which:
            for half in range(halves):
                wo_copy(way, r, cut, half).start()

    along = [(0, r, cut) for cut in range(cuts) for r in (1, 0)]
    back = [(1, r, cut) for cut in range(cuts) for r in (2, 3)]
    early = 3

    def wo_next(way, r, cut):
        for half in range(halves):
            if r != 1:
                wo_copy(way, r, cut, half).wait_recv()
            wo_copy(way, r, cut, half).start()

    def wo_moves(*moves):
        @pl.when(is_helper)
        def _():
            for move in moves:
                wo_next(*move)

    def kv_near(b):
        ref, slot = kv_ref.at[b], kv_in.at[0, b]
        return remote(ref, slot, kv_send.at[0], kv_recv.at[0], partner)

    def kv_far(b):
        ref, slot = kv_ref.at[b], kv_in.at[1, b]
        return remote(ref, slot, kv_send.at[1], kv_recv.at[1], along_x)

    def kv_cross(b):
        at = 2 * (1 - core)
        ref, slot = kv_ref.at[b], kv_in.at[at, b]
        target = place(across[1], 1 - core)
        return remote(ref, slot, kv_send.at[2], kv_recv.at[at], target)

    def kv_slot(slot):
        return remote(kv_ref, kv_in.at[slot], kv_send.at[slot], kv_recv.at[slot], partner)

    def accumulate(rs, p):
        lhs = jnp.concatenate([got[blk(r), p] for r in rs], axis=0)
        span = pl.ds(pl.multiple_of(p * deep, deep), deep)
        for kind in range(3):
            made = jnp.dot(lhs, wq_ref[kind, span], preferred_element_type=jnp.float32)
            for i, r in enumerate(rs):
                acc_ref[blk(r), kind] += made[i * rows : (i + 1) * rows]

    def settle(r, kinds, extra=False):
        b = blk(r)
        for kind in kinds:
            made = acc_ref[b, kind]
            if extra:
                made = made + part_in[b, kind].astype(jnp.float32)
            made = made.astype(q_ref.dtype)
            if kind == 0:
                q_ref[b] = made
            else:
                kv_ref[b, kind - 1] = made

    def share(r):
        @pl.when(tract < 2)
        def _():
            kv_far(blk(r)).start()
            kv_cross(blk(r)).start()

        @pl.when(core == 0)
        def _():
            kv_near(blk(r)).start()

    own_load.wait()
    power = jnp.zeros((rows, 1), jnp.float32)
    for p in range(pieces):
        tokens = raw[:, p * deep : (p + 1) * deep].astype(jnp.float32)
        power += jnp.sum(tokens * tokens, axis=-1, keepdims=True)
    table_load.wait()
    factor = lax.rsqrt(power * (1.0 / width) + 1e-06)
    pl.semaphore_wait(barrier, n - 1 + len(others))

    @pl.when(is_end)
    def _():
        for kind in (1, 2):
            far_first(kind).start()

    def send_own(p):
        @pl.when(is_end)
        def _():
            for part in range(parts):
                tok(0, 0, p, part).start()
            if p == 0:
                far_first(0).start()

        @pl.when(is_helper)
        def _():
            for part in range(parts):
                tok(0, 1, p, part).start()
                if p < near:
                    tok(1, 1, p, part).start()

    for p in range(pieces):
        tokens = raw[:, p * deep : (p + 1) * deep].astype(jnp.float32)
        shaped = tokens * factor * (1.0 + style(1, p * deep)) + style(0, p * deep)
        got[me, p] = shaped.astype(got.dtype)
        if p:
            send_own(p - 1)
    send_own(pieces - 1)
    acc_ref[...] = jnp.zeros_like(acc_ref)
    gate_ref[...] = table_ref[2, pl.ds(level, 1), :]

    @pl.when(is_end)
    def _():
        wq_load.wait()
        @pl.loop(0, pieces)
        def _(p):
            accumulate((0,), p)

        wo_loaded()
        wo_start(0, 0, range(cuts))

        settle(0, (1, 2, 0))
        share(0)
        for r in (1, 2):

            @pl.loop(0, near)
            def _(p):
                tok_take(0, r, p, False)
                accumulate((r,), p)

        for r in (1, 2):
            for kind in (1, 2):
                part_copy(r, kind).wait_recv()
            settle(r, (1, 2), True)
            share(r)

        @pl.loop(0, near)
        def _(p):
            tok_take(0, 3, p, False)
            accumulate((3,), p)

        for kind in (1, 2):
            part_copy(3, kind).wait_recv()
        settle(3, (1, 2), True)
        share(3)
        for r in (1, 2, 3):
            part_copy(r, 0).wait_recv()
            settle(r, (0,), True)

    @pl.when(is_helper)
    def _():
        def pass_on(p):
            tok_take(0, 0, p, True)
            accumulate((0,), p)

        wq_load.wait()
        @pl.loop(0, pieces)
        def _(p):
            tok_take(1, 2, p, p < near)
            accumulate((1, 2), p)
            for at, kind in ((1, 1), (3, 2), (7, 0)):

                @pl.when(p == at)
                def _():
                    far_relay(kind)

            @pl.when(p == near)
            def _():
                wo_loaded()
                wo_start(1, 1, range(cuts - 1))

            for at, kind in ((4, 1), (6, 2)):

                @pl.when(p == at)
                def _():
                    far_hand_x(kind)

            @pl.when(p >= pieces - 2)
            def _():
                pass_on(p - (pieces - 2))

        settle(1, (1, 2, 0))
        share(1)
        settle(2, (1, 2, 0))
        share(2)

        @pl.loop(0, pieces)
        def _(p):
            @pl.when(p + 2 < pieces)
            def _():
                pass_on(p + 2)

            tok_take(1, 3, p, p < near)

            @pl.when(p == pieces - 1)
            def _():
                far_part((3,), (1, 2))

            accumulate((3,), p)

            @pl.when(p == 1)
            def _():
                far_hand_y(1)

            @pl.when(p == 2)
            def _():
                far_hand_x(0)
                far_ready(1)
                far_part((1, 2), (1,))

            @pl.when(p == 3)
            def _():
                far_hand_y(2)

            @pl.when(p == 4)
            def _():
                far_ready(2)
                far_part((1, 2), (2,))
                wo_start(1, 1, (cuts - 1,))

            @pl.when(p == 5)
            def _():
                settle(0, (1, 2, 0))
                share(0)

            @pl.when(p == 6)
            def _():
                wo_next(*along[0])

            @pl.when(p == 5)
            def _():
                far_hand_y(0)

        settle(3, (1, 2))
        share(3)
        far_ready(0)
        far_part((1, 2, 3), (0,))
        settle(3, (0,))
        wo_next(*along[1])

        @pl.when(tract >= 2)
        def _():
            for move in along[2:early]:
                wo_next(*move)


    tokens_here = n * rows
    heads_here = q_ref.shape[2] // HD
    scale = HD ** (-0.5)

    def attend(source, bias):
        for head in range(heads_here):
            lanes = slice(head * HD, (head + 1) * HD)
            queries = q_ref[:, :, lanes].reshape(tokens_here, HD)
            keys = source[:, 0, :, lanes].reshape(tokens_here, HD)
            values = source[:, 1, :, lanes].reshape(tokens_here, HD)
            scores = (
                lax.dot_general(
                    keys, queries, (((1,), (1,)), ((), ())), preferred_element_type=jnp.float32
                )
                * scale
            )
            if bias is not None:
                scores = scores + bias
            peak = jnp.max(scores, axis=0, keepdims=True)
            if bias is not None:
                old = peak_ref[head]
                peak = jnp.maximum(old, peak)
            probs = jnp.exp(scores - peak)
            row_sum = jnp.sum(probs, axis=0, keepdims=True)
            weighted = lax.dot_general(
                values,
                probs.astype(jnp.bfloat16),
                (((0,), (0,)), ((), ())),
                preferred_element_type=jnp.float32,
            )
            if bias is not None:
                rescale = jnp.exp(old - peak)
                row_sum += sum_ref[head] * rescale
                weighted += mix_ref[head] * rescale
            peak_ref[head] = peak
            sum_ref[head] = row_sum
            mix_ref[head] = weighted

    attend(kv_ref, None)

    for ahead in (1, 2, 3):
        if ahead == 2:

            @pl.when(is_helper & (tract >= 2))
            def _():
                wo_next(*back[0])

        @pl.when(tract >= ahead)
        def _():
            kv_slot(ahead - 1).wait_recv()
            seen = visible_ref[0, lax.max(tract - ahead, 0)] > 0
            attend(kv_in.at[ahead - 1], jnp.where(seen, 0.0, -1e30))

    for head in range(heads_here):
        attended = jnp.transpose(mix_ref[head] / sum_ref[head]).astype(jnp.bfloat16)
        att_ref[:, :, head * HD : (head + 1) * HD] = attended.reshape(n, rows, HD)

    def att_line(other, source):
        return remote(
            att_ref.at[other],
            att_all.at[seat, source],
            z_send.at[other],
            z_recv.at[source],
            {"head": other},
        )

    line = [blk(jnp.where(is_end, end, help)) for end, help in ((0, 1), (1, 2), (2, 0), (3, 3))]
    for other in line[1:]:
        att_line(other, me).start()
    att_all[seat, me] = att_ref[me]

    def att_chip(by, z, which):
        ref = att_all.at[which * 2 + core] if z is None else att_all.at[which * 2 + core, z]
        at = a_recv.at[by, 0 if z is None else z]
        return remote(ref, ref, a_send.at[by], at, place(seat_of(by, 0)[0], core))

    def att_pass(by, z, side):
        owner = seat_of(by, 0)[0] * 2 + side
        ref = att_all.at[owner] if z is None else att_all.at[owner, z]
        return remote(ref, ref, a_send.at[chips + by], b_recv.at[by], partner)

    @pl.when(is_helper)
    def _():
        @pl.when(tract < 2)
        def _():
            for move in along[2:early]:
                wo_next(*move)

        for move in along[early:]:
            wo_next(*move)

    for ahead, z in enumerate(line):
        if ahead:
            att_line(z, z).wait_recv()
        for by in range(1, chips):
            att_chip(by, z, chip).start()
        att_pass(0, z, core).start()
        for late, used in ((0, tract < 2), (1, tract >= 2)):

            @pl.when(is_helper & used)
            def _():
                for move in back[ahead + late : min(ahead + late + 1, 3)]:
                    wo_next(*move)

    for ahead, z in enumerate(line):
        for by in range(1, chips):
            att_chip(by, z, seat_of(by, 0)[0]).wait_recv()
            att_pass(by, z, core).start()
        if ahead == 2:
            wo_moves(*back[3:4])
    wo_moves(*back[4:5])
    for by in range(chips):
        att_pass(by, None, 1 - core).wait_recv()

    spans = [(k, 2) for k in range(0, units - 2, 2)] + [(units - 2, 1), (units - 1, 1)]

    def out_copy(by, side, source, at):
        which, lane = seat_of(by, side)
        span = pl.ds(*spans[at])
        return remote(
            out_part.at[which * 2 + lane, span],
            out_in.at[source, span],
            o_send.at[which * 2 + lane],
            o_recv.at[source, at],
            place(which, lane),
        )

    heads_wide = wo_ref.shape[2]

    def finish(ref, source, at):
        first, count = spans[at]
        for k in range(first, first + count):
            span = pl.ds(pl.multiple_of(source * cols_out + k * unit, 128), unit)
            done = ref[source, k].astype(jnp.float32) * gate_ref[:, span]
            out_ref[0, :, span] = done.astype(out_ref.dtype)

    for at, (first, count) in enumerate(spans):

        @pl.when(is_end)
        def _():
            for r in (1, 2, 3):
                for k in range(first, first + count):
                    wo_copy(0, r, k // halves, k % halves).wait_recv()

        total = None
        for z in range(n):
            lhs = att_all[:, z].reshape(seats * rows, heads_wide)
            rhs = jnp.concatenate([wo_ref[z, k] for k in range(first, first + count)], axis=1)
            made = jnp.dot(lhs, rhs, preferred_element_type=jnp.float32)
            total = made if total is None else total + made
        total = total.astype(out_part.dtype).reshape(seats, rows, count * unit)
        for k in range(count):
            out_part[:, first + k] = total[:, :, k * unit : (k + 1) * unit]
        for by, side in others:
            out_copy(by, side, seat, at).start()
        if at == max(0, len(spans) - 3):
            wo_moves(*back[5:])

    for at in range(len(spans)):
        finish(out_part, seat, at)
        for by, side in reversed(others):
            which, lane = seat_of(by, side)
            source = which * 2 + lane
            out_copy(by, side, source, at).wait_recv()
            finish(out_in, source, at)

    for by, side in others:
        which, lane = seat_of(by, side)
        to = which * 2 + lane
        sems = o_send.at[to], o_recv.at[seat, 0]
        remote(out_part.at[to], out_in.at[seat], *sems, partner).wait_send()
    for by in range(chips):
        if by:
            att_chip(by, None, chip).wait_send()
        att_pass(by, None, core).wait_send()
    for ahead in range(1, n):
        att_line(lax.rem(me + ahead, n), me).wait_send()
    for slot, used in ((0, core == 0), (1, tract < 2), (2, tract < 2)):

        @pl.when(used)
        def _():
            kv_slot(slot).wait_send()

    def far_sent(where, which):
        ref = w_far.at[:, far_span(which, core)]
        remote(ref, ref, f_send.at[where], f_recv.at[where, 0], partner).wait_send()

    def wo_sent(way, r):
        ref = wo_ref.at[blk(r)]
        sems = wo_send.at[way, blk(r)], wo_recv.at[blk(r), 0, 0]
        remote(ref, ref, *sems, partner).wait_send()

    @pl.when(is_end)
    def _():
        far_sent(0, chip)
        tok_sent(0, 0, pieces)
        wo_sent(0, 0)

    @pl.when(is_helper)
    def _():
        for slot in range(chips):
            if slot:
                far_sent(slot, across[1] if slot == 3 else chip)
            far_sent(chips + slot, across[slot])
        for r in (1, 2, 3):
            ref = part_ref.at[blk(r)]
            sems = p_send.at[blk(r)], p_recv.at[blk(r), 0]
            remote(ref, ref, *sems, partner).wait_send()
            tok_sent(1, r, near)
            wo_sent(1, r)
        for r in (0, 1):
            tok_sent(0, r, pieces)
            wo_sent(0, r)


PIECES = 8
NEAR = 4


def fits_line(n, tracts, reps, frames, w_out):
    rows, width = frames.shape[1:]
    seats = tracts * reps
    far = (PIECES - NEAR) * (width // PIECES)
    return (
        n == 4
        and (tracts, reps) == (4, 2)
        and rows % 16 == 0
        and width % (PIECES * 128) == 0
        and width % (seats * 256) == 0
        and far % (seats * 16) == 0
        and w_out.shape[0] % 32 == 0
    )


def line_body(frames, levels, visible, w_qkv, w_out, modulation):
    n, tracts = lax.axis_size("head"), lax.axis_size("tract")
    reps = lax.axis_size("rep")
    rows, width = frames.shape[1:]
    cols = w_qkv.shape[2]
    heads_here = cols // HD
    seats = tracts * reps
    chips = seats // 2
    deep = width // PIECES
    units = width // seats // 128
    vmem = pl.BlockSpec(memory_space=pltpu.VMEM)
    hbm = pl.BlockSpec(memory_space=pltpu.HBM)
    smem = pl.BlockSpec(memory_space=pltpu.SMEM)
    half = jnp.bfloat16
    dma = pltpu.SemaphoreType.DMA
    return pl.pallas_call(
        functools.partial(line_kernel, n, tracts, reps, PIECES, NEAR),
        out_shape=pltpu.VMEM(frames.shape, frames.dtype),
        in_specs=[hbm, smem, smem, hbm, hbm, hbm],
        out_specs=vmem,
        scratch_shapes=[
            pltpu.VMEM((3, *modulation.shape[::2]), jnp.float32),
            pltpu.VMEM((1, width), jnp.float32),
            pltpu.VMEM((rows, width), half),
            pltpu.VMEM((n, PIECES, rows, deep), half),
            pltpu.VMEM((3, width, cols), half),
            pltpu.VMEM((3, (PIECES - NEAR) * deep, cols), half),
            pltpu.VMEM((n, units, w_out.shape[0], 128), half),
            pltpu.VMEM((n, 3, rows, cols), jnp.float32),
            pltpu.VMEM((n, rows, cols), half),
            pltpu.VMEM((n, 2, rows, cols), half),
            pltpu.VMEM((max(1, tracts - 1), n, 2, rows, cols), half),
            pltpu.VMEM((n, 3, rows, cols), half),
            pltpu.VMEM((n, 3, rows, cols), half),
            pltpu.VMEM((n, rows, cols), half),
            pltpu.VMEM((heads_here, 1, n * rows), jnp.float32),
            pltpu.VMEM((heads_here, 1, n * rows), jnp.float32),
            pltpu.VMEM((heads_here, HD, n * rows), jnp.float32),
            pltpu.VMEM((seats, n, rows, cols), half),
            pltpu.VMEM((seats, units, rows, 128), half),
            pltpu.VMEM((seats, units, rows, 128), half),
            dma((3,)),
            dma((units,)),
            dma((2, n)),
            dma((n, PIECES, 2)),
            dma((2 * chips,)),
            dma((2 * chips, 3)),
            dma((n,)),
            dma((n, 3)),
            dma((3,)),
            dma((3,)),
            dma((2, n)),
            dma((n, units // 2, 2)),
            dma((n,)),
            dma((n,)),
            dma((2 * chips,)),
            dma((chips, n)),
            dma((chips,)),
            dma((seats,)),
            dma((seats, units // 2 + 1)),
        ],
        compiler_params=pltpu.CompilerParams(
            collective_id=0, has_side_effects=True, vmem_limit_bytes=GRANT
        ),
    )(
        frames,
        levels,
        visible,
        jnp.transpose(w_qkv, (1, 0, 2)),
        w_out,
        jnp.transpose(modulation, (1, 0, 2)),
    )


def body(frames, levels, visible, w_qkv, w_out, modulation):
    n, tracts = lax.axis_size("head"), lax.axis_size("tract")
    reps = lax.axis_size("rep")
    line = fits_line(n, tracts, reps, frames, w_out)
    chosen = line_body if line else ring_body
    return chosen(frames, levels, visible, w_qkv, w_out, modulation)


def solution(mesh):
    placed = (
        P(("rep", "tract"), "head", None),
        P(("rep", "tract")),
        P(("rep", "tract"), None),
        P(None, None, "head"),
        P("head", None),
        P(),
    )
    return jax.shard_map(
        body,
        mesh=mesh,
        in_specs=placed,
        out_specs=P(("rep", "tract"), "head", None),
        check_vma=False,
    )
```

```python
import functools

import jax
import jax.numpy as jnp
from jax import lax
from jax.experimental import pallas as pl
from jax.experimental.pallas import tpu as pltpu
from jax.sharding import PartitionSpec as P

HD = 128
GRANT = 60 * 1024 * 1024
MESH = pl.DeviceIdType.MESH


def meet(n, me, tracts, tract, others):
    barrier = pltpu.get_barrier_semaphore()
    for other in (lax.rem(me + 1, n), lax.rem(me + n - 1, n)):
        pl.semaphore_signal(barrier, inc=1, device_id={"head": other}, device_id_type=MESH)
    for ahead in range(1, tracts):
        other = lax.rem(tract + ahead, tracts)
        pl.semaphore_signal(barrier, inc=1, device_id={"tract": other}, device_id_type=MESH)
    for other in others:
        pl.semaphore_signal(barrier, inc=1, device_id=other, device_id_type=MESH)
    pl.semaphore_wait(barrier, 1 + tracts + len(others))


def sublayer_kernel(
    n,
    tracts,
    reps,
    pieces,
    halves,
    x_ref,
    level_ref,
    visible_ref,
    w_hbm,
    out_hbm,
    table_ref,
    out_ref,
    got,
    wq_ref,
    w_ref,
    q_ref,
    kv_ref,
    kv_in,
    att_ref,
    peak_ref,
    sum_ref,
    acc_ref,
    going,
    landed,
    total_ref,
    load_sem,
    g_send,
    g_recv,
    kv_send,
    kv_recv,
    s_send,
    s_recv,
    w_far,
    att_far,
    f_send,
    f_recv,
):
    me, tract = lax.axis_index("head"), lax.axis_index("tract")
    own = pltpu.make_async_copy(x_ref.at[0], got.at[me], load_sem.at[0])
    own.start()
    load = pltpu.make_async_copy(w_hbm, wq_ref, load_sem.at[1])
    load.start()
    load_out = pltpu.make_async_copy(out_hbm, w_ref, load_sem.at[2])
    load_out.start()
    core, wide = tract % 2, tracts // 2
    chips = wide * reps
    chip = lax.axis_index("rep") * wide + tract // 2
    slab = w_ref.shape[0] // (2 * chips)
    helper = (me == 1) | (me == n - 2)
    ends = (me == 0) | (me == n - 1)

    def seat(by):
        other = lax.rem(chip + by, chips)
        return {"rep": other // wide, "tract": lax.rem(other, wide) * 2 + core}

    def slab_of(which, side):
        start = pl.multiple_of((which * 2 + side) * slab, slab)
        return pl.ds(start, slab)

    def far_copy(kind, span, target, source=None):
        return pltpu.make_async_remote_copy(
            src_ref=(w_far if source is None else source).at[span],
            dst_ref=w_far.at[span],
            send_sem=f_send.at[kind],
            recv_sem=f_recv.at[kind],
            device_id=target,
            device_id_type=MESH,
        )

    inward = {"head": jnp.where(me == 0, 1, n - 2)}
    partner = {"tract": tract + 1 - 2 * core}
    mine = slab_of(chip, core)

    def to_helper():
        return far_copy(0, mine, inward, out_hbm)

    def to_chip(by):
        return far_copy(by, mine, seat(by))

    def from_chip(by):
        return far_copy(by, slab_of(lax.rem(chip + chips - by, chips), core), seat(by))

    def to_partner(by):
        span = slab_of(lax.rem(chip + chips - by, chips), core)
        return far_copy(chips + by, span, partner)

    def from_partner(by):
        span = slab_of(lax.rem(chip + chips - by, chips), 1 - core)
        return far_copy(chips + by, span, partner)

    def att_copy():
        return pltpu.make_async_remote_copy(
            src_ref=att_ref,
            dst_ref=att_far,
            send_sem=f_send.at[2 * chips],
            recv_sem=f_recv.at[2 * chips],
            device_id=inward,
            device_id_type=MESH,
        )

    meet(n, me, tracts, tract, [seat(by) for by in range(1, chips)])
    level = level_ref[0]

    def style(kind):
        return table_ref[kind, pl.ds(level, 1), :]

    rows, width = x_ref.shape[1:]
    part = rows // pieces

    def copy(way, step, piece, first=False):
        side = (way + 1) // 2
        span = pl.ds(piece * part, part)
        block = me - way * step
        return pltpu.make_async_remote_copy(
            src_ref=(x_ref.at[0] if first else got.at[block]).at[span],
            dst_ref=got.at[block].at[span],
            send_sem=g_send.at[side, step, piece],
            recv_sem=g_recv.at[side, step, piece],
            device_id={"head": me + way},
            device_id_type=MESH,
        )

    def arrival(way, step, piece):
        side = (way + 1) // 2
        span = pl.ds(piece * part, part)
        return pltpu.make_async_remote_copy(
            src_ref=x_ref.at[0].at[span],
            dst_ref=got.at[me - way * (step + 1)].at[span],
            send_sem=g_send.at[side, step, piece],
            recv_sem=g_recv.at[side, step, piece],
            device_id={"head": me - way},
            device_id_type=MESH,
        )

    def sends(way, step):
        block, target = me - way * step, me + way
        return (block >= 0) & (block < n) & (target >= 0) & (target < n) & (step < n - 1)

    def receives(way, step):
        block = me - way * (step + 1)
        return (block >= 0) & (block < n)

    def kv_copy(ahead, block):
        return pltpu.make_async_remote_copy(
            src_ref=kv_ref.at[block],
            dst_ref=kv_in.at[ahead - 1, block],
            send_sem=kv_send.at[ahead - 1, block],
            recv_sem=kv_recv.at[ahead - 1, block],
            device_id={"tract": tract + ahead},
            device_id_type=MESH,
        )

    def project(block):
        tokens = got[block].astype(jnp.float32)
        power = jnp.mean(tokens * tokens, axis=-1, keepdims=True)
        normed = tokens * lax.rsqrt(power + 1e-06)
        shaped = (normed * (1.0 + style(1)) + style(0)).astype(jnp.bfloat16)
        for kind in (1, 2, 0):
            made = jnp.dot(shaped, wq_ref[kind], preferred_element_type=jnp.float32)
            made = made.astype(jnp.bfloat16)
            if kind == 0:
                q_ref[block] = made
            else:
                kv_ref[block, kind - 1] = made
            if kind == 2:
                for ahead in range(1, tracts):

                    @pl.when(tract + ahead < tracts)
                    def _():
                        kv_copy(ahead, block).start()

    for piece in range(pieces):
        for way in (-1, 1):

            @pl.when(sends(way, 0))
            def _():
                copy(way, 0, piece, True).start()

    @pl.when(ends)
    def _():
        to_helper().start()

    own.wait()
    load.wait()
    project(me)

    @pl.loop(0, n - 1)
    def _(step):
        for piece in range(pieces):
            for way in (-1, 1):

                @pl.when(receives(way, step))
                def _():
                    arrival(way, step, piece).wait_recv()

                @pl.when(sends(way, step + 1))
                def _():
                    copy(way, step + 1, piece).start()

        @pl.loop(0, 2)
        def _(side):
            way = 2 * side - 1

            @pl.when(receives(way, step))
            def _():
                project(me - way * (step + 1))

        @pl.when(helper & (step == 0))
        def _():
            to_helper().wait_recv()
            for by in range(1, chips):
                to_chip(by).start()
            to_partner(0).start()

    @pl.when(helper)
    def _():
        for by in range(1, chips):
            from_chip(by).wait_recv()
            to_partner(by).start()

    tokens_here = n * rows
    heads_here = q_ref.shape[2] // HD
    scale = HD ** (-0.5)

    def attend(source, allowed):
        for head in range(heads_here):
            lanes = slice(head * HD, (head + 1) * HD)
            queries = q_ref[:, :, lanes].reshape(tokens_here, HD)
            keys = source[:, 0, :, lanes].reshape(tokens_here, HD)
            values = source[:, 1, :, lanes].reshape(tokens_here, HD)
            scores = (
                lax.dot_general(
                    queries, keys, (((1,), (1,)), ((), ())), preferred_element_type=jnp.float32
                )
                * scale
            )
            if allowed is None:
                peak = jnp.max(scores, axis=1, keepdims=True)
                probs = jnp.exp(scores - peak)
            else:
                scores = jnp.where(allowed, scores, -1e30)
                old = peak_ref[head]
                peak = jnp.maximum(old, jnp.max(scores, axis=1, keepdims=True))
                probs = jnp.where(allowed, jnp.exp(scores - peak), 0.0)
                rescale = jnp.exp(old - peak)
            row_sum = jnp.sum(probs, axis=1, keepdims=True)
            weighted = jnp.dot(
                probs.astype(jnp.bfloat16), values, preferred_element_type=jnp.float32
            )
            if allowed is not None:
                row_sum += sum_ref[head] * rescale
                weighted += acc_ref[head] * rescale
            peak_ref[head] = peak
            sum_ref[head] = row_sum
            acc_ref[head] = weighted

    attend(kv_ref, None)
    for ahead in range(1, tracts):

        @pl.when(tract >= ahead)
        def _():
            @pl.loop(0, n)
            def _(block):
                kv_copy(ahead, block).wait_recv()

            attend(kv_in.at[ahead - 1], visible_ref[0, lax.max(tract - ahead, 0)] > 0)

    for head in range(heads_here):
        attended = (acc_ref[head] / sum_ref[head]).astype(jnp.bfloat16)
        att_ref[:, :, head * HD : (head + 1) * HD] = attended.reshape(n, rows, HD)

    @pl.when(ends)
    def _():
        att_copy().start()

    load_out.wait()

    @pl.when(helper)
    def _():
        for by in range(chips):
            from_partner(by).wait_recv()
        att_copy().wait_recv()

    cols = width // halves

    def sum_copy(way, step, piece):
        side = (way + 1) // 2
        span = pl.ds(piece * cols, cols)
        return pltpu.make_async_remote_copy(
            src_ref=going.at[side, step].at[:, span],
            dst_ref=landed.at[side, step].at[:, span],
            send_sem=s_send.at[side, step, piece],
            recv_sem=s_recv.at[side, step, piece],
            device_id={"head": me + way},
            device_id_type=MESH,
        )

    def product(block, piece):
        return jnp.dot(
            att_ref[block],
            w_ref[:, piece * cols : (piece + 1) * cols],
            preferred_element_type=jnp.float32,
        )

    def far_product(block, piece):
        return jnp.dot(
            att_far[block],
            w_far[:, piece * cols : (piece + 1) * cols],
            preferred_element_type=jnp.float32,
        )

    def helps(way):
        return me == (1 if way == 1 else n - 2)

    def owner(way, step):
        return (n - 1 - step) if way == 1 else step

    def sum_sends(way, step):
        block = owner(way, step)
        return (block > me) & (me > 0) if way == 1 else (block < me) & (me < n - 1)

    def sum_receives(way, step):
        block = owner(way, step)
        return (block >= me) & (me > 1) if way == 1 else (block <= me) & (me < n - 2)

    @pl.loop(0, n - 1)
    def _(tick):
        for piece in range(halves):
            span = slice(piece * cols, (piece + 1) * cols)
            for way in (-1, 1):
                side = (way + 1) // 2
                step = tick - (me if way == 1 else n - 1 - me)
                held = (step >= 0) & (step < n - 1)

                @pl.when(held & sum_sends(way, step))
                def _():
                    going[side, step, :, span] = product(owner(way, step), piece).astype(
                        going.dtype
                    )

                    @pl.when(helps(way))
                    def _():
                        going[side, step, :, span] = (
                            going[side, step, :, span].astype(jnp.float32)
                            + far_product(owner(way, step), piece)
                        ).astype(going.dtype)

                    @pl.when(sum_receives(way, step))
                    def _():
                        sum_copy(way, step, piece).wait_recv()
                        going[side, step, :, span] = (
                            going[side, step, :, span].astype(jnp.float32)
                            + landed[side, step, :, span].astype(jnp.float32)
                        ).astype(going.dtype)

                    sum_copy(way, step, piece).start()

    for piece in range(halves):
        span = slice(piece * cols, (piece + 1) * cols)
        total_ref[:, span] = product(me, piece).astype(going.dtype).astype(jnp.float32)
    for piece in range(halves):
        span = slice(piece * cols, (piece + 1) * cols)
        for way in (-1, 1):
            side = (way + 1) // 2
            last = n - 1 - me if way == 1 else me

            @pl.when(helps(way))
            def _():
                total_ref[:, span] += far_product(me, piece)

            @pl.when(me > 1 if way == 1 else me < n - 2)
            def _():
                sum_copy(way, last, piece).wait_recv()
                total_ref[:, span] += landed[side, last, :, span].astype(jnp.float32)

        out_ref[0, :, span] = (
            total_ref[:, span] * table_ref[2, pl.ds(level, 1), span]
        ).astype(out_ref.dtype)

    @pl.loop(0, n - 1)
    def _(step):
        for piece in range(halves):
            for way in (-1, 1):

                @pl.when(sum_sends(way, step))
                def _():
                    sum_copy(way, step, piece).wait_send()

    @pl.loop(0, n)
    def _(block):
        for ahead in range(1, tracts):

            @pl.when(tract + ahead < tracts)
            def _():
                kv_copy(ahead, block).wait_send()

    @pl.loop(0, n - 1)
    def _(step):
        for piece in range(pieces):
            for way in (-1, 1):

                @pl.when(sends(way, step))
                def _():
                    copy(way, step, piece).wait_send()

    @pl.when(ends)
    def _():
        to_helper().wait_send()
        att_copy().wait_send()

    @pl.when(helper)
    def _():
        for by in range(1, chips):
            to_chip(by).wait_send()
        for by in range(chips):
            to_partner(by).wait_send()


def ring_body(frames, levels, visible, w_qkv, w_out, modulation):
    n, tracts = lax.axis_size("head"), lax.axis_size("tract")
    reps = lax.axis_size("rep")
    rows, width = frames.shape[1:]
    cols = w_qkv.shape[2]
    heads_here = cols // HD
    pieces = max(1, rows // 32)
    halves = 4 if width % 512 == 0 else 2
    vmem = pl.BlockSpec(memory_space=pltpu.VMEM)
    hbm = pl.BlockSpec(memory_space=pltpu.HBM)
    smem = pl.BlockSpec(memory_space=pltpu.SMEM)
    half = jnp.bfloat16
    dma = pltpu.SemaphoreType.DMA
    return pl.pallas_call(
        functools.partial(sublayer_kernel, n, tracts, reps, pieces, halves),
        out_shape=jax.ShapeDtypeStruct(frames.shape, frames.dtype),
        in_specs=[hbm, smem, smem, hbm, hbm, vmem],
        out_specs=vmem,
        scratch_shapes=[
            pltpu.VMEM((n, rows, width), half),
            pltpu.VMEM((3, width, cols), half),
            pltpu.VMEM(w_out.shape, half),
            pltpu.VMEM((n, rows, cols), half),
            pltpu.VMEM((n, 2, rows, cols), half),
            pltpu.VMEM((max(1, tracts - 1), n, 2, rows, cols), half),
            pltpu.VMEM((n, rows, cols), half),
            pltpu.VMEM((heads_here, n * rows, 1), jnp.float32),
            pltpu.VMEM((heads_here, n * rows, 1), jnp.float32),
            pltpu.VMEM((heads_here, n * rows, HD), jnp.float32),
            pltpu.VMEM((2, n - 1, rows, width), half),
            pltpu.VMEM((2, n - 1, rows, width), half),
            pltpu.VMEM((rows, width), jnp.float32),
            dma((3,)),
            dma((2, n, pieces)),
            dma((2, n, pieces)),
            dma((tracts, n)),
            dma((tracts, n)),
            dma((2, n, halves)),
            dma((2, n, halves)),
            pltpu.VMEM(w_out.shape, half),
            pltpu.VMEM((n, rows, cols), half),
            dma((tracts * reps + 1,)),
            dma((tracts * reps + 1,)),
        ],
        compiler_params=pltpu.CompilerParams(
            collective_id=0, has_side_effects=True, vmem_limit_bytes=GRANT
        ),
    )(
        frames,
        levels,
        visible,
        jnp.transpose(w_qkv, (1, 0, 2)),
        w_out,
        jnp.transpose(modulation, (1, 0, 2)),
    )


def line_kernel(
    n,
    tracts,
    reps,
    pieces,
    near,
    x_ref,
    level_ref,
    visible_ref,
    w_hbm,
    out_hbm,
    table_hbm,
    out_ref,
    table_ref,
    gate_ref,
    raw,
    got,
    wq_ref,
    w_far,
    wo_ref,
    acc_ref,
    q_ref,
    kv_ref,
    kv_in,
    part_ref,
    part_in,
    att_ref,
    peak_ref,
    sum_ref,
    mix_ref,
    att_all,
    out_part,
    out_in,
    load_sem,
    wo_sem,
    g_send,
    g_recv,
    f_send,
    f_recv,
    p_send,
    p_recv,
    kv_send,
    kv_recv,
    wo_send,
    wo_recv,
    z_send,
    z_recv,
    a_send,
    a_recv,
    b_recv,
    o_send,
    o_recv,
):
    me, tract, rep = lax.axis_index("head"), lax.axis_index("tract"), lax.axis_index("rep")
    rows, width = x_ref.shape[1:]
    deep = width // pieces
    low = me < 2
    sign = jnp.where(low, 1, -1)
    base = jnp.where(low, 0, n - 1)
    is_end = (me == 0) | (me == n - 1)
    is_helper = (me == 1) | (me == n - 2)
    inner, outer = {"head": me + sign}, {"head": me - sign}

    def blk(r):
        return base + sign * r

    core, wide = tract % 2, tracts // 2
    chips = wide * reps
    seats = chips * 2
    chip = rep * wide + tract // 2
    seat = chip * 2 + core
    partner = {"tract": tract + 1 - 2 * core}

    def chip_at(by):
        return lax.rem(chip + by, chips)

    def place(which, side):
        return {"rep": which // wide, "tract": lax.rem(which, wide) * 2 + side}

    across = [
        chip,
        rep * wide + 1 - lax.rem(chip, wide),
        (1 - rep) * wide + lax.rem(chip, wide),
        (1 - rep) * wide + 1 - lax.rem(chip, wide),
    ]
    along_x, along_y = place(across[1], core), place(across[2], core)
    others = [(by, side) for by in (1, 2, 3) for side in (0, 1)] + [(0, 1)]

    def seat_of(by, side):
        return across[(3, 1, 2)[by - 1] if by else 0], core if side == 0 else 1 - core


    own_load = pltpu.make_async_copy(x_ref.at[0], raw, load_sem.at[0])
    own_load.start()
    barrier = pltpu.get_barrier_semaphore()
    for ahead in range(1, n):
        other = lax.rem(me + ahead, n)
        pl.semaphore_signal(barrier, inc=1, device_id={"head": other}, device_id_type=MESH)
    for other in others:
        target = place(*seat_of(*other))
        pl.semaphore_signal(barrier, inc=1, device_id=target, device_id_type=MESH)

    table_load = pltpu.make_async_copy(table_hbm, table_ref, load_sem.at[1])
    table_load.start()
    cols_out = width // seats
    units = wo_ref.shape[1]
    cuts, unit = units // 2, cols_out // units

    def wo_load(k):
        start = pl.multiple_of(seat * cols_out + k * unit, 128)
        src = out_hbm.at[:, pl.ds(start, unit)]
        return pltpu.make_async_copy(src, wo_ref.at[me, k], wo_sem.at[k])

    def wo_loaded():
        for k in range(units):
            wo_load(k).wait()

    wq_load = pltpu.make_async_copy(w_hbm, wq_ref, load_sem.at[2])
    wq_load.start()

    for k in range(units):
        wo_load(k).start()

    level = level_ref[0]

    def style(kind, start):
        return table_ref[kind, pl.ds(level, 1), start : start + deep]

    def remote(src, dst, send, recv, target):
        return pltpu.make_async_remote_copy(
            src_ref=src,
            dst_ref=dst,
            send_sem=send,
            recv_sem=recv,
            device_id=target,
            device_id_type=MESH,
        )

    parts = g_recv.shape[2]
    part_rows = rows // parts

    def row_there(way, r, onward):
        if way == 1:
            return r - 1
        return 1 if r == 1 else 2 if onward else 0

    def row_here(r):
        return max(r - 1, 0)

    def tok(way, r, p, part, row):
        b = blk(r)
        ref = got.at[b, p, pl.ds(part * part_rows, part_rows)]
        target = inner if way == 0 else outer
        return remote(ref, ref, g_send.at[way, b], g_recv.at[row, p, part], target)

    def tok_take(way, r, p, onward):
        for part in range(parts):
            tok(way, r, p, part, row_here(r)).wait_recv()
            if onward is not None:

                @pl.when(onward)
                def _():
                    tok(way, r, p, part, row_there(way, r, True)).start()

    def tok_sent(way, r, count):
        b = blk(r)
        ref = got.at[b, pl.ds(0, count)]
        target = inner if way == 0 else outer
        remote(ref, ref, g_send.at[way, b], g_recv.at[0, 0, 0], target).wait_send()

    far_rows = w_far.shape[1] // seats
    far_base = near * deep

    def far_span(which, side):
        start = (which * 2 + side) * far_rows
        return pl.ds(pl.multiple_of(start, far_rows), far_rows)

    def far_first(kind):
        start = far_base + seat * far_rows
        src = w_hbm.at[kind, pl.ds(pl.multiple_of(start, far_rows), far_rows)]
        dst = w_far.at[kind, far_span(chip, core)]
        return remote(src, dst, f_send.at[0], f_recv.at[0, kind], inner)

    def far_move(slot, kind, which):
        ref = w_far.at[kind, far_span(which, core)]
        target = along_x if slot == 1 else along_y
        return remote(ref, ref, f_send.at[slot], f_recv.at[slot, kind], target)

    def far_pass(slot, kind, side):
        ref = w_far.at[kind, far_span(across[slot], side)]
        where = chips + slot
        return remote(ref, ref, f_send.at[where], f_recv.at[where, kind], partner)

    def far_relay(kind):
        far_first(kind).wait_recv()
        far_move(1, kind, chip).start()
        far_move(2, kind, chip).start()
        far_pass(0, kind, core).start()

    def far_hand_x(kind):
        far_move(1, kind, across[1]).wait_recv()
        far_move(3, kind, across[1]).start()
        far_pass(1, kind, core).start()

    def far_hand_y(kind):
        for slot in (2, 3):
            far_move(slot, kind, across[slot]).wait_recv()
            far_pass(slot, kind, core).start()

    def far_ready(kind):
        for slot in range(chips):
            far_pass(slot, kind, 1 - core).wait_recv()

    def part_copy(r, kind):
        b = blk(r)
        return remote(
            part_ref.at[b, kind],
            part_in.at[b, kind],
            p_send.at[b],
            p_recv.at[b, kind],
            outer,
        )

    def far_part(rs, kinds):
        for kind in kinds:
            total = None
            for p in range(near, pieces):
                lhs = jnp.concatenate([got[blk(r), p] for r in rs], axis=0)
                span = slice((p - near) * deep, (p - near + 1) * deep)
                made = jnp.dot(lhs, w_far[kind, span], preferred_element_type=jnp.float32)
                total = made if total is None else total + made
            total = total.astype(part_ref.dtype)
            for i, r in enumerate(rs):
                part_ref[blk(r), kind] = total[i * rows : (i + 1) * rows]
        for r in rs:
            for kind in kinds:
                part_copy(r, kind).start()

    halves = wo_recv.shape[2]

    def wo_copy(way, r, cut, half, row):
        b = blk(r)
        ref = wo_ref.at[b, cut * halves + half]
        target = inner if way == 0 else outer
        return remote(ref, ref, wo_send.at[way, b], wo_recv.at[row, cut, half], target)

    def wo_start(way, r, which):
        for cut in which:
            for half in range(halves):
                wo_copy(way, r, cut, half, row_there(way, r, False)).start()

    along = [(0, r, cut) for cut in range(cuts) for r in (1, 0)]
    back = [(1, r, cut) for cut in range(cuts) for r in (2, 3)]
    early = 3

    def wo_next(way, r, cut):
        for half in range(halves):
            if r != 1:
                wo_copy(way, r, cut, half, row_here(r)).wait_recv()
            wo_copy(way, r, cut, half, row_there(way, r, True)).start()

    def wo_moves(*moves):
        @pl.when(is_helper)
        def _():
            for move in moves:
                wo_next(*move)

    def kv_near(b, kinds):
        ref, slot = kv_ref.at[b, kinds], kv_in.at[0, b, kinds]
        return remote(ref, slot, kv_send.at[0], kv_recv.at[0], partner)

    def kv_far(b, kinds):
        ref, slot = kv_ref.at[b, kinds], kv_in.at[1, b, kinds]
        return remote(ref, slot, kv_send.at[1], kv_recv.at[1], along_x)

    def kv_cross(b, kinds):
        at = 2 * (1 - core)
        ref, slot = kv_ref.at[b, kinds], kv_in.at[at, b, kinds]
        target = place(across[1], 1 - core)
        return remote(ref, slot, kv_send.at[2], kv_recv.at[at], target)

    def kv_slot(slot):
        return remote(kv_ref, kv_in.at[slot], kv_send.at[slot], kv_recv.at[slot], partner)

    def accumulate(rs, p):
        lhs = jnp.concatenate([got[blk(r), p] for r in rs], axis=0)
        span = pl.ds(pl.multiple_of(p * deep, deep), deep)
        for kind in range(3):
            made = jnp.dot(lhs, wq_ref[kind, span], preferred_element_type=jnp.float32)
            for i, r in enumerate(rs):
                acc_ref[blk(r), kind] += made[i * rows : (i + 1) * rows]

    def settle(r, kinds, extra=False):
        b = blk(r)
        for kind in kinds:
            made = acc_ref[b, kind]
            if extra:
                made = made + part_in[b, kind].astype(jnp.float32)
            made = made.astype(q_ref.dtype)
            if kind == 0:
                q_ref[b] = made
            else:
                kv_ref[b, kind - 1] = made

    def share(r, first=0, count=2):
        kinds = pl.ds(first, count)

        @pl.when(tract < 2)
        def _():
            kv_far(blk(r), kinds).start()
            kv_cross(blk(r), kinds).start()

        @pl.when(core == 0)
        def _():
            kv_near(blk(r), kinds).start()

    own_load.wait()
    power = jnp.zeros((rows, 1), jnp.float32)
    for p in range(pieces):
        tokens = raw[:, p * deep : (p + 1) * deep].astype(jnp.float32)
        power += jnp.sum(tokens * tokens, axis=-1, keepdims=True)
    table_load.wait()
    factor = lax.rsqrt(power * (1.0 / width) + 1e-06)
    pl.semaphore_wait(barrier, n - 1 + len(others))

    @pl.when(is_end)
    def _():
        for kind in (1, 2):
            far_first(kind).start()

    def send_own(p):
        @pl.when(is_end)
        def _():
            for part in range(parts):
                tok(0, 0, p, part, 0).start()
            if p == 0:
                far_first(0).start()

        @pl.when(is_helper)
        def _():
            for part in range(parts):
                tok(0, 1, p, part, 1).start()
                if p < near:
                    tok(1, 1, p, part, 0).start()

    for p in range(pieces):
        tokens = raw[:, p * deep : (p + 1) * deep].astype(jnp.float32)
        shaped = tokens * factor * (1.0 + style(1, p * deep)) + style(0, p * deep)
        got[me, p] = shaped.astype(got.dtype)
        if p:
            send_own(p - 1)
    send_own(pieces - 1)
    acc_ref[...] = jnp.zeros_like(acc_ref)
    gate_ref[...] = table_ref[2, pl.ds(level, 1), :]

    @pl.when(is_end)
    def _():
        wq_load.wait()
        @pl.loop(0, pieces)
        def _(p):
            accumulate((0,), p)

        wo_loaded()
        wo_start(0, 0, range(cuts))

        settle(0, (1, 2, 0))
        share(0)
        for r in (1, 2):

            @pl.loop(0, near)
            def _(p):
                tok_take(0, r, p, None)
                accumulate((r,), p)

        for kind in (1, 2):
            for r in (1, 2):
                part_copy(r, kind).wait_recv()
                settle(r, (kind,), True)
                share(r, kind - 1, 1)

        @pl.loop(0, near)
        def _(p):
            tok_take(0, 3, p, None)
            accumulate((3,), p)

        for kind in (1, 2):
            part_copy(3, kind).wait_recv()
        settle(3, (1, 2), True)
        share(3)
        for r in (1, 2, 3):
            part_copy(r, 0).wait_recv()
            settle(r, (0,), True)

    @pl.when(is_helper)
    def _():
        def pass_on(p):
            tok_take(0, 0, p, True)
            accumulate((0,), p)

        wq_load.wait()
        @pl.loop(0, pieces)
        def _(p):
            tok_take(1, 2, p, p < near)
            accumulate((1, 2), p)
            for at, kind in ((1, 1), (3, 2), (7, 0)):

                @pl.when(p == at)
                def _():
                    far_relay(kind)

            @pl.when(p == near)
            def _():
                wo_loaded()
                wo_start(1, 1, range(cuts - 1))

            for at, kind in ((4, 1), (6, 2)):

                @pl.when(p == at)
                def _():
                    far_hand_x(kind)

            @pl.when(p >= pieces - 2)
            def _():
                pass_on(p - (pieces - 2))

        settle(1, (1, 2, 0))
        share(1)
        settle(2, (1, 2, 0))
        share(2)

        @pl.loop(0, pieces)
        def _(p):
            @pl.when(p + 2 < pieces)
            def _():
                pass_on(p + 2)

            tok_take(1, 3, p, p < near)

            @pl.when(p == pieces - 1)
            def _():
                far_part((3,), (1, 2))

            accumulate((3,), p)

            @pl.when(p == 1)
            def _():
                far_hand_y(1)

            @pl.when(p == 2)
            def _():
                far_hand_x(0)
                far_ready(1)
                far_part((1, 2), (1,))

            @pl.when(p == 3)
            def _():
                far_hand_y(2)

            @pl.when(p == 4)
            def _():
                far_ready(2)
                far_part((1, 2), (2,))
                wo_start(1, 1, (cuts - 1,))

            @pl.when(p == 5)
            def _():
                settle(0, (1, 2, 0))
                share(0)

            @pl.when(p == 6)
            def _():
                wo_next(*along[0])

            @pl.when(p == 5)
            def _():
                far_hand_y(0)

        settle(3, (1, 2))
        share(3)
        far_ready(0)
        far_part((1, 2, 3), (0,))
        settle(3, (0,))
        wo_next(*along[1])

        @pl.when(tract >= 2)
        def _():
            for move in along[2:early]:
                wo_next(*move)


    tokens_here = n * rows
    heads_here = q_ref.shape[2] // HD
    scale = HD ** (-0.5)

    def attend(source, bias):
        for head in range(heads_here):
            lanes = slice(head * HD, (head + 1) * HD)
            queries = q_ref[:, :, lanes].reshape(tokens_here, HD)
            keys = source[:, 0, :, lanes].reshape(tokens_here, HD)
            values = source[:, 1, :, lanes].reshape(tokens_here, HD)
            scores = (
                lax.dot_general(
                    keys, queries, (((1,), (1,)), ((), ())), preferred_element_type=jnp.float32
                )
                * scale
            )
            if bias is not None:
                scores = scores + bias
            peak = jnp.max(scores, axis=0, keepdims=True)
            if bias is not None:
                old = peak_ref[head]
                peak = jnp.maximum(old, peak)
            probs = jnp.exp(scores - peak)
            row_sum = jnp.sum(probs, axis=0, keepdims=True)
            weighted = lax.dot_general(
                values,
                probs.astype(jnp.bfloat16),
                (((0,), (0,)), ((), ())),
                preferred_element_type=jnp.float32,
            )
            if bias is not None:
                rescale = jnp.exp(old - peak)
                row_sum += sum_ref[head] * rescale
                weighted += mix_ref[head] * rescale
            peak_ref[head] = peak
            sum_ref[head] = row_sum
            mix_ref[head] = weighted

    attend(kv_ref, None)

    for ahead in (1, 2, 3):
        if ahead == 2:

            @pl.when(is_helper & (tract >= 2))
            def _():
                wo_next(*back[0])

        @pl.when(tract >= ahead)
        def _():
            kv_slot(ahead - 1).wait_recv()
            seen = visible_ref[0, lax.max(tract - ahead, 0)] > 0
            attend(kv_in.at[ahead - 1], jnp.where(seen, 0.0, -1e30))

    for head in range(heads_here):
        attended = jnp.transpose(mix_ref[head] / sum_ref[head]).astype(jnp.bfloat16)
        att_ref[:, :, head * HD : (head + 1) * HD] = attended.reshape(n, rows, HD)

    def att_line(other, source):
        return remote(
            att_ref.at[other],
            att_all.at[seat, source],
            z_send.at[other],
            z_recv.at[source],
            {"head": other},
        )

    line = [blk(jnp.where(is_end, end, help)) for end, help in ((0, 1), (1, 2), (2, 0), (3, 3))]
    for other in line[1:]:
        att_line(other, me).start()
    att_all[seat, me] = att_ref[me]

    def att_chip(by, z, which):
        ref = att_all.at[which * 2 + core] if z is None else att_all.at[which * 2 + core, z]
        at = a_recv.at[by - 1, 0 if z is None else z]
        return remote(ref, ref, a_send.at[by], at, place(seat_of(by, 0)[0], core))

    def att_pass(by, z, side):
        owner = seat_of(by, 0)[0] * 2 + side
        ref = att_all.at[owner] if z is None else att_all.at[owner, z]
        return remote(ref, ref, a_send.at[chips + by], b_recv.at[by], partner)

    @pl.when(is_helper)
    def _():
        @pl.when(tract < 2)
        def _():
            for move in along[2:early]:
                wo_next(*move)

        for move in along[early:]:
            wo_next(*move)

    for ahead, z in enumerate(line):
        if ahead:
            att_line(z, z).wait_recv()
        for by in range(1, chips):
            att_chip(by, z, chip).start()
        att_pass(0, z, core).start()
        for late, used in ((0, tract < 2), (1, tract >= 2)):

            @pl.when(is_helper & used)
            def _():
                for move in back[ahead + late : min(ahead + late + 1, 3)]:
                    wo_next(*move)

    for ahead, z in enumerate(line):
        for by in range(1, chips):
            att_chip(by, z, seat_of(by, 0)[0]).wait_recv()
            att_pass(by, z, core).start()
        if ahead == 2:
            wo_moves(*back[3:4])
    wo_moves(*back[4:5])
    for by in range(chips):
        att_pass(by, None, 1 - core).wait_recv()

    spans = [(k, 2) for k in range(0, units - 2, 2)] + [(units - 2, 1), (units - 1, 1)]

    def out_copy(by, side, source, at):
        which, lane = seat_of(by, side)
        span = pl.ds(*spans[at])
        return remote(
            out_part.at[which * 2 + lane, span],
            out_in.at[source, span],
            o_send.at[which * 2 + lane],
            o_recv.at[source, at],
            place(which, lane),
        )

    heads_wide = wo_ref.shape[2]

    def finish(ref, source, at):
        first, count = spans[at]
        for k in range(first, first + count):
            span = pl.ds(pl.multiple_of(source * cols_out + k * unit, 128), unit)
            done = ref[source, k].astype(jnp.float32) * gate_ref[:, span]
            out_ref[0, :, span] = done.astype(out_ref.dtype)

    for at, (first, count) in enumerate(spans):

        @pl.when(is_end)
        def _():
            for r in (1, 2, 3):
                for k in range(first, first + count):
                    wo_copy(0, r, k // halves, k % halves, r - 1).wait_recv()

        rhs = [
            jnp.concatenate([wo_ref[z, k] for k in range(first, first + count)], axis=1)
            for z in range(n)
        ]
        for pair in ((1, 2), (3, 0)):
            firsts = [seat_of(by, 0)[0] * 2 for by in pair]
            total = None
            for z in range(n):
                lhs = jnp.concatenate([att_all[pl.ds(q, 2), z] for q in firsts], axis=0)
                lhs = lhs.reshape(4 * rows, heads_wide)
                made = jnp.dot(lhs, rhs[z], preferred_element_type=jnp.float32)
                total = made if total is None else total + made
            total = total.astype(out_part.dtype).reshape(4, rows, count * unit)
            for j, q in enumerate(firsts):
                for k in range(count):
                    columns = slice(k * unit, (k + 1) * unit)
                    out_part[pl.ds(q, 2), first + k] = total[2 * j : 2 * j + 2, :, columns]
            for by, side in others:
                if by in pair:
                    out_copy(by, side, seat, at).start()
        if at == max(0, len(spans) - 3):
            wo_moves(*back[5:])

    for at in range(len(spans)):
        finish(out_part, seat, at)
        for by, side in reversed(others):
            which, lane = seat_of(by, side)
            source = which * 2 + lane
            out_copy(by, side, source, at).wait_recv()
            finish(out_in, source, at)

    for by, side in others:
        which, lane = seat_of(by, side)
        to = which * 2 + lane
        sems = o_send.at[to], o_recv.at[seat, 0]
        remote(out_part.at[to], out_in.at[seat], *sems, partner).wait_send()
    for by in range(chips):
        if by:
            att_chip(by, None, chip).wait_send()
        att_pass(by, None, core).wait_send()
    for ahead in range(1, n):
        att_line(lax.rem(me + ahead, n), me).wait_send()
    for slot, used in ((0, core == 0), (1, tract < 2), (2, tract < 2)):

        @pl.when(used)
        def _():
            kv_slot(slot).wait_send()

    def far_sent(where, which):
        ref = w_far.at[:, far_span(which, core)]
        remote(ref, ref, f_send.at[where], f_recv.at[where, 0], partner).wait_send()

    def wo_sent(way, r):
        ref = wo_ref.at[blk(r)]
        sems = wo_send.at[way, blk(r)], wo_recv.at[0, 0, 0]
        remote(ref, ref, *sems, partner).wait_send()

    @pl.when(is_end)
    def _():
        far_sent(0, chip)
        tok_sent(0, 0, pieces)
        wo_sent(0, 0)

    @pl.when(is_helper)
    def _():
        for slot in range(chips):
            if slot:
                far_sent(slot, across[1] if slot == 3 else chip)
            far_sent(chips + slot, across[slot])
        for r in (1, 2, 3):
            ref = part_ref.at[blk(r)]
            sems = p_send.at[blk(r)], p_recv.at[blk(r), 0]
            remote(ref, ref, *sems, partner).wait_send()
            tok_sent(1, r, near)
            wo_sent(1, r)
        for r in (0, 1):
            tok_sent(0, r, pieces)
            wo_sent(0, r)


PIECES = 8
NEAR = 4


def fits_line(n, tracts, reps, frames, w_out):
    rows, width = frames.shape[1:]
    seats = tracts * reps
    far = (PIECES - NEAR) * (width // PIECES)
    return (
        n == 4
        and (tracts, reps) == (4, 2)
        and rows % 16 == 0
        and width % (PIECES * 128) == 0
        and width % (seats * 256) == 0
        and far % (seats * 16) == 0
        and w_out.shape[0] % 32 == 0
    )


def line_body(frames, levels, visible, w_qkv, w_out, modulation):
    n, tracts = lax.axis_size("head"), lax.axis_size("tract")
    reps = lax.axis_size("rep")
    rows, width = frames.shape[1:]
    cols = w_qkv.shape[2]
    heads_here = cols // HD
    seats = tracts * reps
    chips = seats // 2
    deep = width // PIECES
    units = width // seats // 128
    vmem = pl.BlockSpec(memory_space=pltpu.VMEM)
    hbm = pl.BlockSpec(memory_space=pltpu.HBM)
    smem = pl.BlockSpec(memory_space=pltpu.SMEM)
    half = jnp.bfloat16
    dma = pltpu.SemaphoreType.DMA
    return pl.pallas_call(
        functools.partial(line_kernel, n, tracts, reps, PIECES, NEAR),
        out_shape=pltpu.VMEM(frames.shape, frames.dtype),
        in_specs=[hbm, smem, smem, hbm, hbm, hbm],
        out_specs=vmem,
        scratch_shapes=[
            pltpu.VMEM((3, *modulation.shape[::2]), jnp.float32),
            pltpu.VMEM((1, width), jnp.float32),
            pltpu.VMEM((rows, width), half),
            pltpu.VMEM((n, PIECES, rows, deep), half),
            pltpu.VMEM((3, width, cols), half),
            pltpu.VMEM((3, (PIECES - NEAR) * deep, cols), half),
            pltpu.VMEM((n, units, w_out.shape[0], 128), half),
            pltpu.VMEM((n, 3, rows, cols), jnp.float32),
            pltpu.VMEM((n, rows, cols), half),
            pltpu.VMEM((n, 2, rows, cols), half),
            pltpu.VMEM((max(1, tracts - 1), n, 2, rows, cols), half),
            pltpu.VMEM((n, 3, rows, cols), half),
            pltpu.VMEM((n, 3, rows, cols), half),
            pltpu.VMEM((n, rows, cols), half),
            pltpu.VMEM((heads_here, 1, n * rows), jnp.float32),
            pltpu.VMEM((heads_here, 1, n * rows), jnp.float32),
            pltpu.VMEM((heads_here, HD, n * rows), jnp.float32),
            pltpu.VMEM((seats, n, rows, cols), half),
            pltpu.VMEM((seats, units, rows, 128), half),
            pltpu.VMEM((seats, units, rows, 128), half),
            dma((3,)),
            dma((units,)),
            dma((2, n)),
            dma((n - 1, PIECES, 2)),
            dma((2 * chips,)),
            dma((2 * chips, 3)),
            dma((n,)),
            dma((n, 3)),
            dma((3,)),
            dma((3,)),
            dma((2, n)),
            dma((n - 1, units // 2, 2)),
            dma((n,)),
            dma((n,)),
            dma((2 * chips,)),
            dma((chips - 1, n)),
            dma((chips,)),
            dma((seats,)),
            dma((seats, units // 2 + 1)),
        ],
        compiler_params=pltpu.CompilerParams(
            collective_id=0, has_side_effects=True, vmem_limit_bytes=GRANT
        ),
    )(
        frames,
        levels,
        visible,
        jnp.transpose(w_qkv, (1, 0, 2)),
        w_out,
        jnp.transpose(modulation, (1, 0, 2)),
    )


def body(frames, levels, visible, w_qkv, w_out, modulation):
    n, tracts = lax.axis_size("head"), lax.axis_size("tract")
    reps = lax.axis_size("rep")
    line = fits_line(n, tracts, reps, frames, w_out)
    chosen = line_body if line else ring_body
    return chosen(frames, levels, visible, w_qkv, w_out, modulation)


def solution(mesh):
    placed = (
        P(("rep", "tract"), "head", None),
        P(("rep", "tract")),
        P(("rep", "tract"), None),
        P(None, None, "head"),
        P("head", None),
        P(),
    )
    return jax.shard_map(
        body,
        mesh=mesh,
        in_specs=placed,
        out_specs=P(("rep", "tract"), "head", None),
        check_vma=False,
    )
```

```python
import functools

import jax
import jax.numpy as jnp
from jax import lax
from jax.experimental import pallas as pl
from jax.experimental.pallas import tpu as pltpu
from jax.sharding import PartitionSpec as P

HD = 128
GRANT = 60 * 1024 * 1024
MESH = pl.DeviceIdType.MESH


def meet(n, me, tracts, tract, others):
    barrier = pltpu.get_barrier_semaphore()
    for other in (lax.rem(me + 1, n), lax.rem(me + n - 1, n)):
        pl.semaphore_signal(barrier, inc=1, device_id={"head": other}, device_id_type=MESH)
    for ahead in range(1, tracts):
        other = lax.rem(tract + ahead, tracts)
        pl.semaphore_signal(barrier, inc=1, device_id={"tract": other}, device_id_type=MESH)
    for other in others:
        pl.semaphore_signal(barrier, inc=1, device_id=other, device_id_type=MESH)
    pl.semaphore_wait(barrier, 1 + tracts + len(others))


def sublayer_kernel(
    n,
    tracts,
    reps,
    pieces,
    halves,
    x_ref,
    level_ref,
    visible_ref,
    w_hbm,
    out_hbm,
    table_ref,
    out_ref,
    got,
    wq_ref,
    w_ref,
    q_ref,
    kv_ref,
    kv_in,
    att_ref,
    peak_ref,
    sum_ref,
    acc_ref,
    going,
    landed,
    total_ref,
    load_sem,
    g_send,
    g_recv,
    kv_send,
    kv_recv,
    s_send,
    s_recv,
    w_far,
    att_far,
    f_send,
    f_recv,
):
    me, tract = lax.axis_index("head"), lax.axis_index("tract")
    own = pltpu.make_async_copy(x_ref.at[0], got.at[me], load_sem.at[0])
    own.start()
    load = pltpu.make_async_copy(w_hbm, wq_ref, load_sem.at[1])
    load.start()
    load_out = pltpu.make_async_copy(out_hbm, w_ref, load_sem.at[2])
    load_out.start()
    core, wide = tract % 2, tracts // 2
    chips = wide * reps
    chip = lax.axis_index("rep") * wide + tract // 2
    slab = w_ref.shape[0] // (2 * chips)
    helper = (me == 1) | (me == n - 2)
    ends = (me == 0) | (me == n - 1)

    def seat(by):
        other = lax.rem(chip + by, chips)
        return {"rep": other // wide, "tract": lax.rem(other, wide) * 2 + core}

    def slab_of(which, side):
        start = pl.multiple_of((which * 2 + side) * slab, slab)
        return pl.ds(start, slab)

    def far_copy(kind, span, target, source=None):
        return pltpu.make_async_remote_copy(
            src_ref=(w_far if source is None else source).at[span],
            dst_ref=w_far.at[span],
            send_sem=f_send.at[kind],
            recv_sem=f_recv.at[kind],
            device_id=target,
            device_id_type=MESH,
        )

    inward = {"head": jnp.where(me == 0, 1, n - 2)}
    partner = {"tract": tract + 1 - 2 * core}
    mine = slab_of(chip, core)

    def to_helper():
        return far_copy(0, mine, inward, out_hbm)

    def to_chip(by):
        return far_copy(by, mine, seat(by))

    def from_chip(by):
        return far_copy(by, slab_of(lax.rem(chip + chips - by, chips), core), seat(by))

    def to_partner(by):
        span = slab_of(lax.rem(chip + chips - by, chips), core)
        return far_copy(chips + by, span, partner)

    def from_partner(by):
        span = slab_of(lax.rem(chip + chips - by, chips), 1 - core)
        return far_copy(chips + by, span, partner)

    def att_copy():
        return pltpu.make_async_remote_copy(
            src_ref=att_ref,
            dst_ref=att_far,
            send_sem=f_send.at[2 * chips],
            recv_sem=f_recv.at[2 * chips],
            device_id=inward,
            device_id_type=MESH,
        )

    meet(n, me, tracts, tract, [seat(by) for by in range(1, chips)])
    level = level_ref[0]

    def style(kind):
        return table_ref[kind, pl.ds(level, 1), :]

    rows, width = x_ref.shape[1:]
    part = rows // pieces

    def copy(way, step, piece, first=False):
        side = (way + 1) // 2
        span = pl.ds(piece * part, part)
        block = me - way * step
        return pltpu.make_async_remote_copy(
            src_ref=(x_ref.at[0] if first else got.at[block]).at[span],
            dst_ref=got.at[block].at[span],
            send_sem=g_send.at[side, step, piece],
            recv_sem=g_recv.at[side, step, piece],
            device_id={"head": me + way},
            device_id_type=MESH,
        )

    def arrival(way, step, piece):
        side = (way + 1) // 2
        span = pl.ds(piece * part, part)
        return pltpu.make_async_remote_copy(
            src_ref=x_ref.at[0].at[span],
            dst_ref=got.at[me - way * (step + 1)].at[span],
            send_sem=g_send.at[side, step, piece],
            recv_sem=g_recv.at[side, step, piece],
            device_id={"head": me - way},
            device_id_type=MESH,
        )

    def sends(way, step):
        block, target = me - way * step, me + way
        return (block >= 0) & (block < n) & (target >= 0) & (target < n) & (step < n - 1)

    def receives(way, step):
        block = me - way * (step + 1)
        return (block >= 0) & (block < n)

    def kv_copy(ahead, block):
        return pltpu.make_async_remote_copy(
            src_ref=kv_ref.at[block],
            dst_ref=kv_in.at[ahead - 1, block],
            send_sem=kv_send.at[ahead - 1, block],
            recv_sem=kv_recv.at[ahead - 1, block],
            device_id={"tract": tract + ahead},
            device_id_type=MESH,
        )

    def project(block):
        tokens = got[block].astype(jnp.float32)
        power = jnp.mean(tokens * tokens, axis=-1, keepdims=True)
        normed = tokens * lax.rsqrt(power + 1e-06)
        shaped = (normed * (1.0 + style(1)) + style(0)).astype(jnp.bfloat16)
        for kind in (1, 2, 0):
            made = jnp.dot(shaped, wq_ref[kind], preferred_element_type=jnp.float32)
            made = made.astype(jnp.bfloat16)
            if kind == 0:
                q_ref[block] = made
            else:
                kv_ref[block, kind - 1] = made
            if kind == 2:
                for ahead in range(1, tracts):

                    @pl.when(tract + ahead < tracts)
                    def _():
                        kv_copy(ahead, block).start()

    for piece in range(pieces):
        for way in (-1, 1):

            @pl.when(sends(way, 0))
            def _():
                copy(way, 0, piece, True).start()

    @pl.when(ends)
    def _():
        to_helper().start()

    own.wait()
    load.wait()
    project(me)

    @pl.loop(0, n - 1)
    def _(step):
        for piece in range(pieces):
            for way in (-1, 1):

                @pl.when(receives(way, step))
                def _():
                    arrival(way, step, piece).wait_recv()

                @pl.when(sends(way, step + 1))
                def _():
                    copy(way, step + 1, piece).start()

        @pl.loop(0, 2)
        def _(side):
            way = 2 * side - 1

            @pl.when(receives(way, step))
            def _():
                project(me - way * (step + 1))

        @pl.when(helper & (step == 0))
        def _():
            to_helper().wait_recv()
            for by in range(1, chips):
                to_chip(by).start()
            to_partner(0).start()

    @pl.when(helper)
    def _():
        for by in range(1, chips):
            from_chip(by).wait_recv()
            to_partner(by).start()

    tokens_here = n * rows
    heads_here = q_ref.shape[2] // HD
    scale = HD ** (-0.5)

    def attend(source, allowed):
        for head in range(heads_here):
            lanes = slice(head * HD, (head + 1) * HD)
            queries = q_ref[:, :, lanes].reshape(tokens_here, HD)
            keys = source[:, 0, :, lanes].reshape(tokens_here, HD)
            values = source[:, 1, :, lanes].reshape(tokens_here, HD)
            scores = (
                lax.dot_general(
                    queries, keys, (((1,), (1,)), ((), ())), preferred_element_type=jnp.float32
                )
                * scale
            )
            if allowed is None:
                peak = jnp.max(scores, axis=1, keepdims=True)
                probs = jnp.exp(scores - peak)
            else:
                scores = jnp.where(allowed, scores, -1e30)
                old = peak_ref[head]
                peak = jnp.maximum(old, jnp.max(scores, axis=1, keepdims=True))
                probs = jnp.where(allowed, jnp.exp(scores - peak), 0.0)
                rescale = jnp.exp(old - peak)
            row_sum = jnp.sum(probs, axis=1, keepdims=True)
            weighted = jnp.dot(
                probs.astype(jnp.bfloat16), values, preferred_element_type=jnp.float32
            )
            if allowed is not None:
                row_sum += sum_ref[head] * rescale
                weighted += acc_ref[head] * rescale
            peak_ref[head] = peak
            sum_ref[head] = row_sum
            acc_ref[head] = weighted

    attend(kv_ref, None)
    for ahead in range(1, tracts):

        @pl.when(tract >= ahead)
        def _():
            @pl.loop(0, n)
            def _(block):
                kv_copy(ahead, block).wait_recv()

            attend(kv_in.at[ahead - 1], visible_ref[0, lax.max(tract - ahead, 0)] > 0)

    for head in range(heads_here):
        attended = (acc_ref[head] / sum_ref[head]).astype(jnp.bfloat16)
        att_ref[:, :, head * HD : (head + 1) * HD] = attended.reshape(n, rows, HD)

    @pl.when(ends)
    def _():
        att_copy().start()

    load_out.wait()

    @pl.when(helper)
    def _():
        for by in range(chips):
            from_partner(by).wait_recv()
        att_copy().wait_recv()

    cols = width // halves

    def sum_copy(way, step, piece):
        side = (way + 1) // 2
        span = pl.ds(piece * cols, cols)
        return pltpu.make_async_remote_copy(
            src_ref=going.at[side, step].at[:, span],
            dst_ref=landed.at[side, step].at[:, span],
            send_sem=s_send.at[side, step, piece],
            recv_sem=s_recv.at[side, step, piece],
            device_id={"head": me + way},
            device_id_type=MESH,
        )

    def product(block, piece):
        return jnp.dot(
            att_ref[block],
            w_ref[:, piece * cols : (piece + 1) * cols],
            preferred_element_type=jnp.float32,
        )

    def far_product(block, piece):
        return jnp.dot(
            att_far[block],
            w_far[:, piece * cols : (piece + 1) * cols],
            preferred_element_type=jnp.float32,
        )

    def helps(way):
        return me == (1 if way == 1 else n - 2)

    def owner(way, step):
        return (n - 1 - step) if way == 1 else step

    def sum_sends(way, step):
        block = owner(way, step)
        return (block > me) & (me > 0) if way == 1 else (block < me) & (me < n - 1)

    def sum_receives(way, step):
        block = owner(way, step)
        return (block >= me) & (me > 1) if way == 1 else (block <= me) & (me < n - 2)

    @pl.loop(0, n - 1)
    def _(tick):
        for piece in range(halves):
            span = slice(piece * cols, (piece + 1) * cols)
            for way in (-1, 1):
                side = (way + 1) // 2
                step = tick - (me if way == 1 else n - 1 - me)
                held = (step >= 0) & (step < n - 1)

                @pl.when(held & sum_sends(way, step))
                def _():
                    going[side, step, :, span] = product(owner(way, step), piece).astype(
                        going.dtype
                    )

                    @pl.when(helps(way))
                    def _():
                        going[side, step, :, span] = (
                            going[side, step, :, span].astype(jnp.float32)
                            + far_product(owner(way, step), piece)
                        ).astype(going.dtype)

                    @pl.when(sum_receives(way, step))
                    def _():
                        sum_copy(way, step, piece).wait_recv()
                        going[side, step, :, span] = (
                            going[side, step, :, span].astype(jnp.float32)
                            + landed[side, step, :, span].astype(jnp.float32)
                        ).astype(going.dtype)

                    sum_copy(way, step, piece).start()

    for piece in range(halves):
        span = slice(piece * cols, (piece + 1) * cols)
        total_ref[:, span] = product(me, piece).astype(going.dtype).astype(jnp.float32)
    for piece in range(halves):
        span = slice(piece * cols, (piece + 1) * cols)
        for way in (-1, 1):
            side = (way + 1) // 2
            last = n - 1 - me if way == 1 else me

            @pl.when(helps(way))
            def _():
                total_ref[:, span] += far_product(me, piece)

            @pl.when(me > 1 if way == 1 else me < n - 2)
            def _():
                sum_copy(way, last, piece).wait_recv()
                total_ref[:, span] += landed[side, last, :, span].astype(jnp.float32)

        out_ref[0, :, span] = (
            total_ref[:, span] * table_ref[2, pl.ds(level, 1), span]
        ).astype(out_ref.dtype)

    @pl.loop(0, n - 1)
    def _(step):
        for piece in range(halves):
            for way in (-1, 1):

                @pl.when(sum_sends(way, step))
                def _():
                    sum_copy(way, step, piece).wait_send()

    @pl.loop(0, n)
    def _(block):
        for ahead in range(1, tracts):

            @pl.when(tract + ahead < tracts)
            def _():
                kv_copy(ahead, block).wait_send()

    @pl.loop(0, n - 1)
    def _(step):
        for piece in range(pieces):
            for way in (-1, 1):

                @pl.when(sends(way, step))
                def _():
                    copy(way, step, piece).wait_send()

    @pl.when(ends)
    def _():
        to_helper().wait_send()
        att_copy().wait_send()

    @pl.when(helper)
    def _():
        for by in range(1, chips):
            to_chip(by).wait_send()
        for by in range(chips):
            to_partner(by).wait_send()


def ring_body(frames, levels, visible, w_qkv, w_out, modulation):
    n, tracts = lax.axis_size("head"), lax.axis_size("tract")
    reps = lax.axis_size("rep")
    rows, width = frames.shape[1:]
    cols = w_qkv.shape[2]
    heads_here = cols // HD
    pieces = max(1, rows // 32)
    halves = 4 if width % 512 == 0 else 2
    vmem = pl.BlockSpec(memory_space=pltpu.VMEM)
    hbm = pl.BlockSpec(memory_space=pltpu.HBM)
    smem = pl.BlockSpec(memory_space=pltpu.SMEM)
    half = jnp.bfloat16
    dma = pltpu.SemaphoreType.DMA
    return pl.pallas_call(
        functools.partial(sublayer_kernel, n, tracts, reps, pieces, halves),
        out_shape=jax.ShapeDtypeStruct(frames.shape, frames.dtype),
        in_specs=[hbm, smem, smem, hbm, hbm, vmem],
        out_specs=vmem,
        scratch_shapes=[
            pltpu.VMEM((n, rows, width), half),
            pltpu.VMEM((3, width, cols), half),
            pltpu.VMEM(w_out.shape, half),
            pltpu.VMEM((n, rows, cols), half),
            pltpu.VMEM((n, 2, rows, cols), half),
            pltpu.VMEM((max(1, tracts - 1), n, 2, rows, cols), half),
            pltpu.VMEM((n, rows, cols), half),
            pltpu.VMEM((heads_here, n * rows, 1), jnp.float32),
            pltpu.VMEM((heads_here, n * rows, 1), jnp.float32),
            pltpu.VMEM((heads_here, n * rows, HD), jnp.float32),
            pltpu.VMEM((2, n - 1, rows, width), half),
            pltpu.VMEM((2, n - 1, rows, width), half),
            pltpu.VMEM((rows, width), jnp.float32),
            dma((3,)),
            dma((2, n, pieces)),
            dma((2, n, pieces)),
            dma((tracts, n)),
            dma((tracts, n)),
            dma((2, n, halves)),
            dma((2, n, halves)),
            pltpu.VMEM(w_out.shape, half),
            pltpu.VMEM((n, rows, cols), half),
            dma((tracts * reps + 1,)),
            dma((tracts * reps + 1,)),
        ],
        compiler_params=pltpu.CompilerParams(
            collective_id=0, has_side_effects=True, vmem_limit_bytes=GRANT
        ),
    )(
        frames,
        levels,
        visible,
        jnp.transpose(w_qkv, (1, 0, 2)),
        w_out,
        jnp.transpose(modulation, (1, 0, 2)),
    )


def line_kernel(
    n,
    tracts,
    reps,
    pieces,
    near,
    x_ref,
    level_ref,
    visible_ref,
    w_hbm,
    out_hbm,
    table_hbm,
    out_ref,
    table_ref,
    gate_ref,
    raw,
    got,
    wq_ref,
    w_far,
    wo_ref,
    acc_ref,
    q_ref,
    kv_ref,
    kv_in,
    part_ref,
    part_in,
    att_ref,
    peak_ref,
    sum_ref,
    mix_ref,
    att_all,
    out_part,
    out_in,
    load_sem,
    wo_sem,
    g_send,
    g_recv,
    f_send,
    f_recv,
    p_send,
    p_recv,
    kv_send,
    kv_recv,
    wo_send,
    wo_recv,
    z_send,
    z_recv,
    a_send,
    a_recv,
    b_recv,
    o_send,
    o_recv,
):
    me, tract, rep = lax.axis_index("head"), lax.axis_index("tract"), lax.axis_index("rep")
    rows, width = x_ref.shape[1:]
    deep = width // pieces
    low = me < 2
    sign = jnp.where(low, 1, -1)
    base = jnp.where(low, 0, n - 1)
    is_end = (me == 0) | (me == n - 1)
    is_helper = (me == 1) | (me == n - 2)
    inner, outer = {"head": me + sign}, {"head": me - sign}

    def blk(r):
        return base + sign * r

    core, wide = tract % 2, tracts // 2
    chips = wide * reps
    seats = chips * 2
    chip = rep * wide + tract // 2
    seat = chip * 2 + core
    partner = {"tract": tract + 1 - 2 * core}

    def chip_at(by):
        return lax.rem(chip + by, chips)

    def place(which, side):
        return {"rep": which // wide, "tract": lax.rem(which, wide) * 2 + side}

    across = [
        chip,
        rep * wide + 1 - lax.rem(chip, wide),
        (1 - rep) * wide + lax.rem(chip, wide),
        (1 - rep) * wide + 1 - lax.rem(chip, wide),
    ]
    along_x, along_y = place(across[1], core), place(across[2], core)
    others = [(by, side) for by in (1, 2, 3) for side in (0, 1)] + [(0, 1)]

    def seat_of(by, side):
        return across[(3, 1, 2)[by - 1] if by else 0], core if side == 0 else 1 - core


    own_load = pltpu.make_async_copy(x_ref.at[0], raw, load_sem.at[0])
    own_load.start()
    barrier = pltpu.get_barrier_semaphore()
    for ahead in range(1, n):
        other = lax.rem(me + ahead, n)
        pl.semaphore_signal(barrier, inc=1, device_id={"head": other}, device_id_type=MESH)
    for other in others:
        target = place(*seat_of(*other))
        pl.semaphore_signal(barrier, inc=1, device_id=target, device_id_type=MESH)

    table_load = pltpu.make_async_copy(table_hbm, table_ref, load_sem.at[1])
    table_load.start()
    cols_out = width // seats
    units = wo_ref.shape[1]
    cuts, unit = units // 2, cols_out // units

    def wo_load(k):
        start = pl.multiple_of(seat * cols_out + k * unit, 128)
        src = out_hbm.at[:, pl.ds(start, unit)]
        return pltpu.make_async_copy(src, wo_ref.at[me, k], wo_sem.at[k])

    def wo_loaded():
        for k in range(units):
            wo_load(k).wait()

    wq_load = pltpu.make_async_copy(w_hbm, wq_ref, load_sem.at[2])
    wq_load.start()

    for k in range(units):
        wo_load(k).start()

    level = level_ref[0]

    def style(kind, start):
        return table_ref[kind, pl.ds(level, 1), start : start + deep]

    def remote(src, dst, send, recv, target):
        return pltpu.make_async_remote_copy(
            src_ref=src,
            dst_ref=dst,
            send_sem=send,
            recv_sem=recv,
            device_id=target,
            device_id_type=MESH,
        )

    parts = g_recv.shape[2]
    part_rows = rows // parts

    def row_there(way, r, onward):
        if way == 1:
            return r - 1
        return 1 if r == 1 else 2 if onward else 0

    def row_here(r):
        return max(r - 1, 0)

    def tok(way, r, p, part, row):
        b = blk(r)
        ref = got.at[b, p, pl.ds(part * part_rows, part_rows)]
        target = inner if way == 0 else outer
        return remote(ref, ref, g_send.at[way], g_recv.at[row, p, part], target)

    def tok_take(way, r, p, onward):
        for part in range(parts):
            tok(way, r, p, part, row_here(r)).wait_recv()
            if onward is not None:

                @pl.when(onward)
                def _():
                    tok(way, r, p, part, row_there(way, r, True)).start()

    def tok_sent(way, blocks, count):
        ref = got.at[pl.ds(0, blocks), pl.ds(0, count)]
        remote(ref, ref, g_send.at[way], g_recv.at[0, 0, 0], partner).wait_send()

    far_rows = w_far.shape[1] // seats
    far_base = near * deep

    def far_span(which, side):
        start = (which * 2 + side) * far_rows
        return pl.ds(pl.multiple_of(start, far_rows), far_rows)

    def far_first(kind):
        start = far_base + seat * far_rows
        src = w_hbm.at[kind, pl.ds(pl.multiple_of(start, far_rows), far_rows)]
        dst = w_far.at[kind, far_span(chip, core)]
        return remote(src, dst, f_send.at[0], f_recv.at[0, kind], inner)

    def far_move(slot, kind, which):
        ref = w_far.at[kind, far_span(which, core)]
        target = along_x if slot == 1 else along_y
        return remote(ref, ref, f_send.at[slot], f_recv.at[slot, kind], target)

    def far_pass(slot, kind, side):
        ref = w_far.at[kind, far_span(across[slot], side)]
        where = chips + slot
        return remote(ref, ref, f_send.at[where], f_recv.at[where, kind], partner)

    def far_relay(kind):
        far_first(kind).wait_recv()
        far_move(1, kind, chip).start()
        far_move(2, kind, chip).start()
        far_pass(0, kind, core).start()

    def far_hand_x(kind):
        far_move(1, kind, across[1]).wait_recv()
        far_move(3, kind, across[1]).start()
        far_pass(1, kind, core).start()

    def far_hand_y(kind):
        for slot in (2, 3):
            far_move(slot, kind, across[slot]).wait_recv()
            far_pass(slot, kind, core).start()

    def far_ready(kind):
        for slot in range(chips):
            far_pass(slot, kind, 1 - core).wait_recv()

    def part_copy(r, kind):
        b = blk(r)
        return remote(
            part_ref.at[b, kind],
            part_in.at[b, kind],
            p_send.at[b],
            p_recv.at[b, kind],
            outer,
        )

    def far_part(rs, kinds):
        for kind in kinds:
            total = None
            for p in range(near, pieces):
                lhs = jnp.concatenate([got[blk(r), p] for r in rs], axis=0)
                span = slice((p - near) * deep, (p - near + 1) * deep)
                made = jnp.dot(lhs, w_far[kind, span], preferred_element_type=jnp.float32)
                total = made if total is None else total + made
            total = total.astype(part_ref.dtype)
            for i, r in enumerate(rs):
                part_ref[blk(r), kind] = total[i * rows : (i + 1) * rows]
        for r in rs:
            for kind in kinds:
                part_copy(r, kind).start()

    halves = wo_recv.shape[2]

    def wo_copy(way, r, cut, half, row):
        b = blk(r)
        ref = wo_ref.at[b, cut * halves + half]
        target = inner if way == 0 else outer
        return remote(ref, ref, wo_send.at[way], wo_recv.at[row, cut, half], target)

    def wo_start(way, r, which):
        for cut in which:
            for half in range(halves):
                wo_copy(way, r, cut, half, row_there(way, r, False)).start()

    along = [(0, r, cut) for cut in range(cuts) for r in (1, 0)]
    back = [(1, r, cut) for cut in range(cuts) for r in (2, 3)]
    early = 3

    def wo_next(way, r, cut):
        for half in range(halves):
            if r != 1:
                wo_copy(way, r, cut, half, row_here(r)).wait_recv()
            wo_copy(way, r, cut, half, row_there(way, r, True)).start()

    def wo_moves(*moves):
        @pl.when(is_helper)
        def _():
            for move in moves:
                wo_next(*move)

    def kv_near(b, kinds):
        ref, slot = kv_ref.at[b, kinds], kv_in.at[0, b, kinds]
        return remote(ref, slot, kv_send.at[0], kv_recv.at[0], partner)

    def kv_far(b, kinds):
        ref, slot = kv_ref.at[b, kinds], kv_in.at[1, b, kinds]
        return remote(ref, slot, kv_send.at[1], kv_recv.at[1], along_x)

    def kv_cross(b, kinds):
        at = 2 * (1 - core)
        ref, slot = kv_ref.at[b, kinds], kv_in.at[at, b, kinds]
        target = place(across[1], 1 - core)
        return remote(ref, slot, kv_send.at[2], kv_recv.at[at], target)

    def kv_slot(slot):
        return remote(kv_ref, kv_in.at[slot], kv_send.at[slot], kv_recv.at[slot], partner)

    def accumulate(rs, p):
        lhs = jnp.concatenate([got[blk(r), p] for r in rs], axis=0)
        span = pl.ds(pl.multiple_of(p * deep, deep), deep)
        for kind in range(3):
            made = jnp.dot(lhs, wq_ref[kind, span], preferred_element_type=jnp.float32)
            for i, r in enumerate(rs):
                acc_ref[blk(r), kind] += made[i * rows : (i + 1) * rows]

    def settle(r, kinds, extra=False):
        b = blk(r)
        for kind in kinds:
            made = acc_ref[b, kind]
            if extra:
                made = made + part_in[b, kind].astype(jnp.float32)
            made = made.astype(q_ref.dtype)
            if kind == 0:
                q_ref[b] = made
            else:
                kv_ref[b, kind - 1] = made

    def share(r, first=0, count=2):
        kinds = pl.ds(first, count)

        @pl.when(tract < 2)
        def _():
            kv_far(blk(r), kinds).start()
            kv_cross(blk(r), kinds).start()

        @pl.when(core == 0)
        def _():
            kv_near(blk(r), kinds).start()

    own_load.wait()
    power = jnp.zeros((rows, 1), jnp.float32)
    for p in range(pieces):
        tokens = raw[:, p * deep : (p + 1) * deep].astype(jnp.float32)
        power += jnp.sum(tokens * tokens, axis=-1, keepdims=True)
    table_load.wait()
    factor = lax.rsqrt(power * (1.0 / width) + 1e-06)
    pl.semaphore_wait(barrier, n - 1 + len(others))

    @pl.when(is_end)
    def _():
        for kind in (1, 2):
            far_first(kind).start()

    def send_own(p):
        @pl.when(is_end)
        def _():
            for part in range(parts):
                tok(0, 0, p, part, 0).start()
            if p == 0:
                far_first(0).start()

        @pl.when(is_helper)
        def _():
            for part in range(parts):
                tok(0, 1, p, part, 1).start()
                if p < near:
                    tok(1, 1, p, part, 0).start()

    for p in range(pieces):
        tokens = raw[:, p * deep : (p + 1) * deep].astype(jnp.float32)
        shaped = tokens * factor * (1.0 + style(1, p * deep)) + style(0, p * deep)
        got[me, p] = shaped.astype(got.dtype)
        if p:
            send_own(p - 1)
    send_own(pieces - 1)
    acc_ref[...] = jnp.zeros_like(acc_ref)
    gate_ref[...] = table_ref[2, pl.ds(level, 1), :]

    @pl.when(is_end)
    def _():
        wq_load.wait()
        @pl.loop(0, pieces)
        def _(p):
            accumulate((0,), p)

        wo_loaded()
        wo_start(0, 0, range(cuts))

        settle(0, (1, 2, 0))
        share(0)
        for r in (1, 2):

            @pl.loop(0, near)
            def _(p):
                tok_take(0, r, p, None)
                accumulate((r,), p)

        for kind in (1, 2):
            for r in (1, 2):
                part_copy(r, kind).wait_recv()
                settle(r, (kind,), True)
                share(r, kind - 1, 1)

        @pl.loop(0, near)
        def _(p):
            tok_take(0, 3, p, None)
            accumulate((3,), p)

        for kind in (1, 2):
            part_copy(3, kind).wait_recv()
        settle(3, (1, 2), True)
        share(3)
        for r in (1, 2, 3):
            part_copy(r, 0).wait_recv()
            settle(r, (0,), True)

    @pl.when(is_helper)
    def _():
        def pass_on(p):
            tok_take(0, 0, p, True)
            accumulate((0,), p)

        wq_load.wait()
        @pl.loop(0, pieces)
        def _(p):
            tok_take(1, 2, p, p < near)
            accumulate((1, 2), p)
            for at, kind in ((1, 1), (3, 2), (7, 0)):

                @pl.when(p == at)
                def _():
                    far_relay(kind)

            @pl.when(p == near)
            def _():
                wo_loaded()
                wo_start(1, 1, range(cuts - 1))

            for at, kind in ((4, 1), (6, 2)):

                @pl.when(p == at)
                def _():
                    far_hand_x(kind)

            @pl.when(p >= pieces - 2)
            def _():
                pass_on(p - (pieces - 2))

        settle(1, (1, 2, 0))
        share(1)
        settle(2, (1, 2, 0))
        share(2)

        @pl.loop(0, pieces)
        def _(p):
            @pl.when(p + 2 < pieces)
            def _():
                pass_on(p + 2)

            tok_take(1, 3, p, p < near)

            @pl.when(p == pieces - 1)
            def _():
                far_part((3,), (1, 2))

            accumulate((3,), p)

            @pl.when(p == 1)
            def _():
                far_hand_y(1)

            @pl.when(p == 2)
            def _():
                far_hand_x(0)
                far_ready(1)
                far_part((1, 2), (1,))

            @pl.when(p == 3)
            def _():
                far_hand_y(2)

            @pl.when(p == 4)
            def _():
                far_ready(2)
                far_part((1, 2), (2,))
                wo_start(1, 1, (cuts - 1,))

            @pl.when(p == 5)
            def _():
                settle(0, (1, 2, 0))
                share(0)

            @pl.when(p == 6)
            def _():
                wo_next(*along[0])

            @pl.when(p == 5)
            def _():
                far_hand_y(0)

        settle(3, (1, 2))
        share(3)
        far_ready(0)
        far_part((1, 2, 3), (0,))
        settle(3, (0,))
        wo_next(*along[1])

        @pl.when(tract >= 2)
        def _():
            for move in along[2:early]:
                wo_next(*move)


    tokens_here = n * rows
    heads_here = q_ref.shape[2] // HD
    scale = HD ** (-0.5)

    def attend(source, bias):
        for head in range(heads_here):
            lanes = slice(head * HD, (head + 1) * HD)
            queries = q_ref[:, :, lanes].reshape(tokens_here, HD)
            keys = source[:, 0, :, lanes].reshape(tokens_here, HD)
            values = source[:, 1, :, lanes].reshape(tokens_here, HD)
            scores = (
                lax.dot_general(
                    keys, queries, (((1,), (1,)), ((), ())), preferred_element_type=jnp.float32
                )
                * scale
            )
            if bias is not None:
                scores = scores + bias
            peak = jnp.max(scores, axis=0, keepdims=True)
            if bias is not None:
                old = peak_ref[head]
                peak = jnp.maximum(old, peak)
            probs = jnp.exp(scores - peak)
            row_sum = jnp.sum(probs, axis=0, keepdims=True)
            weighted = lax.dot_general(
                values,
                probs.astype(jnp.bfloat16),
                (((0,), (0,)), ((), ())),
                preferred_element_type=jnp.float32,
            )
            if bias is not None:
                rescale = jnp.exp(old - peak)
                row_sum += sum_ref[head] * rescale
                weighted += mix_ref[head] * rescale
            peak_ref[head] = peak
            sum_ref[head] = row_sum
            mix_ref[head] = weighted

    attend(kv_ref, None)

    for ahead in (1, 2, 3):
        if ahead == 2:

            @pl.when(is_helper & (tract >= 2))
            def _():
                wo_next(*back[0])

        @pl.when(tract >= ahead)
        def _():
            kv_slot(ahead - 1).wait_recv()
            seen = visible_ref[0, lax.max(tract - ahead, 0)] > 0
            attend(kv_in.at[ahead - 1], jnp.where(seen, 0.0, -1e30))

    for head in range(heads_here):
        attended = jnp.transpose(mix_ref[head] / sum_ref[head]).astype(jnp.bfloat16)
        att_ref[:, :, head * HD : (head + 1) * HD] = attended.reshape(n, rows, HD)

    def att_line(other, source):
        return remote(
            att_ref.at[other],
            att_all.at[seat, source],
            z_send.at[0],
            z_recv.at[source],
            {"head": other},
        )

    line = [blk(jnp.where(is_end, end, help)) for end, help in ((0, 1), (1, 2), (2, 0), (3, 3))]
    for other in line[1:]:
        att_line(other, me).start()
    att_all[seat, me] = att_ref[me]

    def att_chip(by, z, which):
        ref = att_all.at[which * 2 + core] if z is None else att_all.at[which * 2 + core, z]
        at = a_recv.at[by - 1, 0 if z is None else z]
        return remote(ref, ref, a_send.at[by], at, place(seat_of(by, 0)[0], core))

    def att_pass(by, z, side):
        owner = seat_of(by, 0)[0] * 2 + side
        ref = att_all.at[owner] if z is None else att_all.at[owner, z]
        return remote(ref, ref, a_send.at[chips + by], b_recv.at[by], partner)

    @pl.when(is_helper)
    def _():
        @pl.when(tract < 2)
        def _():
            for move in along[2:early]:
                wo_next(*move)

        for move in along[early:]:
            wo_next(*move)

    for ahead, z in enumerate(line):
        if ahead:
            att_line(z, z).wait_recv()
        for by in range(1, chips):
            att_chip(by, z, chip).start()
        att_pass(0, z, core).start()
        for late, used in ((0, tract < 2), (1, tract >= 2)):

            @pl.when(is_helper & used)
            def _():
                for move in back[ahead + late : min(ahead + late + 1, 3)]:
                    wo_next(*move)

    for ahead, z in enumerate(line):
        for by in range(1, chips):
            att_chip(by, z, seat_of(by, 0)[0]).wait_recv()
            att_pass(by, z, core).start()
        if ahead == 2:
            wo_moves(*back[3:4])
    wo_moves(*back[4:5])
    for by in range(chips):
        att_pass(by, None, 1 - core).wait_recv()

    spans = [(k, 2) for k in range(0, units - 2, 2)] + [(units - 2, 1), (units - 1, 1)]

    def out_copy(by, side, source, at):
        which, lane = seat_of(by, side)
        span = pl.ds(*spans[at])
        return remote(
            out_part.at[which * 2 + lane, span],
            out_in.at[source, span],
            o_send.at[0],
            o_recv.at[source, at],
            place(which, lane),
        )

    heads_wide = wo_ref.shape[2]

    def finish(ref, source, at):
        first, count = spans[at]
        for k in range(first, first + count):
            span = pl.ds(pl.multiple_of(source * cols_out + k * unit, 128), unit)
            done = ref[source, k].astype(jnp.float32) * gate_ref[:, span]
            out_ref[0, :, span] = done.astype(out_ref.dtype)

    for at, (first, count) in enumerate(spans):

        @pl.when(is_end)
        def _():
            for r in (1, 2, 3):
                for k in range(first, first + count):
                    wo_copy(0, r, k // halves, k % halves, r - 1).wait_recv()

        rhs = [
            jnp.concatenate([wo_ref[z, k] for k in range(first, first + count)], axis=1)
            for z in range(n)
        ]
        for pair in ((1, 2), (3, 0)):
            firsts = [seat_of(by, 0)[0] * 2 for by in pair]
            total = None
            for z in range(n):
                lhs = jnp.concatenate([att_all[pl.ds(q, 2), z] for q in firsts], axis=0)
                lhs = lhs.reshape(4 * rows, heads_wide)
                made = jnp.dot(lhs, rhs[z], preferred_element_type=jnp.float32)
                total = made if total is None else total + made
            total = total.astype(out_part.dtype).reshape(4, rows, count * unit)
            for j, q in enumerate(firsts):
                for k in range(count):
                    columns = slice(k * unit, (k + 1) * unit)
                    out_part[pl.ds(q, 2), first + k] = total[2 * j : 2 * j + 2, :, columns]
            for by, side in others:
                if by in pair:
                    out_copy(by, side, seat, at).start()
        if at == max(0, len(spans) - 3):
            wo_moves(*back[5:])

    for at in range(len(spans)):
        finish(out_part, seat, at)
        for by, side in reversed(others):
            which, lane = seat_of(by, side)
            source = which * 2 + lane
            out_copy(by, side, source, at).wait_recv()
            finish(out_in, source, at)

    peers = pl.ds(0, seats - 1)
    sems = o_send.at[0], o_recv.at[seat, 0]
    remote(out_part.at[peers], out_in.at[peers], *sems, partner).wait_send()
    for by in range(chips):
        if by:
            att_chip(by, None, chip).wait_send()
        att_pass(by, None, core).wait_send()
    ref = att_ref.at[pl.ds(0, n - 1)]
    remote(ref, ref, z_send.at[0], z_recv.at[me], partner).wait_send()
    for slot, used in ((0, core == 0), (1, tract < 2), (2, tract < 2)):

        @pl.when(used)
        def _():
            kv_slot(slot).wait_send()

    def far_sent(where, which):
        ref = w_far.at[:, far_span(which, core)]
        remote(ref, ref, f_send.at[where], f_recv.at[where, 0], partner).wait_send()

    def wo_sent(way, blocks):
        ref = wo_ref.at[pl.ds(0, blocks)]
        sems = wo_send.at[way], wo_recv.at[0, 0, 0]
        remote(ref, ref, *sems, partner).wait_send()

    @pl.when(is_end)
    def _():
        far_sent(0, chip)
        tok_sent(0, 1, pieces)
        wo_sent(0, 1)

    @pl.when(is_helper)
    def _():
        for slot in range(chips):
            if slot:
                far_sent(slot, across[1] if slot == 3 else chip)
            far_sent(chips + slot, across[slot])
        for r in (1, 2, 3):
            ref = part_ref.at[blk(r)]
            sems = p_send.at[blk(r)], p_recv.at[blk(r), 0]
            remote(ref, ref, *sems, partner).wait_send()
        tok_sent(1, 3, near)
        wo_sent(1, 3)
        tok_sent(0, 2, pieces)
        wo_sent(0, 2)


PIECES = 8
NEAR = 4


def fits_line(n, tracts, reps, frames, w_out):
    rows, width = frames.shape[1:]
    seats = tracts * reps
    far = (PIECES - NEAR) * (width // PIECES)
    return (
        n == 4
        and (tracts, reps) == (4, 2)
        and rows % 16 == 0
        and width % (PIECES * 128) == 0
        and width % (seats * 256) == 0
        and far % (seats * 16) == 0
        and w_out.shape[0] % 32 == 0
    )


def line_body(frames, levels, visible, w_qkv, w_out, modulation):
    n, tracts = lax.axis_size("head"), lax.axis_size("tract")
    reps = lax.axis_size("rep")
    rows, width = frames.shape[1:]
    cols = w_qkv.shape[2]
    heads_here = cols // HD
    seats = tracts * reps
    chips = seats // 2
    deep = width // PIECES
    units = width // seats // 128
    vmem = pl.BlockSpec(memory_space=pltpu.VMEM)
    hbm = pl.BlockSpec(memory_space=pltpu.HBM)
    smem = pl.BlockSpec(memory_space=pltpu.SMEM)
    half = jnp.bfloat16
    dma = pltpu.SemaphoreType.DMA
    return pl.pallas_call(
        functools.partial(line_kernel, n, tracts, reps, PIECES, NEAR),
        out_shape=pltpu.VMEM(frames.shape, frames.dtype),
        in_specs=[hbm, smem, smem, hbm, hbm, hbm],
        out_specs=vmem,
        scratch_shapes=[
            pltpu.VMEM((3, *modulation.shape[::2]), jnp.float32),
            pltpu.VMEM((1, width), jnp.float32),
            pltpu.VMEM((rows, width), half),
            pltpu.VMEM((n, PIECES, rows, deep), half),
            pltpu.VMEM((3, width, cols), half),
            pltpu.VMEM((3, (PIECES - NEAR) * deep, cols), half),
            pltpu.VMEM((n, units, w_out.shape[0], 128), half),
            pltpu.VMEM((n, 3, rows, cols), jnp.float32),
            pltpu.VMEM((n, rows, cols), half),
            pltpu.VMEM((n, 2, rows, cols), half),
            pltpu.VMEM((max(1, tracts - 1), n, 2, rows, cols), half),
            pltpu.VMEM((n, 3, rows, cols), half),
            pltpu.VMEM((n, 3, rows, cols), half),
            pltpu.VMEM((n, rows, cols), half),
            pltpu.VMEM((heads_here, 1, n * rows), jnp.float32),
            pltpu.VMEM((heads_here, 1, n * rows), jnp.float32),
            pltpu.VMEM((heads_here, HD, n * rows), jnp.float32),
            pltpu.VMEM((seats, n, rows, cols), half),
            pltpu.VMEM((seats, units, rows, 128), half),
            pltpu.VMEM((seats, units, rows, 128), half),
            dma((3,)),
            dma((units,)),
            dma((2,)),
            dma((n - 1, PIECES, 2)),
            dma((2 * chips,)),
            dma((2 * chips, 3)),
            dma((n,)),
            dma((n, 3)),
            dma((3,)),
            dma((3,)),
            dma((2,)),
            dma((n - 1, units // 2, 2)),
            dma((1,)),
            dma((n,)),
            dma((2 * chips,)),
            dma((chips - 1, n)),
            dma((chips,)),
            dma((1,)),
            dma((seats, units // 2 + 1)),
        ],
        compiler_params=pltpu.CompilerParams(
            collective_id=0, has_side_effects=True, vmem_limit_bytes=GRANT
        ),
    )(
        frames,
        levels,
        visible,
        jnp.transpose(w_qkv, (1, 0, 2)),
        w_out,
        jnp.transpose(modulation, (1, 0, 2)),
    )


def body(frames, levels, visible, w_qkv, w_out, modulation):
    n, tracts = lax.axis_size("head"), lax.axis_size("tract")
    reps = lax.axis_size("rep")
    line = fits_line(n, tracts, reps, frames, w_out)
    chosen = line_body if line else ring_body
    return chosen(frames, levels, visible, w_qkv, w_out, modulation)


def solution(mesh):
    placed = (
        P(("rep", "tract"), "head", None),
        P(("rep", "tract")),
        P(("rep", "tract"), None),
        P(None, None, "head"),
        P("head", None),
        P(),
    )
    return jax.shard_map(
        body,
        mesh=mesh,
        in_specs=placed,
        out_specs=P(("rep", "tract"), "head", None),
        check_vma=False,
    )
```

```python
import functools

import jax
import jax.numpy as jnp
from jax import lax
from jax.experimental import pallas as pl
from jax.experimental.pallas import tpu as pltpu
from jax.sharding import PartitionSpec as P

HD = 128
GRANT = 60 * 1024 * 1024
MESH = pl.DeviceIdType.MESH


def meet(n, me, tracts, tract, others):
    barrier = pltpu.get_barrier_semaphore()
    for other in (lax.rem(me + 1, n), lax.rem(me + n - 1, n)):
        pl.semaphore_signal(barrier, inc=1, device_id={"head": other}, device_id_type=MESH)
    for ahead in range(1, tracts):
        other = lax.rem(tract + ahead, tracts)
        pl.semaphore_signal(barrier, inc=1, device_id={"tract": other}, device_id_type=MESH)
    for other in others:
        pl.semaphore_signal(barrier, inc=1, device_id=other, device_id_type=MESH)
    pl.semaphore_wait(barrier, 1 + tracts + len(others))


def sublayer_kernel(
    n,
    tracts,
    reps,
    pieces,
    halves,
    x_ref,
    level_ref,
    visible_ref,
    w_hbm,
    out_hbm,
    table_ref,
    out_ref,
    got,
    wq_ref,
    w_ref,
    q_ref,
    kv_ref,
    kv_in,
    att_ref,
    peak_ref,
    sum_ref,
    acc_ref,
    going,
    landed,
    total_ref,
    load_sem,
    g_send,
    g_recv,
    kv_send,
    kv_recv,
    s_send,
    s_recv,
    w_far,
    att_far,
    f_send,
    f_recv,
):
    me, tract = lax.axis_index("head"), lax.axis_index("tract")
    own = pltpu.make_async_copy(x_ref.at[0], got.at[me], load_sem.at[0])
    own.start()
    load = pltpu.make_async_copy(w_hbm, wq_ref, load_sem.at[1])
    load.start()
    load_out = pltpu.make_async_copy(out_hbm, w_ref, load_sem.at[2])
    load_out.start()
    core, wide = tract % 2, tracts // 2
    chips = wide * reps
    chip = lax.axis_index("rep") * wide + tract // 2
    slab = w_ref.shape[0] // (2 * chips)
    helper = (me == 1) | (me == n - 2)
    ends = (me == 0) | (me == n - 1)

    def seat(by):
        other = lax.rem(chip + by, chips)
        return {"rep": other // wide, "tract": lax.rem(other, wide) * 2 + core}

    def slab_of(which, side):
        start = pl.multiple_of((which * 2 + side) * slab, slab)
        return pl.ds(start, slab)

    def far_copy(kind, span, target, source=None):
        return pltpu.make_async_remote_copy(
            src_ref=(w_far if source is None else source).at[span],
            dst_ref=w_far.at[span],
            send_sem=f_send.at[kind],
            recv_sem=f_recv.at[kind],
            device_id=target,
            device_id_type=MESH,
        )

    inward = {"head": jnp.where(me == 0, 1, n - 2)}
    partner = {"tract": tract + 1 - 2 * core}
    mine = slab_of(chip, core)

    def to_helper():
        return far_copy(0, mine, inward, out_hbm)

    def to_chip(by):
        return far_copy(by, mine, seat(by))

    def from_chip(by):
        return far_copy(by, slab_of(lax.rem(chip + chips - by, chips), core), seat(by))

    def to_partner(by):
        span = slab_of(lax.rem(chip + chips - by, chips), core)
        return far_copy(chips + by, span, partner)

    def from_partner(by):
        span = slab_of(lax.rem(chip + chips - by, chips), 1 - core)
        return far_copy(chips + by, span, partner)

    def att_copy():
        return pltpu.make_async_remote_copy(
            src_ref=att_ref,
            dst_ref=att_far,
            send_sem=f_send.at[2 * chips],
            recv_sem=f_recv.at[2 * chips],
            device_id=inward,
            device_id_type=MESH,
        )

    meet(n, me, tracts, tract, [seat(by) for by in range(1, chips)])
    level = level_ref[0]

    def style(kind):
        return table_ref[kind, pl.ds(level, 1), :]

    rows, width = x_ref.shape[1:]
    part = rows // pieces

    def copy(way, step, piece, first=False):
        side = (way + 1) // 2
        span = pl.ds(piece * part, part)
        block = me - way * step
        return pltpu.make_async_remote_copy(
            src_ref=(x_ref.at[0] if first else got.at[block]).at[span],
            dst_ref=got.at[block].at[span],
            send_sem=g_send.at[side, step, piece],
            recv_sem=g_recv.at[side, step, piece],
            device_id={"head": me + way},
            device_id_type=MESH,
        )

    def arrival(way, step, piece):
        side = (way + 1) // 2
        span = pl.ds(piece * part, part)
        return pltpu.make_async_remote_copy(
            src_ref=x_ref.at[0].at[span],
            dst_ref=got.at[me - way * (step + 1)].at[span],
            send_sem=g_send.at[side, step, piece],
            recv_sem=g_recv.at[side, step, piece],
            device_id={"head": me - way},
            device_id_type=MESH,
        )

    def sends(way, step):
        block, target = me - way * step, me + way
        return (block >= 0) & (block < n) & (target >= 0) & (target < n) & (step < n - 1)

    def receives(way, step):
        block = me - way * (step + 1)
        return (block >= 0) & (block < n)

    def kv_copy(ahead, block):
        return pltpu.make_async_remote_copy(
            src_ref=kv_ref.at[block],
            dst_ref=kv_in.at[ahead - 1, block],
            send_sem=kv_send.at[ahead - 1, block],
            recv_sem=kv_recv.at[ahead - 1, block],
            device_id={"tract": tract + ahead},
            device_id_type=MESH,
        )

    def project(block):
        tokens = got[block].astype(jnp.float32)
        power = jnp.mean(tokens * tokens, axis=-1, keepdims=True)
        normed = tokens * lax.rsqrt(power + 1e-06)
        shaped = (normed * (1.0 + style(1)) + style(0)).astype(jnp.bfloat16)
        for kind in (1, 2, 0):
            made = jnp.dot(shaped, wq_ref[kind], preferred_element_type=jnp.float32)
            made = made.astype(jnp.bfloat16)
            if kind == 0:
                q_ref[block] = made
            else:
                kv_ref[block, kind - 1] = made
            if kind == 2:
                for ahead in range(1, tracts):

                    @pl.when(tract + ahead < tracts)
                    def _():
                        kv_copy(ahead, block).start()

    for piece in range(pieces):
        for way in (-1, 1):

            @pl.when(sends(way, 0))
            def _():
                copy(way, 0, piece, True).start()

    @pl.when(ends)
    def _():
        to_helper().start()

    own.wait()
    load.wait()
    project(me)

    @pl.loop(0, n - 1)
    def _(step):
        for piece in range(pieces):
            for way in (-1, 1):

                @pl.when(receives(way, step))
                def _():
                    arrival(way, step, piece).wait_recv()

                @pl.when(sends(way, step + 1))
                def _():
                    copy(way, step + 1, piece).start()

        @pl.loop(0, 2)
        def _(side):
            way = 2 * side - 1

            @pl.when(receives(way, step))
            def _():
                project(me - way * (step + 1))

        @pl.when(helper & (step == 0))
        def _():
            to_helper().wait_recv()
            for by in range(1, chips):
                to_chip(by).start()
            to_partner(0).start()

    @pl.when(helper)
    def _():
        for by in range(1, chips):
            from_chip(by).wait_recv()
            to_partner(by).start()

    tokens_here = n * rows
    heads_here = q_ref.shape[2] // HD
    scale = HD ** (-0.5)

    def attend(source, allowed):
        for head in range(heads_here):
            lanes = slice(head * HD, (head + 1) * HD)
            queries = q_ref[:, :, lanes].reshape(tokens_here, HD)
            keys = source[:, 0, :, lanes].reshape(tokens_here, HD)
            values = source[:, 1, :, lanes].reshape(tokens_here, HD)
            scores = (
                lax.dot_general(
                    queries, keys, (((1,), (1,)), ((), ())), preferred_element_type=jnp.float32
                )
                * scale
            )
            if allowed is None:
                peak = jnp.max(scores, axis=1, keepdims=True)
                probs = jnp.exp(scores - peak)
            else:
                scores = jnp.where(allowed, scores, -1e30)
                old = peak_ref[head]
                peak = jnp.maximum(old, jnp.max(scores, axis=1, keepdims=True))
                probs = jnp.where(allowed, jnp.exp(scores - peak), 0.0)
                rescale = jnp.exp(old - peak)
            row_sum = jnp.sum(probs, axis=1, keepdims=True)
            weighted = jnp.dot(
                probs.astype(jnp.bfloat16), values, preferred_element_type=jnp.float32
            )
            if allowed is not None:
                row_sum += sum_ref[head] * rescale
                weighted += acc_ref[head] * rescale
            peak_ref[head] = peak
            sum_ref[head] = row_sum
            acc_ref[head] = weighted

    attend(kv_ref, None)
    for ahead in range(1, tracts):

        @pl.when(tract >= ahead)
        def _():
            @pl.loop(0, n)
            def _(block):
                kv_copy(ahead, block).wait_recv()

            attend(kv_in.at[ahead - 1], visible_ref[0, lax.max(tract - ahead, 0)] > 0)

    for head in range(heads_here):
        attended = (acc_ref[head] / sum_ref[head]).astype(jnp.bfloat16)
        att_ref[:, :, head * HD : (head + 1) * HD] = attended.reshape(n, rows, HD)

    @pl.when(ends)
    def _():
        att_copy().start()

    load_out.wait()

    @pl.when(helper)
    def _():
        for by in range(chips):
            from_partner(by).wait_recv()
        att_copy().wait_recv()

    cols = width // halves

    def sum_copy(way, step, piece):
        side = (way + 1) // 2
        span = pl.ds(piece * cols, cols)
        return pltpu.make_async_remote_copy(
            src_ref=going.at[side, step].at[:, span],
            dst_ref=landed.at[side, step].at[:, span],
            send_sem=s_send.at[side, step, piece],
            recv_sem=s_recv.at[side, step, piece],
            device_id={"head": me + way},
            device_id_type=MESH,
        )

    def product(block, piece):
        return jnp.dot(
            att_ref[block],
            w_ref[:, piece * cols : (piece + 1) * cols],
            preferred_element_type=jnp.float32,
        )

    def far_product(block, piece):
        return jnp.dot(
            att_far[block],
            w_far[:, piece * cols : (piece + 1) * cols],
            preferred_element_type=jnp.float32,
        )

    def helps(way):
        return me == (1 if way == 1 else n - 2)

    def owner(way, step):
        return (n - 1 - step) if way == 1 else step

    def sum_sends(way, step):
        block = owner(way, step)
        return (block > me) & (me > 0) if way == 1 else (block < me) & (me < n - 1)

    def sum_receives(way, step):
        block = owner(way, step)
        return (block >= me) & (me > 1) if way == 1 else (block <= me) & (me < n - 2)

    @pl.loop(0, n - 1)
    def _(tick):
        for piece in range(halves):
            span = slice(piece * cols, (piece + 1) * cols)
            for way in (-1, 1):
                side = (way + 1) // 2
                step = tick - (me if way == 1 else n - 1 - me)
                held = (step >= 0) & (step < n - 1)

                @pl.when(held & sum_sends(way, step))
                def _():
                    going[side, step, :, span] = product(owner(way, step), piece).astype(
                        going.dtype
                    )

                    @pl.when(helps(way))
                    def _():
                        going[side, step, :, span] = (
                            going[side, step, :, span].astype(jnp.float32)
                            + far_product(owner(way, step), piece)
                        ).astype(going.dtype)

                    @pl.when(sum_receives(way, step))
                    def _():
                        sum_copy(way, step, piece).wait_recv()
                        going[side, step, :, span] = (
                            going[side, step, :, span].astype(jnp.float32)
                            + landed[side, step, :, span].astype(jnp.float32)
                        ).astype(going.dtype)

                    sum_copy(way, step, piece).start()

    for piece in range(halves):
        span = slice(piece * cols, (piece + 1) * cols)
        total_ref[:, span] = product(me, piece).astype(going.dtype).astype(jnp.float32)
    for piece in range(halves):
        span = slice(piece * cols, (piece + 1) * cols)
        for way in (-1, 1):
            side = (way + 1) // 2
            last = n - 1 - me if way == 1 else me

            @pl.when(helps(way))
            def _():
                total_ref[:, span] += far_product(me, piece)

            @pl.when(me > 1 if way == 1 else me < n - 2)
            def _():
                sum_copy(way, last, piece).wait_recv()
                total_ref[:, span] += landed[side, last, :, span].astype(jnp.float32)

        out_ref[0, :, span] = (
            total_ref[:, span] * table_ref[2, pl.ds(level, 1), span]
        ).astype(out_ref.dtype)

    @pl.loop(0, n - 1)
    def _(step):
        for piece in range(halves):
            for way in (-1, 1):

                @pl.when(sum_sends(way, step))
                def _():
                    sum_copy(way, step, piece).wait_send()

    @pl.loop(0, n)
    def _(block):
        for ahead in range(1, tracts):

            @pl.when(tract + ahead < tracts)
            def _():
                kv_copy(ahead, block).wait_send()

    @pl.loop(0, n - 1)
    def _(step):
        for piece in range(pieces):
            for way in (-1, 1):

                @pl.when(sends(way, step))
                def _():
                    copy(way, step, piece).wait_send()

    @pl.when(ends)
    def _():
        to_helper().wait_send()
        att_copy().wait_send()

    @pl.when(helper)
    def _():
        for by in range(1, chips):
            to_chip(by).wait_send()
        for by in range(chips):
            to_partner(by).wait_send()


def ring_body(frames, levels, visible, w_qkv, w_out, modulation):
    n, tracts = lax.axis_size("head"), lax.axis_size("tract")
    reps = lax.axis_size("rep")
    rows, width = frames.shape[1:]
    cols = w_qkv.shape[2]
    heads_here = cols // HD
    pieces = max(1, rows // 32)
    halves = 4 if width % 512 == 0 else 2
    vmem = pl.BlockSpec(memory_space=pltpu.VMEM)
    hbm = pl.BlockSpec(memory_space=pltpu.HBM)
    smem = pl.BlockSpec(memory_space=pltpu.SMEM)
    half = jnp.bfloat16
    dma = pltpu.SemaphoreType.DMA
    return pl.pallas_call(
        functools.partial(sublayer_kernel, n, tracts, reps, pieces, halves),
        out_shape=jax.ShapeDtypeStruct(frames.shape, frames.dtype),
        in_specs=[hbm, smem, smem, hbm, hbm, vmem],
        out_specs=vmem,
        scratch_shapes=[
            pltpu.VMEM((n, rows, width), half),
            pltpu.VMEM((3, width, cols), half),
            pltpu.VMEM(w_out.shape, half),
            pltpu.VMEM((n, rows, cols), half),
            pltpu.VMEM((n, 2, rows, cols), half),
            pltpu.VMEM((max(1, tracts - 1), n, 2, rows, cols), half),
            pltpu.VMEM((n, rows, cols), half),
            pltpu.VMEM((heads_here, n * rows, 1), jnp.float32),
            pltpu.VMEM((heads_here, n * rows, 1), jnp.float32),
            pltpu.VMEM((heads_here, n * rows, HD), jnp.float32),
            pltpu.VMEM((2, n - 1, rows, width), half),
            pltpu.VMEM((2, n - 1, rows, width), half),
            pltpu.VMEM((rows, width), jnp.float32),
            dma((3,)),
            dma((2, n, pieces)),
            dma((2, n, pieces)),
            dma((tracts, n)),
            dma((tracts, n)),
            dma((2, n, halves)),
            dma((2, n, halves)),
            pltpu.VMEM(w_out.shape, half),
            pltpu.VMEM((n, rows, cols), half),
            dma((tracts * reps + 1,)),
            dma((tracts * reps + 1,)),
        ],
        compiler_params=pltpu.CompilerParams(
            collective_id=0, has_side_effects=True, vmem_limit_bytes=GRANT
        ),
    )(
        frames,
        levels,
        visible,
        jnp.transpose(w_qkv, (1, 0, 2)),
        w_out,
        jnp.transpose(modulation, (1, 0, 2)),
    )


def line_kernel(
    n,
    tracts,
    reps,
    pieces,
    near,
    x_ref,
    level_ref,
    visible_ref,
    w_hbm,
    out_hbm,
    table_hbm,
    out_ref,
    table_ref,
    gate_ref,
    raw,
    got,
    wq_ref,
    w_far,
    wo_ref,
    acc_ref,
    q_ref,
    kv_ref,
    kv_in,
    part_ref,
    part_in,
    att_ref,
    peak_ref,
    sum_ref,
    mix_ref,
    att_all,
    out_part,
    out_in,
    load_sem,
    wo_sem,
    g_send,
    g_recv,
    f_send,
    f_recv,
    p_send,
    p_recv,
    kv_send,
    kv_recv,
    wo_send,
    wo_recv,
    z_send,
    z_recv,
    a_send,
    a_recv,
    b_recv,
    o_send,
    o_recv,
):
    me, tract, rep = lax.axis_index("head"), lax.axis_index("tract"), lax.axis_index("rep")
    rows, width = x_ref.shape[1:]
    deep = width // pieces
    low = me < 2
    sign = jnp.where(low, 1, -1)
    base = jnp.where(low, 0, n - 1)
    is_end = (me == 0) | (me == n - 1)
    is_helper = (me == 1) | (me == n - 2)
    inner, outer = {"head": me + sign}, {"head": me - sign}

    def blk(r):
        return base + sign * r

    core, wide = tract % 2, tracts // 2
    chips = wide * reps
    seats = chips * 2
    chip = rep * wide + tract // 2
    seat = chip * 2 + core
    partner = {"tract": tract + 1 - 2 * core}

    def chip_at(by):
        return lax.rem(chip + by, chips)

    def place(which, side):
        return {"rep": which // wide, "tract": lax.rem(which, wide) * 2 + side}

    across = [
        chip,
        rep * wide + 1 - lax.rem(chip, wide),
        (1 - rep) * wide + lax.rem(chip, wide),
        (1 - rep) * wide + 1 - lax.rem(chip, wide),
    ]
    along_x, along_y = place(across[1], core), place(across[2], core)
    others = [(by, side) for by in (1, 2, 3) for side in (0, 1)] + [(0, 1)]

    def seat_of(by, side):
        return across[(3, 1, 2)[by - 1] if by else 0], core if side == 0 else 1 - core


    own_load = pltpu.make_async_copy(x_ref.at[0], raw, load_sem.at[0])
    own_load.start()
    barrier = pltpu.get_barrier_semaphore()
    for ahead in range(1, n):
        other = lax.rem(me + ahead, n)
        pl.semaphore_signal(barrier, inc=1, device_id={"head": other}, device_id_type=MESH)
    for other in others:
        target = place(*seat_of(*other))
        pl.semaphore_signal(barrier, inc=1, device_id=target, device_id_type=MESH)

    table_load = pltpu.make_async_copy(table_hbm, table_ref, load_sem.at[1])
    table_load.start()
    cols_out = width // seats
    units = wo_ref.shape[1]
    cuts, unit = units // 2, cols_out // units

    def wo_load(k):
        start = pl.multiple_of(seat * cols_out + k * unit, 128)
        src = out_hbm.at[:, pl.ds(start, unit)]
        return pltpu.make_async_copy(src, wo_ref.at[me, k], wo_sem.at[k])

    def wo_loaded():
        for k in range(units):
            wo_load(k).wait()

    wq_load = pltpu.make_async_copy(w_hbm, wq_ref, load_sem.at[2])
    wq_load.start()

    for k in range(units):
        wo_load(k).start()

    level = level_ref[0]

    def style(kind, start):
        return table_ref[kind, pl.ds(level, 1), start : start + deep]

    def remote(src, dst, send, recv, target):
        return pltpu.make_async_remote_copy(
            src_ref=src,
            dst_ref=dst,
            send_sem=send,
            recv_sem=recv,
            device_id=target,
            device_id_type=MESH,
        )

    parts = g_recv.shape[2]
    part_rows = rows // parts

    def row_there(way, r, onward):
        if way == 1:
            return r - 1
        return 1 if r == 1 else 2 if onward else 0

    def row_here(r):
        return max(r - 1, 0)

    def tok(way, r, p, part, row):
        b = blk(r)
        ref = got.at[b, p, pl.ds(part * part_rows, part_rows)]
        target = inner if way == 0 else outer
        return remote(ref, ref, g_send.at[way], g_recv.at[row, p, part], target)

    def tok_take(way, r, p, onward):
        for part in range(parts):
            tok(way, r, p, part, row_here(r)).wait_recv()
            if onward is not None:

                @pl.when(onward)
                def _():
                    tok(way, r, p, part, row_there(way, r, True)).start()

    def tok_sent(way, blocks, count):
        ref = got.at[pl.ds(0, blocks), pl.ds(0, count)]
        remote(ref, ref, g_send.at[way], g_recv.at[0, 0, 0], partner).wait_send()

    far_rows = w_far.shape[1] // seats
    far_base = near * deep

    def far_span(which, side):
        start = (which * 2 + side) * far_rows
        return pl.ds(pl.multiple_of(start, far_rows), far_rows)

    def far_first(kind):
        start = far_base + seat * far_rows
        src = w_hbm.at[kind, pl.ds(pl.multiple_of(start, far_rows), far_rows)]
        dst = w_far.at[kind, far_span(chip, core)]
        return remote(src, dst, f_send.at[0], f_recv.at[0, kind], inner)

    def far_move(slot, kind, which):
        ref = w_far.at[kind, far_span(which, core)]
        target = along_x if slot == 1 else along_y
        return remote(ref, ref, f_send.at[slot], f_recv.at[slot, kind], target)

    def far_pass(slot, kind, side):
        ref = w_far.at[kind, far_span(across[slot], side)]
        where = chips + slot
        return remote(ref, ref, f_send.at[where], f_recv.at[where, kind], partner)

    def far_relay(kind):
        far_first(kind).wait_recv()
        far_move(1, kind, chip).start()
        far_move(2, kind, chip).start()
        far_pass(0, kind, core).start()

    def far_hand_x(kind):
        far_move(1, kind, across[1]).wait_recv()
        far_move(3, kind, across[1]).start()
        far_pass(1, kind, core).start()

    def far_hand_y(kind):
        for slot in (2, 3):
            far_move(slot, kind, across[slot]).wait_recv()
            far_pass(slot, kind, core).start()

    def far_ready(kind):
        for slot in range(chips):
            far_pass(slot, kind, 1 - core).wait_recv()

    def part_copy(r, kind):
        b = blk(r)
        return remote(
            part_ref.at[b, kind],
            part_in.at[b, kind],
            p_send.at[b],
            p_recv.at[b, kind],
            outer,
        )

    def far_part(rs, kinds):
        for kind in kinds:
            total = None
            for p in range(near, pieces):
                lhs = jnp.concatenate([got[blk(r), p] for r in rs], axis=0)
                span = slice((p - near) * deep, (p - near + 1) * deep)
                made = jnp.dot(lhs, w_far[kind, span], preferred_element_type=jnp.float32)
                total = made if total is None else total + made
            total = total.astype(part_ref.dtype)
            for i, r in enumerate(rs):
                part_ref[blk(r), kind] = total[i * rows : (i + 1) * rows]
        for r in rs:
            for kind in kinds:
                part_copy(r, kind).start()

    halves = wo_recv.shape[2]

    def wo_copy(way, r, cut, half, row):
        b = blk(r)
        ref = wo_ref.at[b, cut * halves + half]
        target = inner if way == 0 else outer
        return remote(ref, ref, wo_send.at[way], wo_recv.at[row, cut, half], target)

    def wo_start(way, r, which):
        for cut in which:
            for half in range(halves):
                wo_copy(way, r, cut, half, row_there(way, r, False)).start()

    along = [(0, r, cut) for cut in range(cuts) for r in (1, 0)]
    back = [(1, r, cut) for cut in range(cuts) for r in (2, 3)]
    early = 3

    def wo_next(way, r, cut):
        for half in range(halves):
            if r != 1:
                wo_copy(way, r, cut, half, row_here(r)).wait_recv()
            wo_copy(way, r, cut, half, row_there(way, r, True)).start()

    def wo_moves(*moves):
        @pl.when(is_helper)
        def _():
            for move in moves:
                wo_next(*move)

    def kv_near(b, kinds):
        ref, slot = kv_ref.at[b, kinds], kv_in.at[0, b, kinds]
        return remote(ref, slot, kv_send.at[0], kv_recv.at[0], partner)

    def kv_far(b, kinds):
        ref, slot = kv_ref.at[b, kinds], kv_in.at[1, b, kinds]
        return remote(ref, slot, kv_send.at[1], kv_recv.at[1], along_x)

    def kv_cross(b, kinds):
        at = 2 * (1 - core)
        ref, slot = kv_ref.at[b, kinds], kv_in.at[at, b, kinds]
        target = place(across[1], 1 - core)
        return remote(ref, slot, kv_send.at[2], kv_recv.at[at], target)

    def kv_slot(slot):
        return remote(kv_ref, kv_in.at[slot], kv_send.at[slot], kv_recv.at[slot], partner)

    def accumulate(rs, p):
        lhs = jnp.concatenate([got[blk(r), p] for r in rs], axis=0)
        span = pl.ds(pl.multiple_of(p * deep, deep), deep)
        for kind in range(3):
            made = jnp.dot(lhs, wq_ref[kind, span], preferred_element_type=jnp.float32)
            for i, r in enumerate(rs):
                acc_ref[blk(r), kind] += made[i * rows : (i + 1) * rows]

    def settle(r, kinds, extra=False):
        b = blk(r)
        for kind in kinds:
            made = acc_ref[b, kind]
            if extra:
                made = made + part_in[b, kind].astype(jnp.float32)
            made = made.astype(q_ref.dtype)
            if kind == 0:
                q_ref[b] = made
            else:
                kv_ref[b, kind - 1] = made

    def share(r, first=0, count=2):
        kinds = pl.ds(first, count)

        @pl.when(tract < 2)
        def _():
            kv_far(blk(r), kinds).start()
            kv_cross(blk(r), kinds).start()

        @pl.when(core == 0)
        def _():
            kv_near(blk(r), kinds).start()

    own_load.wait()
    power = jnp.zeros((rows, 1), jnp.float32)
    for p in range(pieces):
        tokens = raw[:, p * deep : (p + 1) * deep].astype(jnp.float32)
        power += jnp.sum(tokens * tokens, axis=-1, keepdims=True)
    table_load.wait()
    factor = lax.rsqrt(power * (1.0 / width) + 1e-06)
    pl.semaphore_wait(barrier, n - 1 + len(others))

    @pl.when(is_end)
    def _():
        for kind in (1, 2):
            far_first(kind).start()

    def send_own(p):
        @pl.when(is_end)
        def _():
            for part in range(parts):
                tok(0, 0, p, part, 0).start()
            if p == 0:
                far_first(0).start()

        @pl.when(is_helper)
        def _():
            for part in range(parts):
                tok(0, 1, p, part, 1).start()
                if p < near:
                    tok(1, 1, p, part, 0).start()

    for p in range(pieces):
        tokens = raw[:, p * deep : (p + 1) * deep].astype(jnp.float32)
        shaped = tokens * factor * (1.0 + style(1, p * deep)) + style(0, p * deep)
        got[me, p] = shaped.astype(got.dtype)
        if p:
            send_own(p - 1)
    send_own(pieces - 1)
    acc_ref[...] = jnp.zeros_like(acc_ref)
    gate_ref[...] = table_ref[2, pl.ds(level, 1), :]

    @pl.when(is_end)
    def _():
        wq_load.wait()
        @pl.loop(0, pieces)
        def _(p):
            accumulate((0,), p)

        wo_loaded()
        wo_start(0, 0, range(cuts))

        settle(0, (1, 2, 0))
        share(0)
        for r in (1, 2):

            @pl.loop(0, near)
            def _(p):
                tok_take(0, r, p, None)
                accumulate((r,), p)

        for kind in (1, 2):
            for r in (1, 2):
                part_copy(r, kind).wait_recv()
                settle(r, (kind,), True)
                share(r, kind - 1, 1)

        @pl.loop(0, near)
        def _(p):
            tok_take(0, 3, p, None)
            accumulate((3,), p)

        for kind in (1, 2):
            part_copy(3, kind).wait_recv()
        settle(3, (1, 2), True)
        share(3)
        for r in (1, 2, 3):
            part_copy(r, 0).wait_recv()
            settle(r, (0,), True)

    @pl.when(is_helper)
    def _():
        def pass_on(p):
            tok_take(0, 0, p, True)
            accumulate((0,), p)

        wq_load.wait()
        @pl.loop(0, pieces)
        def _(p):
            tok_take(1, 2, p, p < near)
            accumulate((1, 2), p)
            for at, kind in ((1, 1), (3, 2), (7, 0)):

                @pl.when(p == at)
                def _():
                    far_relay(kind)

            @pl.when(p == near)
            def _():
                wo_loaded()
                wo_start(1, 1, range(cuts - 1))

            for at, kind in ((4, 1), (6, 2)):

                @pl.when(p == at)
                def _():
                    far_hand_x(kind)

            @pl.when(p >= pieces - 2)
            def _():
                pass_on(p - (pieces - 2))

        settle(1, (1, 2, 0))
        share(1)
        settle(2, (1, 2, 0))
        share(2)

        @pl.loop(0, pieces)
        def _(p):
            @pl.when(p + 2 < pieces)
            def _():
                pass_on(p + 2)

            tok_take(1, 3, p, p < near)

            @pl.when(p == pieces - 1)
            def _():
                far_part((3,), (1, 2))

            accumulate((3,), p)

            @pl.when(p == 1)
            def _():
                far_hand_y(1)

            @pl.when(p == 2)
            def _():
                far_hand_x(0)
                far_ready(1)
                far_part((1, 2), (1,))

            @pl.when(p == 3)
            def _():
                far_hand_y(2)

            @pl.when(p == 4)
            def _():
                far_ready(2)
                far_part((1, 2), (2,))
                wo_start(1, 1, (cuts - 1,))

            @pl.when(p == 5)
            def _():
                settle(0, (1, 2, 0))
                share(0)

            @pl.when(p == 6)
            def _():
                wo_next(*along[0])

            @pl.when(p == 5)
            def _():
                far_hand_y(0)

        settle(3, (1, 2))
        share(3)
        far_ready(0)
        far_part((1, 2, 3), (0,))
        settle(3, (0,))
        wo_next(*along[1])

        @pl.when(tract >= 2)
        def _():
            for move in along[2:early]:
                wo_next(*move)


    tokens_here = n * rows
    heads_here = q_ref.shape[2] // HD
    scale = HD ** (-0.5)

    def attend(source, bias):
        for head in range(heads_here):
            lanes = slice(head * HD, (head + 1) * HD)
            queries = q_ref[:, :, lanes].reshape(tokens_here, HD)
            keys = source[:, 0, :, lanes].reshape(tokens_here, HD)
            values = source[:, 1, :, lanes].reshape(tokens_here, HD)
            scores = (
                lax.dot_general(
                    keys, queries, (((1,), (1,)), ((), ())), preferred_element_type=jnp.float32
                )
                * scale
            )
            if bias is not None:
                scores = scores + bias
            peak = jnp.max(scores, axis=0, keepdims=True)
            if bias is not None:
                old = peak_ref[head]
                peak = jnp.maximum(old, peak)
            probs = jnp.exp(scores - peak)
            row_sum = jnp.sum(probs, axis=0, keepdims=True)
            weighted = lax.dot_general(
                values,
                probs.astype(jnp.bfloat16),
                (((0,), (0,)), ((), ())),
                preferred_element_type=jnp.float32,
            )
            if bias is not None:
                rescale = jnp.exp(old - peak)
                row_sum += sum_ref[head] * rescale
                weighted += mix_ref[head] * rescale
            peak_ref[head] = peak
            sum_ref[head] = row_sum
            mix_ref[head] = weighted

    attend(kv_ref, None)

    for ahead in (1, 2, 3):
        if ahead == 2:

            @pl.when(is_helper & (tract >= 2))
            def _():
                wo_next(*back[0])

        @pl.when(tract >= ahead)
        def _():
            kv_slot(ahead - 1).wait_recv()
            seen = visible_ref[0, lax.max(tract - ahead, 0)] > 0
            attend(kv_in.at[ahead - 1], jnp.where(seen, 0.0, -1e30))

    for head in range(heads_here):
        attended = jnp.transpose(mix_ref[head] / sum_ref[head]).astype(jnp.bfloat16)
        att_ref[:, :, head * HD : (head + 1) * HD] = attended.reshape(n, rows, HD)

    def att_line(other, source):
        return remote(
            att_ref.at[other],
            att_all.at[seat, source],
            z_send.at[0],
            z_recv.at[source],
            {"head": other},
        )

    line = [blk(jnp.where(is_end, end, help)) for end, help in ((0, 1), (1, 2), (2, 0), (3, 3))]
    for other in line[1:]:
        att_line(other, me).start()
    att_all[seat, me] = att_ref[me]

    def att_chip(by, z, which):
        ref = att_all.at[which * 2 + core] if z is None else att_all.at[which * 2 + core, z]
        at = a_recv.at[by - 1, 0 if z is None else z]
        return remote(ref, ref, a_send.at[0], at, place(seat_of(by, 0)[0], core))

    def att_pass(by, z, side):
        owner = seat_of(by, 0)[0] * 2 + side
        ref = att_all.at[owner] if z is None else att_all.at[owner, z]
        return remote(ref, ref, a_send.at[1], b_recv.at[0], partner)

    @pl.when(is_helper)
    def _():
        @pl.when(tract < 2)
        def _():
            for move in along[2:early]:
                wo_next(*move)

        for move in along[early:]:
            wo_next(*move)

    for ahead, z in enumerate(line):
        if ahead:
            att_line(z, z).wait_recv()
        for by in range(1, chips):
            att_chip(by, z, chip).start()
        att_pass(0, z, core).start()
        for late, used in ((0, tract < 2), (1, tract >= 2)):

            @pl.when(is_helper & used)
            def _():
                for move in back[ahead + late : min(ahead + late + 1, 3)]:
                    wo_next(*move)

    for ahead, z in enumerate(line):
        for by in range(1, chips):
            att_chip(by, z, seat_of(by, 0)[0]).wait_recv()
            att_pass(by, z, core).start()
        if ahead == 2:
            wo_moves(*back[3:4])
    wo_moves(*back[4:5])
    def att_passes(count):
        ref = att_all.at[pl.ds(0, count)]
        return remote(ref, ref, a_send.at[1], b_recv.at[0], partner)

    att_passes(chips).wait_recv()

    spans = [(k, 2) for k in range(0, units - 2, 2)] + [(units - 2, 1), (units - 1, 1)]

    def out_copy(by, side, source, at):
        which, lane = seat_of(by, side)
        span = pl.ds(*spans[at])
        return remote(
            out_part.at[which * 2 + lane, span],
            out_in.at[source, span],
            o_send.at[0],
            o_recv.at[source, at],
            place(which, lane),
        )

    heads_wide = wo_ref.shape[2]

    def finish(ref, source, at):
        first, count = spans[at]
        for k in range(first, first + count):
            span = pl.ds(pl.multiple_of(source * cols_out + k * unit, 128), unit)
            done = ref[source, k].astype(jnp.float32) * gate_ref[:, span]
            out_ref[0, :, span] = done.astype(out_ref.dtype)

    for at, (first, count) in enumerate(spans):

        @pl.when(is_end)
        def _():
            for r in (1, 2, 3):
                for k in range(first, first + count):
                    wo_copy(0, r, k // halves, k % halves, r - 1).wait_recv()

        rhs = [
            jnp.concatenate([wo_ref[z, k] for k in range(first, first + count)], axis=1)
            for z in range(n)
        ]
        for pair in ((1, 2), (3, 0)):
            firsts = [seat_of(by, 0)[0] * 2 for by in pair]
            total = None
            for z in range(n):
                lhs = jnp.concatenate([att_all[pl.ds(q, 2), z] for q in firsts], axis=0)
                lhs = lhs.reshape(4 * rows, heads_wide)
                made = jnp.dot(lhs, rhs[z], preferred_element_type=jnp.float32)
                total = made if total is None else total + made
            total = total.astype(out_part.dtype).reshape(4, rows, count * unit)
            for j, q in enumerate(firsts):
                for k in range(count):
                    columns = slice(k * unit, (k + 1) * unit)
                    out_part[pl.ds(q, 2), first + k] = total[2 * j : 2 * j + 2, :, columns]
            for by, side in others:
                if by in pair:
                    out_copy(by, side, seat, at).start()
        if at == max(0, len(spans) - 3):
            wo_moves(*back[5:])

    for at in range(len(spans)):
        finish(out_part, seat, at)
        for by, side in reversed(others):
            which, lane = seat_of(by, side)
            source = which * 2 + lane
            out_copy(by, side, source, at).wait_recv()
            finish(out_in, source, at)

    peers = pl.ds(0, seats - 1)
    sems = o_send.at[0], o_recv.at[seat, 0]
    remote(out_part.at[peers], out_in.at[peers], *sems, partner).wait_send()
    ref = att_all.at[pl.ds(0, chips - 1)]
    remote(ref, ref, a_send.at[0], b_recv.at[0], partner).wait_send()
    att_passes(chips).wait_send()
    ref = att_ref.at[pl.ds(0, n - 1)]
    remote(ref, ref, z_send.at[0], z_recv.at[me], partner).wait_send()
    for slot, used in ((0, core == 0), (1, tract < 2), (2, tract < 2)):

        @pl.when(used)
        def _():
            kv_slot(slot).wait_send()

    def far_sent(where, which):
        ref = w_far.at[:, far_span(which, core)]
        remote(ref, ref, f_send.at[where], f_recv.at[where, 0], partner).wait_send()

    def wo_sent(way, blocks):
        ref = wo_ref.at[pl.ds(0, blocks)]
        sems = wo_send.at[way], wo_recv.at[0, 0, 0]
        remote(ref, ref, *sems, partner).wait_send()

    @pl.when(is_end)
    def _():
        far_sent(0, chip)
        tok_sent(0, 1, pieces)
        wo_sent(0, 1)

    @pl.when(is_helper)
    def _():
        for slot in range(chips):
            if slot:
                far_sent(slot, across[1] if slot == 3 else chip)
            far_sent(chips + slot, across[slot])
        for r in (1, 2, 3):
            ref = part_ref.at[blk(r)]
            sems = p_send.at[blk(r)], p_recv.at[blk(r), 0]
            remote(ref, ref, *sems, partner).wait_send()
        tok_sent(1, 3, near)
        wo_sent(1, 3)
        tok_sent(0, 2, pieces)
        wo_sent(0, 2)


PIECES = 8
NEAR = 4


def fits_line(n, tracts, reps, frames, w_out):
    rows, width = frames.shape[1:]
    seats = tracts * reps
    far = (PIECES - NEAR) * (width // PIECES)
    return (
        n == 4
        and (tracts, reps) == (4, 2)
        and rows % 16 == 0
        and width % (PIECES * 128) == 0
        and width % (seats * 256) == 0
        and far % (seats * 16) == 0
        and w_out.shape[0] % 32 == 0
    )


def line_body(frames, levels, visible, w_qkv, w_out, modulation):
    n, tracts = lax.axis_size("head"), lax.axis_size("tract")
    reps = lax.axis_size("rep")
    rows, width = frames.shape[1:]
    cols = w_qkv.shape[2]
    heads_here = cols // HD
    seats = tracts * reps
    chips = seats // 2
    deep = width // PIECES
    units = width // seats // 128
    vmem = pl.BlockSpec(memory_space=pltpu.VMEM)
    hbm = pl.BlockSpec(memory_space=pltpu.HBM)
    smem = pl.BlockSpec(memory_space=pltpu.SMEM)
    half = jnp.bfloat16
    dma = pltpu.SemaphoreType.DMA
    return pl.pallas_call(
        functools.partial(line_kernel, n, tracts, reps, PIECES, NEAR),
        out_shape=pltpu.VMEM(frames.shape, frames.dtype),
        in_specs=[hbm, smem, smem, hbm, hbm, hbm],
        out_specs=vmem,
        scratch_shapes=[
            pltpu.VMEM((3, *modulation.shape[::2]), jnp.float32),
            pltpu.VMEM((1, width), jnp.float32),
            pltpu.VMEM((rows, width), half),
            pltpu.VMEM((n, PIECES, rows, deep), half),
            pltpu.VMEM((3, width, cols), half),
            pltpu.VMEM((3, (PIECES - NEAR) * deep, cols), half),
            pltpu.VMEM((n, units, w_out.shape[0], 128), half),
            pltpu.VMEM((n, 3, rows, cols), jnp.float32),
            pltpu.VMEM((n, rows, cols), half),
            pltpu.VMEM((n, 2, rows, cols), half),
            pltpu.VMEM((max(1, tracts - 1), n, 2, rows, cols), half),
            pltpu.VMEM((n, 3, rows, cols), half),
            pltpu.VMEM((n, 3, rows, cols), half),
            pltpu.VMEM((n, rows, cols), half),
            pltpu.VMEM((heads_here, 1, n * rows), jnp.float32),
            pltpu.VMEM((heads_here, 1, n * rows), jnp.float32),
            pltpu.VMEM((heads_here, HD, n * rows), jnp.float32),
            pltpu.VMEM((seats, n, rows, cols), half),
            pltpu.VMEM((seats, units, rows, 128), half),
            pltpu.VMEM((seats, units, rows, 128), half),
            dma((3,)),
            dma((units,)),
            dma((2,)),
            dma((n - 1, PIECES, 2)),
            dma((2 * chips,)),
            dma((2 * chips, 3)),
            dma((n,)),
            dma((n, 3)),
            dma((3,)),
            dma((3,)),
            dma((2,)),
            dma((n - 1, units // 2, 2)),
            dma((1,)),
            dma((n,)),
            dma((2,)),
            dma((chips - 1, n)),
            dma((1,)),
            dma((1,)),
            dma((seats, units // 2 + 1)),
        ],
        compiler_params=pltpu.CompilerParams(
            collective_id=0, has_side_effects=True, vmem_limit_bytes=GRANT
        ),
    )(
        frames,
        levels,
        visible,
        jnp.transpose(w_qkv, (1, 0, 2)),
        w_out,
        jnp.transpose(modulation, (1, 0, 2)),
    )


def body(frames, levels, visible, w_qkv, w_out, modulation):
    n, tracts = lax.axis_size("head"), lax.axis_size("tract")
    reps = lax.axis_size("rep")
    line = fits_line(n, tracts, reps, frames, w_out)
    chosen = line_body if line else ring_body
    return chosen(frames, levels, visible, w_qkv, w_out, modulation)


def solution(mesh):
    placed = (
        P(("rep", "tract"), "head", None),
        P(("rep", "tract")),
        P(("rep", "tract"), None),
        P(None, None, "head"),
        P("head", None),
        P(),
    )
    return jax.shard_map(
        body,
        mesh=mesh,
        in_specs=placed,
        out_specs=P(("rep", "tract"), "head", None),
        check_vma=False,
    )
```
